32 devices in a mesh: fsdp: 8 (over z, x), seq: 4 (over y, core).
Axes of the slice: x: 2, y: 2, z: 4, core: 2. Of those that a mesh axis runs over, the one named last changes fastest.
Arguments:
- block_input: bfloat16 [8, 1024, 2048], P('fsdp', 'seq'), may hold values from -6 to 6
- cotangent: bfloat16 [8, 1024, 2048], P('fsdp', 'seq'), may hold values from -6 to 6
- item_starts: int32 [8, 3], P('fsdp'), may hold values from 0 to 960, as said below
- item_lengths: int32 [8, 3], P('fsdp'), may hold values from 64 to 768, as said below
- pad_mask: int32 [8, 1024], P('fsdp'), may hold values 0 or 1
- ln1_gain: float32 [2048], P('fsdp'), may hold values from 0.5 to 1.5
- ln1_shift: float32 [2048], P('fsdp'), may hold values from -3 to 3
- w_qkv: bfloat16 [2048, 6144], P('fsdp'), may hold values from -0.125 to 0.125
- w_out: bfloat16 [2048, 2048], P('fsdp'), may hold values from -0.5 to 0.5
- ln2_gain: float32 [2048], P('fsdp'), may hold values from 0.5 to 1.5
- ln2_shift: float32 [2048], P('fsdp'), may hold values from -3 to 3
- w_up: bfloat16 [2048, 8192], P('fsdp'), may hold values from -0.125 to 0.125
- up_bias: float32 [8192], P('fsdp'), may hold values from -3 to 3
- w_down: bfloat16 [8192, 2048], P('fsdp'), may hold values from -0.0625 to 0.0625
- down_bias: float32 [2048], P('fsdp'), may hold values from -3 to 3
Outputs:
- block_output: bfloat16 [8, 1024, 2048], P('fsdp', 'seq')
- input_grad: float32 [8, 1024, 2048], P('fsdp', 'seq')
- ln1_gain_grad: float32 [2048], P('fsdp')
- ln1_shift_grad: float32 [2048], P('fsdp')
- w_qkv_grad: float32 [2048, 6144], P('fsdp')
- w_out_grad: float32 [2048, 2048], P('fsdp')
- ln2_gain_grad: float32 [2048], P('fsdp')
- ln2_shift_grad: float32 [2048], P('fsdp')
- w_up_grad: float32 [2048, 8192], P('fsdp')
- up_bias_grad: float32 [8192], P('fsdp')
- w_down_grad: float32 [8192, 2048], P('fsdp')
- down_bias_grad: float32 [2048], P('fsdp')
The draws below stay inside these ranges and needn't reach their ends.
Inputs may be any that keep to these rules, and one draw needn't show every extreme that they name: `item_starts`: each row holds three items that lie in order inside its 1024 positions without intersection, each starting no earlier than the end of the one before; positions between or after them belong to no item. `item_lengths`: each item has at least 64 positions, the three of a row at most 1024 together.
All inputs are finite; a program needn't handle non-finite values. No bound on the sum of `pad_mask` on one device may be relied on, other than what follows from the above.
Results may differ from the reference program's by a relative error of at most 0.0095.
Values may be sent and summed in bfloat16 or wider, within the bound.
No kernel may reach another device: no remote copies, remote signals or barrier semaphores. Data moves between devices by JAX's collectives and lax.ppermute only.
A program may use at most 512 MiB of HBM per device.

```python
import jax
import jax.numpy as jnp
from jax import lax

D = 2048
H = 16
HD = 128
FF = 8192
LEN = 1024
ROWS = 8


def item_layout(key):
    row_keys = jax.random.split(jax.random.fold_in(key, 29), ROWS)
    row_numbers = jnp.arange(ROWS, dtype=jnp.int32)

    def one_row(row_key, row_number):
        parts = jax.random.split(row_key, 5)
        first_row = row_number == 0
        longest = jax.random.randint(parts[0], (), LEN // 2, 3 * LEN // 4 + 1)
        longest = jnp.where(first_row, 3 * LEN // 4, longest)
        middle = jax.random.randint(parts[1], (), LEN // 16, (LEN - longest) // 2 + 1)
        shortest = jax.random.randint(parts[2], (), LEN // 16, LEN - longest - middle + 1)
        shortest = jnp.where(first_row, LEN // 16, shortest)
        order = jax.random.permutation(parts[3], 3)
        order = jnp.where(first_row, jnp.arange(3, dtype=order.dtype), order)
        sizes_row = jnp.stack([longest, middle, shortest])[order]
        room = LEN - longest - middle - shortest
        spaces = jax.random.randint(parts[4], (3,), 0, room // 3 + 1)
        spaces = jnp.where(first_row, jnp.stack([0, 0, room]).astype(spaces.dtype), spaces)
        earlier = jnp.concatenate([jnp.zeros((1,), jnp.int32), jnp.cumsum(sizes_row)[:2].astype(jnp.int32)])
        offsets = jnp.cumsum(spaces).astype(jnp.int32) + earlier
        return (offsets.astype(jnp.int32), sizes_row.astype(jnp.int32))
    return jax.vmap(one_row)(row_keys, row_numbers)


def draw_item_starts(key, part):
    return item_layout(key)[0]


def draw_item_lengths(key, part):
    return item_layout(key)[1]


def place_ends(result, rng, smallest, largest):
    longest = result.shape.index(max(result.shape))
    spots = []
    for shift in (0, 1):
        where = [jax.random.randint(jax.random.fold_in(rng, axis), (), 0, length) for axis, length in enumerate(result.shape)]
        where[longest] = (where[longest] + shift) % result.shape[longest]
        spots.append(tuple(where))
    return result.at[spots[0]].set(smallest).at[spots[1]].set(largest)


def shard_levels(rng, extent, cuts, least, top_value):
    factor_of = 1.0
    for position, blocks in cuts:
        steps = jax.random.uniform(jax.random.fold_in(jax.random.fold_in(rng, 6), position), (blocks,), jnp.float32, least / len(cuts), top_value / len(cuts))
        factor_of = factor_of * jnp.repeat(jnp.exp(steps), extent[position] // blocks).reshape((-1,) + (1,) * (len(extent) - 1 - position))
    return factor_of


def bell_draw(rng, extent, deviation, bound, pieces=(), kind=jnp.bfloat16):
    level = shard_levels(rng, extent, pieces, -0.22, 0.18) if pieces else 1.0
    entries = jax.random.normal(rng, extent, jnp.float32) * deviation * level
    return jnp.minimum(jnp.maximum(entries, -bound), bound).astype(kind)


def setup_inputs(seed: int = 0) -> dict:
    streams_of = jax.random.split(jax.random.key(seed), 16)
    block_input = bell_draw(streams_of[0], (ROWS, LEN, D), 1.0, 6.0, ((0, 8), (1, 4)))
    cotangent = bell_draw(streams_of[1], (ROWS, LEN, D), 1.0, 6.0, ((0, 8), (1, 4)))
    item_starts = draw_item_starts(jax.random.fold_in(streams_of[15], 71), 0)
    item_lengths = draw_item_lengths(jax.random.fold_in(streams_of[15], 71), 0)
    pad_mask = place_ends((jax.random.randint(streams_of[4], (ROWS, LEN), 0, 8) < 7).astype(jnp.int32), jax.random.fold_in(streams_of[4], 1), 0, 1)
    ln1_gain = jnp.clip(1.0 + 0.1 * jax.random.normal(streams_of[5], (D,), jnp.float32), 0.5, 1.5)
    ln1_shift = bell_draw(streams_of[6], (D,), 0.5, 3.0, ((0, 8),), jnp.float32)
    w_qkv = bell_draw(streams_of[7], (D, 3 * D), D ** -0.5, 0.125, ((0, 8),))
    w_out = bell_draw(streams_of[8], (D, D), (D // 16) ** -0.5, 0.5, ((0, 8),))
    ln2_gain = jnp.clip(1.0 + 0.1 * jax.random.normal(streams_of[9], (D,), jnp.float32), 0.5, 1.5)
    ln2_shift = bell_draw(streams_of[10], (D,), 0.5, 3.0, ((0, 8),), jnp.float32)
    w_up = bell_draw(streams_of[11], (D, FF), D ** -0.5, 0.125, ((0, 8),))
    up_bias = bell_draw(streams_of[12], (FF,), 0.5, 3.0, ((0, 8),), jnp.float32)
    w_down = bell_draw(streams_of[13], (FF, D), FF ** -0.5, 0.0625, ((0, 8),))
    down_bias = bell_draw(streams_of[14], (D,), 0.5, 3.0, ((0, 8),), jnp.float32)
    return dict(block_input=block_input, cotangent=cotangent, item_starts=item_starts, item_lengths=item_lengths, pad_mask=pad_mask, ln1_gain=ln1_gain, ln1_shift=ln1_shift, w_qkv=w_qkv, w_out=w_out, ln2_gain=ln2_gain, ln2_shift=ln2_shift, w_up=w_up, up_bias=up_bias, w_down=w_down, down_bias=down_bias)


@jax.custom_vjp
def low(v):
    return lax.optimization_barrier(v.astype(jnp.bfloat16)).astype(jnp.float32)

@jax.custom_vjp
def low_back(v):
    return v

def low_keep(v):
    return (low(v), None)

def low_pass(kept, grad):
    return (grad,)

def back_keep(v):
    return (v, None)

def back_low(kept, grad):
    return (low(grad),)
low.defvjp(low_keep, low_pass)
low_back.defvjp(back_keep, back_low)
EPSILON = 1e-05
MASKED = -1e+30

def layer_norm(values, gain_vec, shift_vec):
    center = values - lax.optimization_barrier(jnp.mean(values, axis=-1, keepdims=True))
    spread = lax.optimization_barrier(jnp.mean(center * center, axis=-1, keepdims=True))
    return center * lax.rsqrt(spread + EPSILON) * gain_vec + shift_vec

def matmul(left, right):
    return jnp.dot(left, right, precision=lax.Precision.HIGHEST)

def item_numbers(starts, lengths, positions):
    inside = (positions[None, :] >= starts[:, None]) & (positions[None, :] < (starts + lengths)[:, None])
    labels = jnp.arange(1, starts.shape[0] + 1, dtype=jnp.int32)
    return (lax.optimization_barrier(jnp.sum(jnp.where(inside, labels[:, None], 0), axis=0)) - 1).astype(jnp.int32)

def visible_mask(query_pos, key_pos, query_item, key_item, key_pad):
    same_item = (query_item[:, None] == key_item[None, :]) & (query_item[:, None] >= 0)
    before = key_pos[None, :] < query_pos[:, None]
    return same_item & before & (key_pad[None, :] == 1) | (key_pos[None, :] == query_pos[:, None])

def row_forward(row_values, weights, visible):
    gain_one, shift_one, w_qkv, w_out, gain_two, shift_two, w_up, up_bias, w_down, down_bias = weights
    normed_one = low(layer_norm(row_values, gain_one, shift_one))
    projected = low(low_back(matmul(normed_one, w_qkv)))
    query_rows = projected[:, :D].reshape(LEN, H, HD)
    key_rows = projected[:, D:2 * D].reshape(LEN, H, HD)
    value_rows = projected[:, 2 * D:].reshape(LEN, H, HD)
    scores = jnp.einsum('qhd,khd->hqk', query_rows, key_rows, precision=lax.Precision.HIGHEST) * HD ** (-0.5)
    scores = low_back(scores)
    scores = jnp.where(visible[None], scores, MASKED)
    row_peak = lax.optimization_barrier(jnp.max(scores, axis=-1, keepdims=True))
    exp_scores = jnp.exp(scores - row_peak)
    attn_probs = exp_scores / lax.optimization_barrier(jnp.sum(exp_scores, axis=-1, keepdims=True))
    mixed_rows = jnp.einsum('hqk,khd->qhd', low(attn_probs), value_rows, precision=lax.Precision.HIGHEST)
    mixed_rows = low(low_back(mixed_rows.reshape(LEN, D)))
    residual_one = row_values + low_back(matmul(mixed_rows, w_out))
    normed_two = low(layer_norm(residual_one, gain_two, shift_two))
    hidden_pre = low_back(matmul(normed_two, w_up) + up_bias)
    activated = low(jax.nn.gelu(hidden_pre))
    return residual_one + low_back(matmul(activated, w_down) + down_bias)

def reference(block_input, cotangent, item_starts, item_lengths, pad_mask, ln1_gain, ln1_shift, w_qkv, w_out, ln2_gain, ln2_shift, w_up, up_bias, w_down, down_bias):
    params = tuple((weight.astype(jnp.float32) for weight in (ln1_gain, ln1_shift, w_qkv, w_out, ln2_gain, ln2_shift, w_up, up_bias, w_down, down_bias)))
    positions = jnp.arange(LEN, dtype=jnp.int32)

    def one_row(running, row_data):
        row_input, row_cot, starts, lengths, row_pad = row_data
        item_label = item_numbers(starts, lengths, positions)
        visible = visible_mask(positions, positions, item_label, item_label, row_pad)

        def forward(row_values, *weights):
            return row_forward(row_values, weights, visible)
        output, pullback = jax.vjp(forward, row_input.astype(jnp.float32), *params)
        all_grads = pullback(row_cot.astype(jnp.float32))
        running = tuple((total + grad_part for total, grad_part in zip(running, all_grads[1:])))
        return (running, (output.astype(jnp.bfloat16), all_grads[0]))
    zero_grads = tuple((jnp.zeros_like(weight) for weight in params))
    totals, (outputs, input_grads) = lax.scan(one_row, zero_grads, (block_input, cotangent, item_starts, item_lengths, pad_mask))
    return (outputs, input_grads, totals[0], totals[1], totals[2], totals[3], totals[4], totals[5], totals[6], totals[7], totals[8], totals[9])
```

```python
import functools

import jax
import jax.numpy as jnp
import numpy as np
from jax import lax
from jax.experimental import pallas as pl
from jax.experimental.pallas import tpu as pltpu
from jax.sharding import Mesh
from jax.sharding import PartitionSpec as P

H = 16
HD = 128


EPSILON = 1e-05
MASKED = -1e30
SWAP = ((0, 1), (1, 0))
VMEM_LIMIT = 56 << 20
GELU_A = float(np.sqrt(2.0 / np.pi))
GELU_B = 0.044715


def layer_norm(values, gain_vec, shift_vec):
    center = values - jnp.mean(values, axis=-1, keepdims=True)
    spread = jnp.mean(center * center, axis=-1, keepdims=True)
    return center * lax.rsqrt(spread + EPSILON) * gain_vec + shift_vec


def contract_rows(left, right):
    return lax.dot_general(
        left, right, (((0,), (0,)), ((), ())), preferred_element_type=jnp.float32
    )


def times_transpose(left, right):
    return lax.dot_general(
        left, right, (((1,), (1,)), ((), ())), preferred_element_type=jnp.float32
    )


def item_numbers(starts, lengths, positions):
    inside = (positions[None, :] >= starts[:, None]) & (
        positions[None, :] < (starts + lengths)[:, None]
    )
    labels = jnp.arange(1, starts.shape[0] + 1, dtype=jnp.int32)
    return jnp.sum(jnp.where(inside, labels[:, None], 0), axis=0) - 1


def visible_mask(query_pos, key_pos, query_item, key_item, key_pad):
    same_item = (query_item[:, None] == key_item[None, :]) & (query_item[:, None] >= 0)
    before = key_pos[None, :] < query_pos[:, None]
    return same_item & before & (key_pad[None, :] == 1) | (key_pos[None, :] == query_pos[:, None])


def masked_scores(query_rows, key_rows, visible, score_scale):
    scores = (
        jnp.einsum("qhd,khd->hqk", query_rows, key_rows, preferred_element_type=jnp.float32)
        * score_scale
    )
    return jnp.where(visible[None], scores, MASKED)


def attend_rows(query_rows, key_rows, value_rows, visible, score_scale):
    scores = masked_scores(query_rows, key_rows, visible, score_scale)
    row_peak = jnp.max(scores, axis=-1, keepdims=True)
    exp_scores = jnp.exp(scores - row_peak)
    row_total = jnp.sum(exp_scores, axis=-1, keepdims=True)
    attn_probs = exp_scores / row_total
    mixed_rows = jnp.einsum(
        "hqk,khd->qhd",
        attn_probs.astype(jnp.bfloat16),
        value_rows,
        preferred_element_type=jnp.float32,
    )
    return (mixed_rows, row_peak + jnp.log(row_total))


def attend_back(query_rows, key_rows, value_rows, visible, log_total, mixed_grad, score_scale):
    scores = masked_scores(query_rows, key_rows, visible, score_scale)
    attn_probs = jnp.exp(scores - log_total)
    prob_grad = jnp.einsum(
        "qhd,khd->hqk", mixed_grad, value_rows, preferred_element_type=jnp.float32
    )
    value_part = jnp.einsum(
        "hqk,qhd->khd",
        attn_probs.astype(jnp.bfloat16),
        mixed_grad,
        preferred_element_type=jnp.float32,
    )
    inner_sum = jnp.sum(prob_grad * attn_probs, axis=-1, keepdims=True)
    score_grad = (attn_probs * (prob_grad - inner_sum)).astype(jnp.bfloat16)
    query_grad = (
        jnp.einsum("hqk,khd->qhd", score_grad, key_rows, preferred_element_type=jnp.float32)
        * score_scale
    )
    key_part = (
        jnp.einsum("hqk,qhd->khd", score_grad, query_rows, preferred_element_type=jnp.float32)
        * score_scale
    )
    return (query_grad.astype(jnp.bfloat16), key_part, value_part)


def plain_shards(
    block_input,
    cotangent,
    item_starts,
    item_lengths,
    pad_mask,
    ln1_gain,
    ln1_shift,
    w_qkv,
    w_out,
    ln2_gain,
    ln2_shift,
    w_up,
    up_bias,
    w_down,
    down_bias,
):
    rows_here, tok_count, model_width = block_input.shape
    seq_count = lax.axis_size("seq")
    shard_count = lax.axis_size("fsdp")
    length = tok_count * seq_count
    score_scale = HD ** (-0.5)
    piece_d = ln1_gain.shape[0]
    seq_first = lax.axis_index("seq") * tok_count
    packed = jnp.concatenate([ln1_gain, ln1_shift, ln2_gain, ln2_shift, down_bias, up_bias])
    vector_table = lax.all_gather(packed, "fsdp", axis=0, tiled=True).reshape(shard_count, -1)

    def vector_part(slot):
        return vector_table[:, slot * piece_d : (slot + 1) * piece_d].reshape(-1)

    gain_one, shift_one, gain_two, shift_two, bias_down = [vector_part(slot) for slot in range(5)]
    bias_up = vector_table[:, 5 * piece_d :].reshape(-1)
    qkv_full, out_full = (
        lax.all_gather(w_qkv, "fsdp", axis=0, tiled=True),
        lax.all_gather(w_out, "fsdp", axis=0, tiled=True),
    )
    inputs = block_input.reshape(rows_here * tok_count, model_width).astype(jnp.float32)
    normed_one = layer_norm(inputs, gain_one, shift_one).astype(jnp.bfloat16)
    projected = jnp.dot(normed_one, qkv_full, preferred_element_type=jnp.float32).astype(
        jnp.bfloat16
    )
    query_all = projected[:, :model_width].reshape(rows_here, tok_count, H, HD)
    kv_local = projected[:, model_width:].reshape(rows_here, tok_count, 2 * model_width)
    kv_whole = lax.all_gather(kv_local, "seq", axis=1, tiled=True)
    key_all = kv_whole[:, :, :model_width].reshape(rows_here, length, H, HD)
    value_all = kv_whole[:, :, model_width:].reshape(rows_here, length, H, HD)
    positions = jnp.arange(length, dtype=jnp.int32)
    query_pos = seq_first + jnp.arange(tok_count, dtype=jnp.int32)
    row_index = 0
    item_label = item_numbers(item_starts[row_index], item_lengths[row_index], positions)
    query_item = lax.dynamic_slice_in_dim(item_label, seq_first, tok_count)
    visible = visible_mask(query_pos, positions, query_item, item_label, pad_mask[row_index])
    mixed_part, log_total = attend_rows(
        query_all[row_index], key_all[row_index], value_all[row_index], visible, score_scale
    )
    visible_list = [visible]
    mixed_list = [mixed_part]
    logsum_list = [log_total]
    mixed_all = (
        jnp.stack(mixed_list).reshape(rows_here * tok_count, model_width).astype(jnp.bfloat16)
    )
    residual_one = inputs + jnp.dot(mixed_all, out_full, preferred_element_type=jnp.float32)
    up_full, down_full = (
        lax.all_gather(w_up, "fsdp", axis=0, tiled=True),
        lax.all_gather(w_down, "fsdp", axis=0, tiled=True),
    )
    normed_two = layer_norm(residual_one, gain_two, shift_two).astype(jnp.bfloat16)
    hidden_pre = jnp.dot(normed_two, up_full, preferred_element_type=jnp.float32) + bias_up
    activated = jax.nn.gelu(hidden_pre).astype(jnp.bfloat16)
    block_output = (
        residual_one + jnp.dot(activated, down_full, preferred_element_type=jnp.float32) + bias_down
    )
    output_shard = block_output.astype(jnp.bfloat16).reshape(rows_here, tok_count, model_width)
    up_full, down_full = (
        lax.all_gather(w_up, "fsdp", axis=0, tiled=True),
        lax.all_gather(w_down, "fsdp", axis=0, tiled=True),
    )
    cot_flat = cotangent.reshape(rows_here * tok_count, model_width)
    cot_wide = cot_flat.astype(jnp.float32)
    down_grad = contract_rows(activated, cot_flat)
    down_bias_part = jnp.sum(cot_wide, axis=0)
    act_grad = times_transpose(cot_flat, down_full)
    gelu_back = jax.vjp(jax.nn.gelu, hidden_pre)[1]
    hidden_grad = gelu_back(act_grad)[0].astype(jnp.bfloat16)
    up_grad = contract_rows(normed_two, hidden_grad)
    up_bias_part = jnp.sum(hidden_grad.astype(jnp.float32), axis=0)
    norm_two_grad = times_transpose(hidden_grad, up_full)
    norm_two_back = jax.vjp(layer_norm, residual_one, gain_two, shift_two)[1]
    resid_part, gain_two_grad, shift_two_grad = norm_two_back(norm_two_grad)
    residual_grad = cot_wide + resid_part
    up_sum, down_sum = (
        lax.psum_scatter(up_grad, "fsdp", scatter_dimension=0, tiled=True),
        lax.psum_scatter(down_grad, "fsdp", scatter_dimension=0, tiled=True),
    )
    qkv_full, out_full = (
        lax.all_gather(w_qkv, "fsdp", axis=0, tiled=True),
        lax.all_gather(w_out, "fsdp", axis=0, tiled=True),
    )
    branch_grad = residual_grad.astype(jnp.bfloat16)
    out_grad = contract_rows(mixed_all, branch_grad)
    mixed_grad = (
        times_transpose(branch_grad, out_full)
        .astype(jnp.bfloat16)
        .reshape(rows_here, tok_count, H, HD)
    )
    row_index = 0
    query_grad, key_part, value_part = attend_back(
        query_all[row_index],
        key_all[row_index],
        value_all[row_index],
        visible_list[row_index],
        logsum_list[row_index],
        mixed_grad[row_index],
        score_scale,
    )
    query_list = [query_grad.reshape(tok_count, model_width)]
    kv_list = [
        jnp.concatenate(
            [key_part.reshape(length, model_width), value_part.reshape(length, model_width)], axis=1
        )
    ]
    kv_terms = jnp.stack(kv_list)
    kv_grad = lax.psum_scatter(kv_terms, "seq", scatter_dimension=1, tiled=True).astype(
        jnp.bfloat16
    )
    proj_grad = jnp.concatenate(
        [
            jnp.stack(query_list).reshape(rows_here * tok_count, model_width),
            kv_grad.reshape(rows_here * tok_count, 2 * model_width),
        ],
        axis=1,
    )
    qkv_grad = contract_rows(normed_one, proj_grad)
    norm_one_grad = times_transpose(proj_grad, qkv_full)
    norm_one_back = jax.vjp(layer_norm, inputs, gain_one, shift_one)[1]
    input_part, gain_one_grad, shift_one_grad = norm_one_back(norm_one_grad)
    input_grad = (residual_grad + input_part).reshape(rows_here, tok_count, model_width)
    vector_grad = jnp.concatenate(
        [
            piece_grad.reshape(shard_count, -1)
            for piece_grad in (
                gain_one_grad,
                shift_one_grad,
                gain_two_grad,
                shift_two_grad,
                down_bias_part,
                up_bias_part,
            )
        ],
        axis=1,
    ).reshape(-1)
    qkv_sum, out_sum, vector_sum = (
        lax.psum_scatter(qkv_grad, "fsdp", scatter_dimension=0, tiled=True),
        lax.psum_scatter(out_grad, "fsdp", scatter_dimension=0, tiled=True),
        lax.psum_scatter(vector_grad, "fsdp", scatter_dimension=0, tiled=True),
    )
    up_total, down_total, qkv_total, out_total, vector_total = lax.psum(
        (up_sum, down_sum, qkv_sum, out_sum, vector_sum), "seq"
    )
    gain_one_out = vector_total[0:piece_d]
    shift_one_out = vector_total[piece_d : 2 * piece_d]
    gain_two_out = vector_total[2 * piece_d : 3 * piece_d]
    shift_two_out = vector_total[3 * piece_d : 4 * piece_d]
    down_bias_out = vector_total[4 * piece_d : 5 * piece_d]
    up_bias_out = vector_total[5 * piece_d :]
    return (
        output_shard,
        input_grad,
        gain_one_out,
        shift_one_out,
        qkv_total,
        out_total,
        gain_two_out,
        shift_two_out,
        up_total,
        up_bias_out,
        down_total,
        down_bias_out,
    )


def piece_owner(zi, xi, z_count):
    return [
        lax.rem(zi - j + z_count, z_count) * 2 + jnp.bitwise_xor(xi, dx)
        for dx in range(2)
        for j in range(z_count)
    ]


def gather_pieces(shard, z_count):
    line = [shard]
    for j in range(1, z_count):
        line.append(lax.ppermute(shard, "z", [(i, (i + j) % z_count) for i in range(z_count)]))
    return line + [lax.ppermute(piece, "x", SWAP) for piece in line]


def reduce_pieces(pieces, z_count):
    wide = jnp.float32
    far = [lax.ppermute(piece, "x", SWAP) for piece in pieces[z_count:]]
    total = pieces[0].astype(wide) + far[0].astype(wide)
    for j in range(1, z_count):
        part = (pieces[j].astype(wide) + far[j].astype(wide)).astype(jnp.bfloat16)
        total = total + lax.ppermute(
            part, "z", [(i, (i - j) % z_count) for i in range(z_count)]
        ).astype(wide)
    return total.astype(jnp.bfloat16)


def seq_pieces(block):
    other = lax.ppermute(block, "y", SWAP)
    return [block, lax.ppermute(block, "c", SWAP), other, lax.ppermute(other, "c", SWAP)]


def by_bit(bit, mine, theirs):
    return jnp.where(bit == 0, mine, theirs), jnp.where(bit == 0, theirs, mine)


def gather_tokens(block, yi, ci):
    parts = seq_pieces(block)
    near = by_bit(ci, parts[0], parts[1])
    far = by_bit(ci, parts[2], parts[3])
    rows = [jnp.where(yi == 0, n, f) for n, f in zip(near, far)]
    rows += [jnp.where(yi == 0, f, n) for n, f in zip(near, far)]
    return jnp.concatenate(rows, axis=0)


def scatter_tokens(partial, yi, ci):
    tokens = partial.shape[0] // 4
    parts = partial.reshape(2, 2, tokens, partial.shape[1])
    away = lax.dynamic_index_in_dim(parts, 1 - ci, 1, keepdims=False)
    home = lax.dynamic_index_in_dim(parts, ci, 1, keepdims=False)
    total = home.astype(jnp.float32) + lax.ppermute(away, "c", SWAP).astype(jnp.float32)
    away = lax.dynamic_index_in_dim(total, 1 - yi, 0, keepdims=False).astype(jnp.bfloat16)
    home = lax.dynamic_index_in_dim(total, yi, 0, keepdims=False)
    return home + lax.ppermute(away, "y", SWAP).astype(jnp.float32)


def params(limit=VMEM_LIMIT):
    return pltpu.CompilerParams(vmem_limit_bytes=limit)


def load_weight(offsets, pieces, held, sems):
    copies = []
    for p, piece in enumerate(pieces):
        rows, cols = piece.shape
        row = pl.multiple_of(offsets[0, p], rows)
        col = pl.multiple_of(offsets[1, p], cols)
        copies.append(
            pltpu.make_async_copy(
                piece, held.at[pl.ds(row, rows), pl.ds(col, cols)], sems.at[p]
            )
        )
    for copy in copies:
        copy.start()
    for copy in copies:
        copy.wait()


def weight_matmul(left, pieces, offsets, shape, back, body, extras, outs, tile, chunk):
    rows = left.shape[0]
    depth, width = shape
    out_width = depth if back else width
    n_pieces, n_extras = len(pieces), len(extras)

    def kernel(offs_ref, left_ref, *refs):
        piece_refs = refs[:n_pieces]
        extra_refs = refs[n_pieces : n_pieces + n_extras]
        out_refs = refs[n_pieces + n_extras : -2]
        held, sems = refs[-2:]

        @pl.when(pl.program_id(0) == 0)
        def _():
            load_weight(offs_ref, piece_refs, held, sems)

        for start in range(0, out_width, chunk):
            cols = pl.ds(start, chunk)
            if back:
                values = lax.dot_general(
                    left_ref[...],
                    held[cols, :],
                    (((1,), (1,)), ((), ())),
                    preferred_element_type=jnp.float32,
                )
            else:
                values = jnp.dot(
                    left_ref[...], held[:, cols], preferred_element_type=jnp.float32
                )
            body(values, cols, extra_refs, out_refs, pl.program_id(0) == 0)

    def tile_spec(array_rows, array_cols):
        if array_rows == 1:
            return pl.BlockSpec((1, array_cols), lambda i, offs: (0, 0))
        return pl.BlockSpec((tile, array_cols), lambda i, offs: (i, 0))

    flops = 2 * rows * depth * width
    moved = 2 * (left.size + depth * width) + sum(
        a.size * a.dtype.itemsize for a in list(extras) + list(outs)
    )
    return pl.pallas_call(
        kernel,
        grid_spec=pltpu.PrefetchScalarGridSpec(
            num_scalar_prefetch=1,
            grid=(rows // tile,),
            in_specs=[pl.BlockSpec((tile, left.shape[1]), lambda i, offs: (i, 0))]
            + [pl.BlockSpec(memory_space=pl.ANY)] * n_pieces
            + [tile_spec(*a.shape) for a in extras],
            out_specs=[tile_spec(*a.shape) for a in outs],
            scratch_shapes=[
                pltpu.VMEM((depth, width), jnp.bfloat16),
                pltpu.SemaphoreType.DMA((n_pieces,)),
            ],
        ),
        out_shape=list(outs),
        cost_estimate=pl.CostEstimate(flops=flops, bytes_accessed=moved, transcendentals=0),
        compiler_params=params(),
    )(offsets, left, *pieces, *extras)


def store_low(values, cols, extra_refs, out_refs, first):
    out_refs[0][:, cols] = values.astype(jnp.bfloat16)


def store_gelu(values, cols, extra_refs, out_refs, first):
    hidden = values + extra_refs[0][:, cols]
    square = hidden * hidden
    bend = jnp.tanh(GELU_A * hidden * (1.0 + GELU_B * square))
    half = 0.5 * (1.0 + bend)
    out_refs[0][:, cols] = (hidden * half).astype(jnp.bfloat16)
    slope = half + 0.5 * hidden * (1.0 - bend * bend) * (
        GELU_A * (1.0 + 3.0 * GELU_B * square)
    )
    out_refs[1][:, cols] = slope


def store_hidden_grad(values, cols, extra_refs, out_refs, first):
    low = (values * extra_refs[0][:, cols]).astype(jnp.bfloat16)
    out_refs[0][:, cols] = low
    column_sum = jnp.sum(low.astype(jnp.float32), axis=0, keepdims=True)
    sums = out_refs[1]

    @pl.when(first)
    def _():
        sums[:, cols] = column_sum

    @pl.when(jnp.logical_not(first))
    def _():
        sums[:, cols] += column_sum


def weight_grad(left, right, owners, block):
    rows, depth = left.shape
    width = right.shape[1]
    count = depth // block

    def kernel(owner_ref, left_ref, right_ref, *refs):
        outs, held, sems = refs[:count], refs[count], refs[count + 1]
        step = pl.program_id(0)
        slot = lax.rem(step, 2)

        @pl.when(step >= 2)
        def _():
            pltpu.make_async_copy(held.at[slot], outs[0], sems.at[slot]).wait()

        held[slot] = lax.dot_general(
            left_ref[...],
            right_ref[...],
            (((0,), (0,)), ((), ())),
            preferred_element_type=jnp.float32,
        ).astype(jnp.bfloat16)
        for k in range(count):

            @pl.when(step == k)
            def _():
                pltpu.make_async_copy(held.at[slot], outs[k], sems.at[slot]).start()

        @pl.when(step == count - 1)
        def _():
            pltpu.make_async_copy(held.at[1 - slot], outs[0], sems.at[1 - slot]).wait()
            pltpu.make_async_copy(held.at[slot], outs[0], sems.at[slot]).wait()

    return pl.pallas_call(
        kernel,
        grid_spec=pltpu.PrefetchScalarGridSpec(
            num_scalar_prefetch=1,
            grid=(count,),
            in_specs=[
                pl.BlockSpec((rows, block), lambda k, owner: (0, owner[k])),
                pl.BlockSpec((rows, width), lambda k, owner: (0, 0)),
            ],
            out_specs=[pl.BlockSpec(memory_space=pl.ANY)] * count,
            scratch_shapes=[
                pltpu.VMEM((2, block, width), jnp.bfloat16),
                pltpu.SemaphoreType.DMA((2,)),
            ],
        ),
        out_shape=[jax.ShapeDtypeStruct((block, width), jnp.bfloat16)] * count,
        cost_estimate=pl.CostEstimate(
            flops=2 * rows * depth * width,
            bytes_accessed=2 * (left.size + right.size + depth * width),
            transcendentals=0,
        ),
        compiler_params=params(),
    )(owners, left, right)


def visible_tile(query_item, key_item, first_query, n_query, n_key):
    query_pos = first_query + lax.broadcasted_iota(jnp.int32, (n_query, n_key), 0)
    key_pos = lax.broadcasted_iota(jnp.int32, (n_query, n_key), 1)
    return ((query_item == key_item) & (key_pos < query_pos)) | (key_pos == query_pos)


def head_spec(length, first):
    return pl.BlockSpec((length, HD), lambda h: (0, first + h))


def attention(projected, query_item, key_item, heads, tile):
    length = projected.shape[0]
    scale = HD ** (-0.5)

    def kernel(q_ref, k_ref, v_ref, qi_ref, ki_ref, mixed_ref, log_ref):
        for start in range(0, length, tile):
            stop = start + tile
            rows = slice(start, stop)
            scores = (
                lax.dot_general(
                    q_ref[rows, :],
                    k_ref[:stop, :],
                    (((1,), (1,)), ((), ())),
                    preferred_element_type=jnp.float32,
                )
                * scale
            )
            seen = visible_tile(qi_ref[rows, :], ki_ref[:, :stop], start, tile, stop)
            scores = jnp.where(seen, scores, MASKED)
            peak = jnp.max(scores, axis=-1, keepdims=True)
            weights = jnp.exp(scores - peak)
            total = jnp.sum(weights, axis=-1, keepdims=True)
            probs = (weights * (1.0 / total)).astype(jnp.bfloat16)
            mixed_ref[rows, :] = jnp.dot(
                probs, v_ref[:stop, :], preferred_element_type=jnp.float32
            ).astype(jnp.bfloat16)
            log_ref[0, rows, :] = peak + jnp.log(total)

    whole = lambda rows, cols: pl.BlockSpec((rows, cols), lambda h: (0, 0))
    return pl.pallas_call(
        kernel,
        grid=(heads,),
        in_specs=[head_spec(length, g * heads) for g in range(3)]
        + [whole(length, 1), whole(1, length)],
        out_specs=[head_spec(length, 0), pl.BlockSpec((1, length, 1), lambda h: (h, 0, 0))],
        out_shape=[
            jax.ShapeDtypeStruct((length, heads * HD), jnp.bfloat16),
            jax.ShapeDtypeStruct((heads, length, 1), jnp.float32),
        ],
        cost_estimate=pl.CostEstimate(
            flops=4 * heads * length * length * HD,
            bytes_accessed=8 * length * heads * HD,
            transcendentals=heads * length * length,
        ),
        compiler_params=params(),
    )(projected, projected, projected, query_item, key_item)


def attention_back(projected, mixed_grad, log_total, query_item, key_item, heads, tile):
    length = projected.shape[0]
    scale = HD ** (-0.5)

    def kernel(q_ref, k_ref, v_ref, g_ref, log_ref, qi_ref, ki_ref, grad_ref, dk_ref, dv_ref):
        head = pl.program_id(0)

        def place(group):
            return pl.ds(pl.multiple_of((group * heads + head) * HD, HD), HD)

        for start in reversed(range(0, length, tile)):
            stop = start + tile
            rows = slice(start, stop)
            query, grad = q_ref[rows, :], g_ref[rows, :]
            key, value = k_ref[:stop, :], v_ref[:stop, :]
            scores = (
                lax.dot_general(
                    query, key, (((1,), (1,)), ((), ())), preferred_element_type=jnp.float32
                )
                * scale
            )
            seen = visible_tile(qi_ref[rows, :], ki_ref[:, :stop], start, tile, stop)
            probs = jnp.exp(jnp.where(seen, scores, MASKED) - log_ref[0, rows, :])
            prob_grad = lax.dot_general(
                grad, value, (((1,), (1,)), ((), ())), preferred_element_type=jnp.float32
            )
            inner = jnp.sum(prob_grad * probs, axis=-1, keepdims=True)
            score_grad = (probs * (prob_grad - inner)).astype(jnp.bfloat16)
            grad_ref[rows, place(0)] = (
                jnp.dot(score_grad, key, preferred_element_type=jnp.float32) * scale
            ).astype(jnp.bfloat16)
            key_part = lax.dot_general(
                score_grad, query, (((0,), (0,)), ((), ())), preferred_element_type=jnp.float32
            )
            value_part = lax.dot_general(
                probs.astype(jnp.bfloat16),
                grad,
                (((0,), (0,)), ((), ())),
                preferred_element_type=jnp.float32,
            )
            if stop == length:
                dk_ref[...] = key_part
                dv_ref[...] = value_part
            else:
                dk_ref[:stop, :] += key_part
                dv_ref[:stop, :] += value_part
        grad_ref[:, place(1)] = (dk_ref[...] * scale).astype(jnp.bfloat16)
        grad_ref[:, place(2)] = dv_ref[...].astype(jnp.bfloat16)

    whole = lambda rows, cols: pl.BlockSpec((rows, cols), lambda h: (0, 0))
    return pl.pallas_call(
        kernel,
        grid=(heads,),
        in_specs=[head_spec(length, g * heads) for g in range(3)]
        + [
            head_spec(length, 0),
            pl.BlockSpec((1, length, 1), lambda h: (h, 0, 0)),
            whole(length, 1),
            whole(1, length),
        ],
        out_specs=whole(length, 3 * heads * HD),
        out_shape=jax.ShapeDtypeStruct((length, 3 * heads * HD), jnp.bfloat16),
        scratch_shapes=[pltpu.VMEM((length, HD), jnp.float32)] * 2,
        cost_estimate=pl.CostEstimate(
            flops=10 * heads * length * length * HD,
            bytes_accessed=16 * length * heads * HD,
            transcendentals=heads * length * length,
        ),
        compiler_params=params(),
    )(projected, projected, projected, mixed_grad, log_total, query_item, key_item)


def widen(pieces, places, grid, piece_block, out_block, out_index, out_shape, write):
    def kernel(place_ref, *refs):
        for r in range(4):
            write(place_ref[r], refs[r], refs[4])

    return pl.pallas_call(
        kernel,
        grid_spec=pltpu.PrefetchScalarGridSpec(
            num_scalar_prefetch=1,
            grid=(grid,),
            in_specs=[pl.BlockSpec(piece_block[0], lambda i, pos: piece_block[1](i))] * 4,
            out_specs=pl.BlockSpec(out_block, lambda i, pos: out_index(i)),
        ),
        out_shape=jax.ShapeDtypeStruct(out_shape, jnp.float32),
        cost_estimate=pl.CostEstimate(
            flops=0, bytes_accessed=6 * int(np.prod(out_shape)), transcendentals=0
        ),
        compiler_params=params(),
    )(places, *pieces)


def widen_columns(pieces, places, blocks):
    rows, width = pieces[0].shape
    part = width // blocks

    def write(pos, piece, out):
        out[:, pl.ds(pl.multiple_of(pos * part, part), part)] = piece[...].astype(jnp.float32)

    return widen(
        pieces,
        places,
        blocks,
        ((rows, part), lambda i: (0, i)),
        (rows, 4 * part),
        lambda i: (0, i),
        (rows, 4 * width),
        write,
    )


def widen_rows(pieces, places):
    rows, width = pieces[0].shape

    def write(pos, piece, out):
        @pl.when(pos == pl.program_id(0))
        def _():
            out[...] = piece[...].astype(jnp.float32)

    return widen(
        pieces,
        places,
        4,
        ((rows, width), lambda i: (0, 0)),
        (rows, width),
        lambda i: (i, 0),
        (4 * rows, width),
        write,
    )


def widen_heads(pieces, places):
    rows, width = pieces[0].shape
    part = width // 3

    def write(pos, piece, out):
        first = lax.div(pos, 2) * part * 2 + lax.rem(pos, 2) * HD
        for i in range(part // HD):
            cols = pl.ds(pl.multiple_of(first + 2 * i * HD, HD), HD)
            out[:, cols] = piece[:, i * HD : (i + 1) * HD].astype(jnp.float32)

    return widen(
        pieces,
        places,
        3,
        ((rows, part), lambda i: (0, i)),
        (rows, 4 * part),
        lambda i: (0, i),
        (rows, 4 * width),
        write,
    )


def widen_quarters(pieces, places):
    rows, width = pieces[0].shape

    def write(pos, piece, out):
        row = pl.multiple_of(lax.rem(pos, 2) * rows, rows)
        col = pl.multiple_of(lax.div(pos, 2) * width, width)
        out[pl.ds(row, rows), pl.ds(col, width)] = piece[...].astype(jnp.float32)

    return widen(
        pieces,
        places,
        1,
        ((rows, width), lambda i: (0, 0)),
        (2 * rows, 2 * width),
        lambda i: (0, 0),
        (2 * rows, 2 * width),
        write,
    )


def norm_back(values, gain_vec, incoming):
    center = values - jnp.mean(values, axis=-1, keepdims=True)
    spread = jnp.mean(center * center, axis=-1, keepdims=True)
    inverse = lax.rsqrt(spread + EPSILON)
    unit = center * inverse
    scaled = incoming * gain_vec
    inner = jnp.mean(scaled * unit, axis=-1, keepdims=True)
    grad = (scaled - jnp.mean(scaled, axis=-1, keepdims=True) - unit * inner) * inverse
    return grad, jnp.sum(incoming * unit, axis=0), jnp.sum(incoming, axis=0)


def split_shards(
    block_input,
    cotangent,
    item_starts,
    item_lengths,
    pad_mask,
    ln1_gain,
    ln1_shift,
    w_qkv,
    w_out,
    ln2_gain,
    ln2_shift,
    w_up,
    up_bias,
    w_down,
    down_bias,
):
    low, wide = jnp.bfloat16, jnp.float32
    z_count = lax.axis_size("z")
    shard_count = 2 * z_count
    zi, xi, yi, ci = [lax.axis_index(name) for name in ("z", "x", "y", "c")]
    si = 2 * yi + ci
    tok_count, model = block_input.shape[1:]
    length = 4 * tok_count
    piece_d, ff_piece = ln1_gain.shape[0], up_bias.shape[0]
    ff_part = ff_piece // 4
    ff_here = ff_part * shard_count
    heads = H // 4
    owners = jnp.stack(piece_owner(zi, xi, z_count)).astype(jnp.int32)
    zeros = jnp.zeros_like(owners)
    places = jnp.stack([jnp.bitwise_xor(si, r) for r in range(4)]).astype(jnp.int32)

    packed = jnp.concatenate([ln1_gain, ln1_shift, ln2_gain, ln2_shift, down_bias, up_bias])
    vector_stack = jnp.stack(gather_pieces(packed, z_count))
    hit = owners[None, :] == jnp.arange(shard_count, dtype=jnp.int32)[:, None]
    vector_table = jnp.sum(jnp.where(hit[:, :, None], vector_stack[None], 0.0), axis=1)

    def vector_part(slot):
        return vector_table[:, slot * piece_d : (slot + 1) * piece_d].reshape(-1)

    gain_one, shift_one, gain_two, shift_two, bias_down = [vector_part(slot) for slot in range(5)]
    bias_up = lax.dynamic_index_in_dim(
        vector_table[:, 5 * piece_d :].reshape(shard_count, 4, ff_part), si, 1, keepdims=False
    ).reshape(1, ff_here)

    qkv_slice = w_qkv.reshape(piece_d, 3, 2, heads, 2, HD)
    qkv_slice = lax.dynamic_index_in_dim(qkv_slice, yi, 2, keepdims=False)
    qkv_slice = lax.dynamic_index_in_dim(qkv_slice, ci, 3, keepdims=False)
    qkv_slice = qkv_slice.reshape(piece_d, 3 * heads * HD)
    out_slice = w_out.reshape(2, piece_d // 2, 2, model // 2)
    out_slice = lax.dynamic_index_in_dim(out_slice, yi, 2, keepdims=False)
    out_slice = lax.dynamic_index_in_dim(out_slice, ci, 0, keepdims=False)
    up_slice = lax.dynamic_index_in_dim(
        w_up.reshape(piece_d, shard_count, 4, ff_part), si, 2, keepdims=False
    ).reshape(piece_d, ff_here)
    down_slice = lax.dynamic_index_in_dim(
        w_down.reshape(4, ff_part, model), si, 0, keepdims=False
    )

    qkv_parts = gather_pieces(qkv_slice, z_count)
    out_parts = gather_pieces(out_slice, z_count)
    out_parts = out_parts + [lax.ppermute(piece, "y", SWAP) for piece in out_parts]
    up_parts = gather_pieces(up_slice, z_count)
    down_parts = gather_pieces(down_slice, z_count)
    row_offsets = jnp.stack([owners * piece_d, zeros])
    out_offsets = jnp.stack(
        [
            jnp.concatenate([owners, owners]) * (piece_d // 2),
            jnp.concatenate([zeros + yi, zeros + 1 - yi]) * (model // 2),
        ]
    )
    ff_offsets = jnp.stack([owners * ff_part, zeros])

    def shape(rows, cols, kind=low):
        return jax.ShapeDtypeStruct((rows, cols), kind)

    inputs = block_input.reshape(tok_count, model).astype(wide)
    normed_one = gather_tokens(layer_norm(inputs, gain_one, shift_one).astype(low), yi, ci)
    (projected,) = weight_matmul(
        normed_one,
        qkv_parts,
        row_offsets,
        (model, 3 * heads * HD),
        False,
        store_low,
        (),
        (shape(length, 3 * heads * HD),),
        256,
        512,
    )
    positions = jnp.arange(length, dtype=jnp.int32)
    item_label = item_numbers(item_starts[0], item_lengths[0], positions)
    query_item = item_label[:, None]
    key_item = jnp.where((item_label >= 0) & (pad_mask[0] == 1), item_label, -2)[None, :]
    mixed_heads, log_total = attention(projected, query_item, key_item, heads, 256)
    halves = mixed_heads.reshape(2, 2 * tok_count, heads * HD)
    away = lax.dynamic_index_in_dim(halves, 1 - yi, 0, keepdims=False)
    home = lax.dynamic_index_in_dim(halves, yi, 0, keepdims=False)
    mixed = jnp.concatenate(by_bit(yi, home, lax.ppermute(away, "y", SWAP)), axis=1)
    (out_partial,) = weight_matmul(
        mixed,
        out_parts,
        out_offsets,
        (model // 2, model),
        False,
        store_low,
        (),
        (shape(2 * tok_count, model),),
        256,
        512,
    )
    halves = out_partial.reshape(2, tok_count, model)
    away = lax.dynamic_index_in_dim(halves, 1 - ci, 0, keepdims=False)
    home = lax.dynamic_index_in_dim(halves, ci, 0, keepdims=False)
    residual_one = (
        inputs + home.astype(wide) + lax.ppermute(away, "c", SWAP).astype(wide)
    )
    normed_two = gather_tokens(
        layer_norm(residual_one, gain_two, shift_two).astype(low), yi, ci
    )
    activated, slope = weight_matmul(
        normed_two,
        up_parts,
        row_offsets,
        (model, ff_here),
        False,
        store_gelu,
        (bias_up,),
        (shape(length, ff_here), shape(length, ff_here, wide)),
        256,
        512,
    )
    (down_partial,) = weight_matmul(
        activated,
        down_parts,
        ff_offsets,
        (ff_here, model),
        False,
        store_low,
        (),
        (shape(length, model),),
        256,
        512,
    )
    block_output = residual_one + scatter_tokens(down_partial, yi, ci) + bias_down
    output_shard = block_output.astype(low).reshape(1, tok_count, model)

    cot_flat = cotangent.reshape(tok_count, model)
    cot_wide = cot_flat.astype(wide)
    cot_all = gather_tokens(cot_flat, yi, ci)
    down_bias_part = jnp.sum(cot_wide, axis=0)
    down_grads = weight_grad(activated, cot_all, owners, ff_part)
    down_shard = reduce_pieces(down_grads, z_count)
    hidden_grad, up_bias_part = weight_matmul(
        cot_all,
        down_parts,
        ff_offsets,
        (ff_here, model),
        True,
        store_hidden_grad,
        (slope,),
        (shape(length, ff_here), shape(1, ff_here, wide)),
        256,
        512,
    )
    (norm_two_partial,) = weight_matmul(
        hidden_grad,
        up_parts,
        row_offsets,
        (model, ff_here),
        True,
        store_low,
        (),
        (shape(length, model),),
        256,
        512,
    )
    up_grads = weight_grad(normed_two, hidden_grad, owners, piece_d)
    up_shard = reduce_pieces(up_grads, z_count)
    norm_two_grad = scatter_tokens(norm_two_partial, yi, ci)
    resid_part, gain_two_grad, shift_two_grad = norm_back(residual_one, gain_two, norm_two_grad)
    residual_grad = cot_wide + resid_part
    branch_grad = residual_grad.astype(low)
    branch_pair = jnp.concatenate(
        by_bit(ci, branch_grad, lax.ppermute(branch_grad, "c", SWAP)), axis=0
    )
    (mixed_grad_pair,) = weight_matmul(
        branch_pair,
        out_parts,
        out_offsets,
        (model // 2, model),
        True,
        store_low,
        (),
        (shape(2 * tok_count, model // 2),),
        256,
        512,
    )
    halves = mixed_grad_pair.reshape(2 * tok_count, 2, heads * HD)
    away = lax.dynamic_index_in_dim(halves, 1 - yi, 1, keepdims=False)
    home = lax.dynamic_index_in_dim(halves, yi, 1, keepdims=False)
    mixed_grad = jnp.concatenate(by_bit(yi, home, lax.ppermute(away, "y", SWAP)), axis=0)
    out_grad = contract_rows(mixed, branch_pair).astype(low)
    out_grad = out_grad.reshape(shard_count, piece_d // 2, 2, model // 2)
    away = lax.dynamic_index_in_dim(out_grad, 1 - yi, 2, keepdims=False)
    home = lax.dynamic_index_in_dim(out_grad, yi, 2, keepdims=False)
    out_grad = (home.astype(wide) + lax.ppermute(away, "y", SWAP).astype(wide)).astype(low)
    out_grads = [
        lax.dynamic_index_in_dim(out_grad, owners[k], 0, keepdims=False)
        for k in range(shard_count)
    ]
    out_shard = reduce_pieces(out_grads, z_count)
    proj_grad = attention_back(
        projected, mixed_grad, log_total, query_item, key_item, heads, 256
    )
    qkv_grads = weight_grad(normed_one, proj_grad, owners, piece_d)
    qkv_shard = reduce_pieces(qkv_grads, z_count)
    (norm_one_partial,) = weight_matmul(
        proj_grad,
        qkv_parts,
        row_offsets,
        (model, 3 * heads * HD),
        True,
        store_low,
        (),
        (shape(length, model),),
        256,
        512,
    )
    norm_one_grad = scatter_tokens(norm_one_partial, yi, ci)
    input_part, gain_one_grad, shift_one_grad = norm_back(inputs, gain_one, norm_one_grad)
    input_grad = (residual_grad + input_part).reshape(1, tok_count, model)

    up_bias_grad = jnp.where(
        (jnp.arange(4, dtype=jnp.int32) == si)[None, :, None],
        up_bias_part.reshape(shard_count, 1, ff_part),
        0.0,
    ).reshape(shard_count, ff_piece)
    vector_grad = jnp.concatenate(
        [
            part.reshape(shard_count, -1)
            for part in (
                gain_one_grad,
                shift_one_grad,
                gain_two_grad,
                shift_two_grad,
                down_bias_part,
                up_bias_grad,
            )
        ],
        axis=1,
    )
    vector_total = lax.dynamic_index_in_dim(
        lax.psum(vector_grad, ("z", "x", "y", "c")), 2 * zi + xi, 0, keepdims=False
    )
    down_total = widen_rows(seq_pieces(down_shard), places)
    up_total = widen_columns(seq_pieces(up_shard), places, shard_count)
    out_total = widen_quarters(seq_pieces(out_shard), places)
    qkv_total = widen_heads(seq_pieces(qkv_shard), places)
    vectors = [vector_total[slot * piece_d : (slot + 1) * piece_d] for slot in range(5)]
    return (
        output_shard,
        input_grad,
        vectors[0],
        vectors[1],
        qkv_total,
        out_total,
        vectors[2],
        vectors[3],
        up_total,
        vector_total[5 * piece_d :],
        down_total,
        vectors[4],
    )


def solution(mesh):
    shard_count, seq_count = mesh.shape["fsdp"], mesh.shape["seq"]

    def step(*args):
        model, hidden = args[0].shape[2], args[12].shape[0]
        rows_each = args[0].shape[0] // shard_count
        if (
            rows_each == 1
            and seq_count == 4
            and model // shard_count == 2 * HD
            and hidden // (4 * shard_count) % 256 == 0
        ):
            fsdp, seq = ("z", "x"), ("y", "c")
            devices = mesh.devices.reshape(shard_count // 2, 2, 2, 2)
            inner, body = Mesh(devices, fsdp + seq), split_shards
        else:
            fsdp, seq = "fsdp", "seq"
            inner, body = mesh, plain_shards
        rows, tokens = P(fsdp, None), P(fsdp, seq, None)
        vector = P(fsdp)
        placed = (tokens, tokens, rows, rows, rows, vector, vector, rows, rows)
        placed += (vector, vector, rows, vector, rows, vector)
        given = (tokens, tokens, vector, vector, rows, rows, vector, vector)
        given += (rows, vector, rows, vector)
        return jax.shard_map(
            body, mesh=inner, in_specs=placed, out_specs=given, check_vma=False
        )(*args)

    return step
```

```python
import functools

import jax
import jax.numpy as jnp
import numpy as np
from jax import lax
from jax.experimental import pallas as pl
from jax.experimental.pallas import tpu as pltpu
from jax.sharding import Mesh
from jax.sharding import PartitionSpec as P

H = 16
HD = 128


EPSILON = 1e-05
MASKED = -1e30
SWAP = ((0, 1), (1, 0))
VMEM_LIMIT = 56 << 20
GELU_A = float(np.sqrt(2.0 / np.pi))
GELU_B = 0.044715


def layer_norm(values, gain_vec, shift_vec):
    center = values - jnp.mean(values, axis=-1, keepdims=True)
    spread = jnp.mean(center * center, axis=-1, keepdims=True)
    return center * lax.rsqrt(spread + EPSILON) * gain_vec + shift_vec


def contract_rows(left, right):
    return lax.dot_general(
        left, right, (((0,), (0,)), ((), ())), preferred_element_type=jnp.float32
    )


def times_transpose(left, right):
    return lax.dot_general(
        left, right, (((1,), (1,)), ((), ())), preferred_element_type=jnp.float32
    )


def item_numbers(starts, lengths, positions):
    inside = (positions[None, :] >= starts[:, None]) & (
        positions[None, :] < (starts + lengths)[:, None]
    )
    labels = jnp.arange(1, starts.shape[0] + 1, dtype=jnp.int32)
    return jnp.sum(jnp.where(inside, labels[:, None], 0), axis=0) - 1


def visible_mask(query_pos, key_pos, query_item, key_item, key_pad):
    same_item = (query_item[:, None] == key_item[None, :]) & (query_item[:, None] >= 0)
    before = key_pos[None, :] < query_pos[:, None]
    return same_item & before & (key_pad[None, :] == 1) | (key_pos[None, :] == query_pos[:, None])


def masked_scores(query_rows, key_rows, visible, score_scale):
    scores = (
        jnp.einsum("qhd,khd->hqk", query_rows, key_rows, preferred_element_type=jnp.float32)
        * score_scale
    )
    return jnp.where(visible[None], scores, MASKED)


def attend_rows(query_rows, key_rows, value_rows, visible, score_scale):
    scores = masked_scores(query_rows, key_rows, visible, score_scale)
    row_peak = jnp.max(scores, axis=-1, keepdims=True)
    exp_scores = jnp.exp(scores - row_peak)
    row_total = jnp.sum(exp_scores, axis=-1, keepdims=True)
    attn_probs = exp_scores / row_total
    mixed_rows = jnp.einsum(
        "hqk,khd->qhd",
        attn_probs.astype(jnp.bfloat16),
        value_rows,
        preferred_element_type=jnp.float32,
    )
    return (mixed_rows, row_peak + jnp.log(row_total))


def attend_back(query_rows, key_rows, value_rows, visible, log_total, mixed_grad, score_scale):
    scores = masked_scores(query_rows, key_rows, visible, score_scale)
    attn_probs = jnp.exp(scores - log_total)
    prob_grad = jnp.einsum(
        "qhd,khd->hqk", mixed_grad, value_rows, preferred_element_type=jnp.float32
    )
    value_part = jnp.einsum(
        "hqk,qhd->khd",
        attn_probs.astype(jnp.bfloat16),
        mixed_grad,
        preferred_element_type=jnp.float32,
    )
    inner_sum = jnp.sum(prob_grad * attn_probs, axis=-1, keepdims=True)
    score_grad = (attn_probs * (prob_grad - inner_sum)).astype(jnp.bfloat16)
    query_grad = (
        jnp.einsum("hqk,khd->qhd", score_grad, key_rows, preferred_element_type=jnp.float32)
        * score_scale
    )
    key_part = (
        jnp.einsum("hqk,qhd->khd", score_grad, query_rows, preferred_element_type=jnp.float32)
        * score_scale
    )
    return (query_grad.astype(jnp.bfloat16), key_part, value_part)


def plain_shards(
    block_input,
    cotangent,
    item_starts,
    item_lengths,
    pad_mask,
    ln1_gain,
    ln1_shift,
    w_qkv,
    w_out,
    ln2_gain,
    ln2_shift,
    w_up,
    up_bias,
    w_down,
    down_bias,
):
    rows_here, tok_count, model_width = block_input.shape
    seq_count = lax.axis_size("seq")
    shard_count = lax.axis_size("fsdp")
    length = tok_count * seq_count
    score_scale = HD ** (-0.5)
    piece_d = ln1_gain.shape[0]
    seq_first = lax.axis_index("seq") * tok_count
    packed = jnp.concatenate([ln1_gain, ln1_shift, ln2_gain, ln2_shift, down_bias, up_bias])
    vector_table = lax.all_gather(packed, "fsdp", axis=0, tiled=True).reshape(shard_count, -1)

    def vector_part(slot):
        return vector_table[:, slot * piece_d : (slot + 1) * piece_d].reshape(-1)

    gain_one, shift_one, gain_two, shift_two, bias_down = [vector_part(slot) for slot in range(5)]
    bias_up = vector_table[:, 5 * piece_d :].reshape(-1)
    qkv_full, out_full = (
        lax.all_gather(w_qkv, "fsdp", axis=0, tiled=True),
        lax.all_gather(w_out, "fsdp", axis=0, tiled=True),
    )
    inputs = block_input.reshape(rows_here * tok_count, model_width).astype(jnp.float32)
    normed_one = layer_norm(inputs, gain_one, shift_one).astype(jnp.bfloat16)
    projected = jnp.dot(normed_one, qkv_full, preferred_element_type=jnp.float32).astype(
        jnp.bfloat16
    )
    query_all = projected[:, :model_width].reshape(rows_here, tok_count, H, HD)
    kv_local = projected[:, model_width:].reshape(rows_here, tok_count, 2 * model_width)
    kv_whole = lax.all_gather(kv_local, "seq", axis=1, tiled=True)
    key_all = kv_whole[:, :, :model_width].reshape(rows_here, length, H, HD)
    value_all = kv_whole[:, :, model_width:].reshape(rows_here, length, H, HD)
    positions = jnp.arange(length, dtype=jnp.int32)
    query_pos = seq_first + jnp.arange(tok_count, dtype=jnp.int32)
    row_index = 0
    item_label = item_numbers(item_starts[row_index], item_lengths[row_index], positions)
    query_item = lax.dynamic_slice_in_dim(item_label, seq_first, tok_count)
    visible = visible_mask(query_pos, positions, query_item, item_label, pad_mask[row_index])
    mixed_part, log_total = attend_rows(
        query_all[row_index], key_all[row_index], value_all[row_index], visible, score_scale
    )
    visible_list = [visible]
    mixed_list = [mixed_part]
    logsum_list = [log_total]
    mixed_all = (
        jnp.stack(mixed_list).reshape(rows_here * tok_count, model_width).astype(jnp.bfloat16)
    )
    residual_one = inputs + jnp.dot(mixed_all, out_full, preferred_element_type=jnp.float32)
    up_full, down_full = (
        lax.all_gather(w_up, "fsdp", axis=0, tiled=True),
        lax.all_gather(w_down, "fsdp", axis=0, tiled=True),
    )
    normed_two = layer_norm(residual_one, gain_two, shift_two).astype(jnp.bfloat16)
    hidden_pre = jnp.dot(normed_two, up_full, preferred_element_type=jnp.float32) + bias_up
    activated = jax.nn.gelu(hidden_pre).astype(jnp.bfloat16)
    block_output = (
        residual_one + jnp.dot(activated, down_full, preferred_element_type=jnp.float32) + bias_down
    )
    output_shard = block_output.astype(jnp.bfloat16).reshape(rows_here, tok_count, model_width)
    up_full, down_full = (
        lax.all_gather(w_up, "fsdp", axis=0, tiled=True),
        lax.all_gather(w_down, "fsdp", axis=0, tiled=True),
    )
    cot_flat = cotangent.reshape(rows_here * tok_count, model_width)
    cot_wide = cot_flat.astype(jnp.float32)
    down_grad = contract_rows(activated, cot_flat)
    down_bias_part = jnp.sum(cot_wide, axis=0)
    act_grad = times_transpose(cot_flat, down_full)
    gelu_back = jax.vjp(jax.nn.gelu, hidden_pre)[1]
    hidden_grad = gelu_back(act_grad)[0].astype(jnp.bfloat16)
    up_grad = contract_rows(normed_two, hidden_grad)
    up_bias_part = jnp.sum(hidden_grad.astype(jnp.float32), axis=0)
    norm_two_grad = times_transpose(hidden_grad, up_full)
    norm_two_back = jax.vjp(layer_norm, residual_one, gain_two, shift_two)[1]
    resid_part, gain_two_grad, shift_two_grad = norm_two_back(norm_two_grad)
    residual_grad = cot_wide + resid_part
    up_sum, down_sum = (
        lax.psum_scatter(up_grad, "fsdp", scatter_dimension=0, tiled=True),
        lax.psum_scatter(down_grad, "fsdp", scatter_dimension=0, tiled=True),
    )
    qkv_full, out_full = (
        lax.all_gather(w_qkv, "fsdp", axis=0, tiled=True),
        lax.all_gather(w_out, "fsdp", axis=0, tiled=True),
    )
    branch_grad = residual_grad.astype(jnp.bfloat16)
    out_grad = contract_rows(mixed_all, branch_grad)
    mixed_grad = (
        times_transpose(branch_grad, out_full)
        .astype(jnp.bfloat16)
        .reshape(rows_here, tok_count, H, HD)
    )
    row_index = 0
    query_grad, key_part, value_part = attend_back(
        query_all[row_index],
        key_all[row_index],
        value_all[row_index],
        visible_list[row_index],
        logsum_list[row_index],
        mixed_grad[row_index],
        score_scale,
    )
    query_list = [query_grad.reshape(tok_count, model_width)]
    kv_list = [
        jnp.concatenate(
            [key_part.reshape(length, model_width), value_part.reshape(length, model_width)], axis=1
        )
    ]
    kv_terms = jnp.stack(kv_list)
    kv_grad = lax.psum_scatter(kv_terms, "seq", scatter_dimension=1, tiled=True).astype(
        jnp.bfloat16
    )
    proj_grad = jnp.concatenate(
        [
            jnp.stack(query_list).reshape(rows_here * tok_count, model_width),
            kv_grad.reshape(rows_here * tok_count, 2 * model_width),
        ],
        axis=1,
    )
    qkv_grad = contract_rows(normed_one, proj_grad)
    norm_one_grad = times_transpose(proj_grad, qkv_full)
    norm_one_back = jax.vjp(layer_norm, inputs, gain_one, shift_one)[1]
    input_part, gain_one_grad, shift_one_grad = norm_one_back(norm_one_grad)
    input_grad = (residual_grad + input_part).reshape(rows_here, tok_count, model_width)
    vector_grad = jnp.concatenate(
        [
            piece_grad.reshape(shard_count, -1)
            for piece_grad in (
                gain_one_grad,
                shift_one_grad,
                gain_two_grad,
                shift_two_grad,
                down_bias_part,
                up_bias_part,
            )
        ],
        axis=1,
    ).reshape(-1)
    qkv_sum, out_sum, vector_sum = (
        lax.psum_scatter(qkv_grad, "fsdp", scatter_dimension=0, tiled=True),
        lax.psum_scatter(out_grad, "fsdp", scatter_dimension=0, tiled=True),
        lax.psum_scatter(vector_grad, "fsdp", scatter_dimension=0, tiled=True),
    )
    up_total, down_total, qkv_total, out_total, vector_total = lax.psum(
        (up_sum, down_sum, qkv_sum, out_sum, vector_sum), "seq"
    )
    gain_one_out = vector_total[0:piece_d]
    shift_one_out = vector_total[piece_d : 2 * piece_d]
    gain_two_out = vector_total[2 * piece_d : 3 * piece_d]
    shift_two_out = vector_total[3 * piece_d : 4 * piece_d]
    down_bias_out = vector_total[4 * piece_d : 5 * piece_d]
    up_bias_out = vector_total[5 * piece_d :]
    return (
        output_shard,
        input_grad,
        gain_one_out,
        shift_one_out,
        qkv_total,
        out_total,
        gain_two_out,
        shift_two_out,
        up_total,
        up_bias_out,
        down_total,
        down_bias_out,
    )


def gather_small(vector, z_count):
    line = [vector]
    for j in range(1, z_count):
        line.append(lax.ppermute(vector, "z", [(i, (i + j) % z_count) for i in range(z_count)]))
    return line + [lax.ppermute(piece, "x", SWAP) for piece in line]


def gather_weight(shard, *others):
    near = lax.all_gather(shard, "z", axis=0, tiled=False)
    return [near, lax.ppermute(after(near, *others), "x", SWAP)]


def stage(flag, work, *args):
    shapes = jax.eval_shape(work, *args)

    def nothing(*_):
        return jax.tree.map(lambda a: jnp.zeros(a.shape, a.dtype), shapes)

    return lax.cond(flag, work, nothing, *args)


class Line:
    def __init__(self):
        self.last = ()

    def enter(self, value):
        return after(value, *self.last)

    def leave(self, *results):
        self.last = results[:1]
        return results


def after(value, *others):
    return lax.optimization_barrier((value,) + others)[0]


def seq_pieces(block, *others):
    return core_pieces(block, after(lax.ppermute(block, "y", SWAP), *others))


def core_pieces(block, other):
    return [block, lax.ppermute(block, "c", SWAP), other, lax.ppermute(other, "c", SWAP)]


def by_bit(bit, mine, theirs):
    return jnp.where(bit == 0, mine, theirs), jnp.where(bit == 0, theirs, mine)


def gather_tokens(block, yi, ci, *others):
    parts = seq_pieces(block, *others)
    near = by_bit(ci, parts[0], parts[1])
    far = by_bit(ci, parts[2], parts[3])
    rows = [jnp.where(yi == 0, n, f) for n, f in zip(near, far)]
    rows += [jnp.where(yi == 0, f, n) for n, f in zip(near, far)]
    return jnp.concatenate(rows, axis=0)


def core_sum(partial, yi, ci):
    tokens = partial.shape[0] // 4
    parts = partial.reshape(2, 2, tokens, partial.shape[1])
    away = lax.dynamic_index_in_dim(parts, 1 - ci, 1, keepdims=False)
    home = lax.dynamic_index_in_dim(parts, ci, 1, keepdims=False)
    total = home.astype(jnp.float32) + lax.ppermute(away, "c", SWAP).astype(jnp.float32)
    away = lax.dynamic_index_in_dim(total, 1 - yi, 0, keepdims=False).astype(jnp.bfloat16)
    return lax.dynamic_index_in_dim(total, yi, 0, keepdims=False), away


def home_sum(home, other):
    return home + other.astype(jnp.float32)


def scatter_tokens(partial, yi, ci, *others):
    home, away = core_sum(partial, yi, ci)
    return home_sum(home, after(lax.ppermute(away, "y", SWAP), *others))


COST_SCALE = 0.01


def cost(flops, bytes_accessed, transcendentals):
    return pl.CostEstimate(
        flops=int(flops * COST_SCALE),
        bytes_accessed=int(bytes_accessed * COST_SCALE),
        transcendentals=int(transcendentals * COST_SCALE),
    )


def params(limit=VMEM_LIMIT):
    return pltpu.CompilerParams(vmem_limit_bytes=limit)


def load_weight(offsets, pieces, held, sems):
    copies = []
    for piece in pieces:
        count, rows, cols = piece.shape
        for k in range(count):
            b = len(copies)
            row = pl.multiple_of(offsets[0, b], rows)
            col = pl.multiple_of(offsets[1, b], cols)
            copies.append(
                pltpu.make_async_copy(
                    piece.at[k], held.at[pl.ds(row, rows), pl.ds(col, cols)], sems.at[b]
                )
            )
    for copy in copies:
        copy.start()
    for copy in copies:
        copy.wait()


def weight_matmul(left, pieces, offsets, shape, back, body, extras, outs, tile, chunk):
    rows = left.shape[0]
    depth, width = shape
    out_width = depth if back else width
    n_pieces, n_extras = len(pieces), len(extras)

    def kernel(offs_ref, left_ref, *refs):
        piece_refs = refs[:n_pieces]
        extra_refs = refs[n_pieces : n_pieces + n_extras]
        out_refs = refs[n_pieces + n_extras : -2]
        held, sems = refs[-2:]

        @pl.when(pl.program_id(0) == 0)
        def _():
            load_weight(offs_ref, piece_refs, held, sems)

        for start in range(0, out_width, chunk):
            cols = pl.ds(start, chunk)
            if back:
                values = lax.dot_general(
                    left_ref[...],
                    held[cols, :],
                    (((1,), (1,)), ((), ())),
                    preferred_element_type=jnp.float32,
                )
            else:
                values = jnp.dot(
                    left_ref[...], held[:, cols], preferred_element_type=jnp.float32
                )
            body(values, cols, extra_refs, out_refs, pl.program_id(0) == 0)

    def tile_spec(array_rows, array_cols):
        if array_rows == 1:
            return pl.BlockSpec((1, array_cols), lambda i, offs: (0, 0))
        return pl.BlockSpec((tile, array_cols), lambda i, offs: (i, 0))

    flops = 2 * rows * depth * width
    moved = 2 * (left.size + depth * width) + sum(
        a.size * a.dtype.itemsize for a in list(extras) + list(outs)
    )
    return pl.pallas_call(
        kernel,
        grid_spec=pltpu.PrefetchScalarGridSpec(
            num_scalar_prefetch=1,
            grid=(rows // tile,),
            in_specs=[pl.BlockSpec((tile, left.shape[1]), lambda i, offs: (i, 0))]
            + [pl.BlockSpec(memory_space=pl.ANY)] * n_pieces
            + [tile_spec(*a.shape) for a in extras],
            out_specs=[tile_spec(*a.shape) for a in outs],
            scratch_shapes=[
                pltpu.VMEM((depth, width), jnp.bfloat16),
                pltpu.SemaphoreType.DMA((sum(p.shape[0] for p in pieces),)),
            ],
        ),
        out_shape=list(outs),
        cost_estimate=cost(flops=flops, bytes_accessed=moved, transcendentals=0),
        compiler_params=params(),
    )(offsets, left, *pieces, *extras)


def store_low(values, cols, extra_refs, out_refs, first):
    out_refs[0][:, cols] = values.astype(jnp.bfloat16)


def store_gelu(values, cols, extra_refs, out_refs, first):
    hidden = values + extra_refs[0][:, cols]
    square = hidden * hidden
    bend = jnp.tanh(GELU_A * hidden * (1.0 + GELU_B * square))
    half = 0.5 * (1.0 + bend)
    out_refs[0][:, cols] = (hidden * half).astype(jnp.bfloat16)
    slope = half + 0.5 * hidden * (1.0 - bend * bend) * (
        GELU_A * (1.0 + 3.0 * GELU_B * square)
    )
    out_refs[1][:, cols] = slope


def store_hidden_grad(values, cols, extra_refs, out_refs, first):
    low = (values * extra_refs[0][:, cols]).astype(jnp.bfloat16)
    out_refs[0][:, cols] = low
    column_sum = jnp.sum(low.astype(jnp.float32), axis=0, keepdims=True)
    sums = out_refs[1]

    @pl.when(first)
    def _():
        sums[:, cols] = column_sum

    @pl.when(jnp.logical_not(first))
    def _():
        sums[:, cols] += column_sum


def weight_grad(left, right, where, count, block, width, *addends):
    rows = left.shape[0]
    parts = max(len(addends), 1)
    part = width // parts

    def kernel(where_ref, left_ref, right_ref, *refs):
        for n in range(parts):
            cols = slice(n * part, (n + 1) * part)
            value = lax.dot_general(
                left_ref[...],
                right_ref[:, cols],
                (((0,), (0,)), ((), ())),
                preferred_element_type=jnp.float32,
            )
            if addends:
                value = value + refs[n][0].astype(jnp.float32)
            refs[-1][0, :, cols] = value.astype(jnp.bfloat16)

    piece = pl.BlockSpec((1, block, width), lambda k, at: (k, 0, 0))
    return pl.pallas_call(
        kernel,
        grid_spec=pltpu.PrefetchScalarGridSpec(
            num_scalar_prefetch=1,
            grid=(count,),
            in_specs=[
                pl.BlockSpec((rows, block), lambda k, at: (0, at[k])),
                pl.BlockSpec((rows, width), lambda k, at: (0, at[count])),
            ]
            + [pl.BlockSpec((1, block, part), lambda k, at: (k, 0, 0))] * len(addends),
            out_specs=piece,
        ),
        out_shape=jax.ShapeDtypeStruct((count, block, width), jnp.bfloat16),
        cost_estimate=cost(
            flops=2 * rows * count * block * width,
            bytes_accessed=2 * rows * (count * block + width)
            + 4 * count * block * width,
            transcendentals=0,
        ),
        compiler_params=params(),
    )(where, left, right, *addends)


def slice_weights(w_qkv, w_out, w_up, w_down, yi, ci, shard_count):
    rows, model = w_out.shape
    heads = H // 4
    ff_part = w_down.shape[0] // 4
    half = 3 * heads * HD // 2
    steps = shard_count
    part = ff_part // steps

    def kernel(at_ref, qkv_ref, out_ref, up_ref, down_ref, *to):
        y, c = at_ref[0], at_ref[1]
        step = pl.program_id(0)
        for n in range(2):
            qkv_to, up_to = to[n], to[3 + n]

            @pl.when(step == n)
            def _():
                for i in range(half // HD):
                    head = n * (half // HD) + i
                    col = (head // heads) * H + 2 * (head % heads) + c + 2 * heads * y
                    col = pl.ds(pl.multiple_of(col * HD, HD), HD)
                    qkv_to[:, i * HD : (i + 1) * HD] = qkv_ref[:, col]

            @pl.when(step // (steps // 2) == n)
            def _():
                up_to[...] = up_ref[...]

        @pl.when(step == 0)
        def _():
            to[2][...] = out_ref[...]

        to[5][...] = down_ref[...]

    def pair(block, index):
        return [pl.BlockSpec(block, functools.partial(index, n)) for n in range(2)]

    up_half = steps // 2
    return pl.pallas_call(
        kernel,
        grid_spec=pltpu.PrefetchScalarGridSpec(
            num_scalar_prefetch=1,
            grid=(steps,),
            in_specs=[
                pl.BlockSpec((rows, 3 * model), lambda i, at: (0, 0)),
                pl.BlockSpec((rows // 2, model // 2), lambda i, at: (at[1], at[0])),
                pl.BlockSpec((rows, ff_part), lambda i, at: (0, 4 * i + 2 * at[0] + at[1])),
                pl.BlockSpec(
                    (part, model), lambda i, at: ((2 * at[0] + at[1]) * steps + i, 0)
                ),
            ],
            out_specs=pair((rows, half), lambda n, i, at: (0, 0))
            + [pl.BlockSpec((rows // 2, model // 2), lambda i, at: (0, 0))]
            + pair(
                (rows, ff_part),
                lambda n, i, at: (0, jnp.clip(i - n * up_half, 0, up_half - 1)),
            )
            + [pl.BlockSpec((part, model), lambda i, at: (i, 0))],
        ),
        out_shape=[
            jax.ShapeDtypeStruct(shape, jnp.bfloat16)
            for shape in [(rows, half)] * 2
            + [(rows // 2, model // 2)]
            + [(rows, ff_part * up_half)] * 2
            + [(ff_part, model)]
        ],
        cost_estimate=cost(flops=0, bytes_accessed=12 << 20, transcendentals=0),
        compiler_params=params(),
    )(jnp.stack([yi, ci]).astype(jnp.int32), w_qkv, w_out, w_up, w_down)


def visible_tile(query_item, key_item, first_query, n_query, n_key):
    query_pos = first_query + lax.broadcasted_iota(jnp.int32, (n_query, n_key), 0)
    key_pos = lax.broadcasted_iota(jnp.int32, (n_query, n_key), 1)
    return ((query_item == key_item) & (key_pos < query_pos)) | (key_pos == query_pos)


def head_spec(length, first):
    return pl.BlockSpec((length, HD), lambda h: (0, first + h))


def attention(projected, query_item, key_item, heads, tile):
    length = projected.shape[0]
    scale = HD ** (-0.5)

    def kernel(q_ref, k_ref, v_ref, qi_ref, ki_ref, mixed_ref, log_ref):
        for start in range(0, length, tile):
            stop = start + tile
            rows = slice(start, stop)
            scores = (
                lax.dot_general(
                    q_ref[rows, :],
                    k_ref[:stop, :],
                    (((1,), (1,)), ((), ())),
                    preferred_element_type=jnp.float32,
                )
                * scale
            )
            seen = visible_tile(qi_ref[rows, :], ki_ref[:, :stop], start, tile, stop)
            scores = jnp.where(seen, scores, MASKED)
            peak = jnp.max(scores, axis=-1, keepdims=True)
            weights = jnp.exp(scores - peak)
            total = jnp.sum(weights, axis=-1, keepdims=True)
            probs = (weights * (1.0 / total)).astype(jnp.bfloat16)
            mixed_ref[rows, :] = jnp.dot(
                probs, v_ref[:stop, :], preferred_element_type=jnp.float32
            ).astype(jnp.bfloat16)
            log_ref[0, rows, :] = peak + jnp.log(total)

    whole = lambda rows, cols: pl.BlockSpec((rows, cols), lambda h: (0, 0))
    return pl.pallas_call(
        kernel,
        grid=(heads,),
        in_specs=[head_spec(length, g * heads) for g in range(3)]
        + [whole(length, 1), whole(1, length)],
        out_specs=[head_spec(length, 0), pl.BlockSpec((1, length, 1), lambda h: (h, 0, 0))],
        out_shape=[
            jax.ShapeDtypeStruct((length, heads * HD), jnp.bfloat16),
            jax.ShapeDtypeStruct((heads, length, 1), jnp.float32),
        ],
        cost_estimate=cost(
            flops=4 * heads * length * length * HD,
            bytes_accessed=8 * length * heads * HD,
            transcendentals=heads * length * length,
        ),
        compiler_params=params(),
    )(projected, projected, projected, query_item, key_item)


def attention_back(projected, mixed_grad, log_total, query_item, key_item, heads, tile):
    length = projected.shape[0]
    scale = HD ** (-0.5)

    def kernel(q_ref, k_ref, v_ref, g_ref, log_ref, qi_ref, ki_ref, grad_ref, dk_ref, dv_ref):
        head = pl.program_id(0)

        def place(group):
            return pl.ds(pl.multiple_of((group * heads + head) * HD, HD), HD)

        for start in reversed(range(0, length, tile)):
            stop = start + tile
            rows = slice(start, stop)
            query, grad = q_ref[rows, :], g_ref[rows, :]
            key, value = k_ref[:stop, :], v_ref[:stop, :]
            scores = (
                lax.dot_general(
                    query, key, (((1,), (1,)), ((), ())), preferred_element_type=jnp.float32
                )
                * scale
            )
            seen = visible_tile(qi_ref[rows, :], ki_ref[:, :stop], start, tile, stop)
            probs = jnp.exp(jnp.where(seen, scores, MASKED) - log_ref[0, rows, :])
            prob_grad = lax.dot_general(
                grad, value, (((1,), (1,)), ((), ())), preferred_element_type=jnp.float32
            )
            inner = jnp.sum(prob_grad * probs, axis=-1, keepdims=True)
            score_grad = (probs * (prob_grad - inner)).astype(jnp.bfloat16)
            grad_ref[rows, place(0)] = (
                jnp.dot(score_grad, key, preferred_element_type=jnp.float32) * scale
            ).astype(jnp.bfloat16)
            key_part = lax.dot_general(
                score_grad, query, (((0,), (0,)), ((), ())), preferred_element_type=jnp.float32
            )
            value_part = lax.dot_general(
                probs.astype(jnp.bfloat16),
                grad,
                (((0,), (0,)), ((), ())),
                preferred_element_type=jnp.float32,
            )
            if stop == length:
                dk_ref[...] = key_part
                dv_ref[...] = value_part
            else:
                dk_ref[:stop, :] += key_part
                dv_ref[:stop, :] += value_part
        grad_ref[:, place(1)] = (dk_ref[...] * scale).astype(jnp.bfloat16)
        grad_ref[:, place(2)] = dv_ref[...].astype(jnp.bfloat16)

    whole = lambda rows, cols: pl.BlockSpec((rows, cols), lambda h: (0, 0))
    return pl.pallas_call(
        kernel,
        grid=(heads,),
        in_specs=[head_spec(length, g * heads) for g in range(3)]
        + [
            head_spec(length, 0),
            pl.BlockSpec((1, length, 1), lambda h: (h, 0, 0)),
            whole(length, 1),
            whole(1, length),
        ],
        out_specs=whole(length, 3 * heads * HD),
        out_shape=jax.ShapeDtypeStruct((length, 3 * heads * HD), jnp.bfloat16),
        scratch_shapes=[pltpu.VMEM((length, HD), jnp.float32)] * 2,
        cost_estimate=cost(
            flops=10 * heads * length * length * HD,
            bytes_accessed=16 * length * heads * HD,
            transcendentals=heads * length * length,
        ),
        compiler_params=params(),
    )(projected, projected, projected, mixed_grad, log_total, query_item, key_item)


def widen(chunks, places, grid, piece_specs, out_block, out_index, out_shape, write):
    def kernel(place_ref, *refs):
        for n in range(len(chunks)):
            for r in range(4):
                write(n, place_ref[r], refs[4 * n + r], refs[-1])

    return pl.pallas_call(
        kernel,
        grid_spec=pltpu.PrefetchScalarGridSpec(
            num_scalar_prefetch=1,
            grid=(grid,),
            in_specs=[
                pl.BlockSpec(block, functools.partial(lambda at, i, pos: at(i), at))
                for block, at in piece_specs
                for _ in range(4)
            ],
            out_specs=pl.BlockSpec(out_block, lambda i, pos: out_index(i)),
        ),
        out_shape=jax.ShapeDtypeStruct(out_shape, jnp.float32),
        cost_estimate=cost(
            flops=0, bytes_accessed=6 * int(np.prod(out_shape)), transcendentals=0
        ),
        compiler_params=params(),
    )(places, *[piece for pieces in chunks for piece in pieces])


def widen_columns(pieces, places, blocks):
    rows, width = pieces[0].shape
    part = width // blocks

    def write(n, pos, piece, out):
        out[:, pl.ds(pl.multiple_of(pos * part, part), part)] = piece[...].astype(jnp.float32)

    return widen(
        [pieces],
        places,
        blocks,
        [((rows, part), lambda i: (0, i))],
        (rows, 4 * part),
        lambda i: (0, i),
        (rows, 4 * width),
        write,
    )


def widen_rows(pieces, places):
    rows, width = pieces[0].shape

    def write(n, pos, piece, out):
        @pl.when(pos == pl.program_id(0))
        def _():
            out[...] = piece[...].astype(jnp.float32)

    return widen(
        [pieces],
        places,
        4,
        [((rows, width), lambda i: (0, 0))],
        (rows, width),
        lambda i: (i, 0),
        (4 * rows, width),
        write,
    )


def widen_heads(pieces, places):
    rows, width = pieces[0].shape
    part = width // 3

    def write(n, pos, piece, out):
        first = lax.div(pos, 2) * part * 2 + lax.rem(pos, 2) * HD
        for i in range(part // HD):
            cols = pl.ds(pl.multiple_of(first + 2 * i * HD, HD), HD)
            out[:, cols] = piece[:, i * HD : (i + 1) * HD].astype(jnp.float32)

    return widen(
        [pieces],
        places,
        3,
        [((rows, part), lambda i: (0, i))],
        (rows, 4 * part),
        lambda i: (0, i),
        (rows, 4 * width),
        write,
    )


def widen_quarters(pieces, places):
    rows, width = pieces[0].shape

    def write(n, pos, piece, out):
        row = pl.multiple_of(lax.rem(pos, 2) * rows, rows)
        col = pl.multiple_of(lax.div(pos, 2) * width, width)
        out[pl.ds(row, rows), pl.ds(col, width)] = piece[...].astype(jnp.float32)

    return widen(
        [pieces],
        places,
        1,
        [((rows, width), lambda i: (0, 0))],
        (2 * rows, 2 * width),
        lambda i: (0, 0),
        (2 * rows, 2 * width),
        write,
    )


def norm_back(values, gain_vec, incoming):
    center = values - jnp.mean(values, axis=-1, keepdims=True)
    spread = jnp.mean(center * center, axis=-1, keepdims=True)
    inverse = lax.rsqrt(spread + EPSILON)
    unit = center * inverse
    scaled = incoming * gain_vec
    inner = jnp.mean(scaled * unit, axis=-1, keepdims=True)
    grad = (scaled - jnp.mean(scaled, axis=-1, keepdims=True) - unit * inner) * inverse
    return grad, jnp.sum(incoming * unit, axis=0), jnp.sum(incoming, axis=0)


def split_shards(
    block_input,
    cotangent,
    item_starts,
    item_lengths,
    pad_mask,
    ln1_gain,
    ln1_shift,
    w_qkv,
    w_out,
    ln2_gain,
    ln2_shift,
    w_up,
    up_bias,
    w_down,
    down_bias,
):
    low, wide = jnp.bfloat16, jnp.float32
    z_count = lax.axis_size("z")
    shard_count = 2 * z_count
    zi, xi, yi, ci = [lax.axis_index(name) for name in ("z", "x", "y", "c")]
    si = 2 * yi + ci
    tok_count, model = block_input.shape[1:]
    length = 4 * tok_count
    piece_d, ff_piece = ln1_gain.shape[0], up_bias.shape[0]
    ff_part = ff_piece // 4
    ff_here = ff_part * shard_count
    heads = H // 4
    places = jnp.stack([jnp.bitwise_xor(si, r) for r in range(4)]).astype(jnp.int32)

    packed = jnp.concatenate([ln1_gain, ln1_shift, ln2_gain, ln2_shift, down_bias, up_bias])
    vector_stack = jnp.stack(gather_small(packed, z_count))
    owners = jnp.stack(
        [
            lax.rem(zi - j + z_count, z_count) * 2 + jnp.bitwise_xor(xi, dx)
            for dx in range(2)
            for j in range(z_count)
        ]
    )
    hit = owners[None, :] == jnp.arange(shard_count, dtype=jnp.int32)[:, None]
    vector_table = jnp.sum(jnp.where(hit[:, :, None], vector_stack[None], 0.0), axis=1)

    def vector_part(slot):
        return vector_table[:, slot * piece_d : (slot + 1) * piece_d].reshape(-1)

    gain_one, shift_one, gain_two, shift_two, bias_down = [vector_part(slot) for slot in range(5)]
    bias_up = lax.dynamic_index_in_dim(
        vector_table[:, 5 * piece_d :].reshape(shard_count, 4, ff_part), si, 1, keepdims=False
    ).reshape(1, ff_here)

    line = Line()
    flag = item_lengths[0, 0] > 0
    slices = slice_weights(w_qkv, w_out, w_up, w_down, yi, ci, shard_count)
    half = model // 2
    qkv_width = 3 * heads * HD
    qkv_parts = gather_weight(slices[0]) + gather_weight(slices[1])
    down_pair = jnp.stack([slices[5], lax.ppermute(slices[5], "x", SWAP)])
    inputs = after(block_input, down_pair).reshape(tok_count, model).astype(wide)
    normed_one = layer_norm(inputs, gain_one, shift_one).astype(low)
    out_parts = gather_weight(after(slices[2], normed_one), qkv_parts[1])
    out_parts = out_parts + [lax.ppermute(piece, "y", SWAP) for piece in out_parts]

    near_blocks = [2 * z + xi for z in range(z_count)]
    far_blocks = [2 * z + 1 - xi for z in range(z_count)]
    split = near_blocks + far_blocks
    paired = [b for pair in zip(near_blocks, far_blocks) for b in pair]
    zero = jnp.zeros_like(xi)

    def table(*rows):
        return jnp.stack([jnp.stack(row) for row in rows]).astype(jnp.int32)

    def halves_at(first, second, rows, width):
        return table(
            [b * rows for b in first + second],
            [zero] * shard_count + [zero + width] * shard_count,
        )

    qkv_offsets = halves_at(split, split, piece_d, qkv_width // 2)
    up_offsets = halves_at(split, split, piece_d, ff_here // 2)
    down_offsets = table([b * ff_part for b in paired], [zero] * shard_count)
    out_offsets = table(
        [b * (piece_d // 2) for b in split] * 2,
        [yi * half] * shard_count + [(1 - yi) * half] * shard_count,
    )

    def blocks_at(blocks, n):
        return table(blocks + [zero + n])[0]

    def sum_small(terms):
        def term(j):
            return lax.dynamic_index_in_dim(
                terms, lax.rem(zi - j + z_count, z_count), 0, keepdims=False
            )

        total = term(0).astype(wide)
        for j in range(1, z_count):
            total = total + lax.ppermute(
                term(j), "z", [(i, (i - j) % z_count) for i in range(z_count)]
            ).astype(wide)
        return total

    def plain_matmul(left, pieces, offsets, shape, back, body, extras, outs):
        return weight_matmul(left, pieces, offsets, shape, back, body, extras, outs, 256, 512)

    def matmul(left, *others):
        return line.leave(*plain_matmul(line.enter(left), *others))

    def grad_chunk(left, right, blocks, n, block, width, *addends):
        return line.leave(
            weight_grad(
                line.enter(left), right, blocks_at(blocks, n), len(blocks), block, width, *addends
            )
        )[0]

    def far_terms(left, right, block):
        terms = grad_chunk(left, right, far_blocks, 0, block, right.shape[1])
        return lax.ppermute(terms, "x", SWAP)

    def near_terms(left, right, block, addend):
        width = right.shape[1]
        return weight_grad(
            left, right, blocks_at(near_blocks, 0), z_count, block, width, addend
        )

    def sum_over_z(total):
        return lax.psum_scatter(total, "z", scatter_dimension=0, tiled=False)

    def shape(rows, cols, kind=low):
        return jax.ShapeDtypeStruct((rows, cols), kind)

    normed_one = gather_tokens(normed_one, yi, ci, qkv_parts[0])
    cot_flat = after(cotangent.reshape(tok_count, model), normed_one)
    cot_wide = cot_flat.astype(wide)
    cot_all = gather_tokens(cot_flat, yi, ci, qkv_parts[2])
    (projected,) = matmul(
        after(normed_one, cot_all),
        qkv_parts,
        qkv_offsets,
        (model, qkv_width),
        False,
        store_low,
        (),
        (shape(length, qkv_width),),
    )
    up_parts = gather_weight(slices[3], projected)
    up_high = lax.all_gather(slices[4], "z", axis=0, tiled=False)
    down_parts = [lax.all_gather(down_pair, "z", axis=0, tiled=True)]
    positions = jnp.arange(length, dtype=jnp.int32)
    item_label = item_numbers(item_starts[0], item_lengths[0], positions)
    query_item = item_label[:, None]
    key_item = jnp.where((item_label >= 0) & (pad_mask[0] == 1), item_label, -2)[None, :]
    mixed_heads, log_total = line.leave(
        *attention(line.enter(projected), query_item, key_item, heads, 256)
    )

    def attend_out(mixed_heads):
        halves = mixed_heads.reshape(2, 2 * tok_count, heads * HD)
        away = lax.dynamic_index_in_dim(halves, 1 - yi, 0, keepdims=False)
        mine = lax.dynamic_index_in_dim(halves, yi, 0, keepdims=False)
        other = lax.ppermute(away, "y", SWAP)
        mixed = jnp.concatenate(by_bit(yi, mine, other), axis=1)
        (out_partial,) = plain_matmul(
            mixed,
            out_parts,
            out_offsets,
            (half, model),
            False,
            store_low,
            (),
            (shape(2 * tok_count, model),),
        )
        halves = out_partial.reshape(2, tok_count, model)
        away = lax.dynamic_index_in_dim(halves, 1 - ci, 0, keepdims=False)
        home = lax.dynamic_index_in_dim(halves, ci, 0, keepdims=False)
        residual_one = (
            inputs + home.astype(wide) + lax.ppermute(away, "c", SWAP).astype(wide)
        )
        normed_two = layer_norm(residual_one, gain_two, shift_two).astype(low)
        return normed_two, residual_one, mine, other

    normed_two, residual_one, mixed_home, mixed_other = line.leave(
        *stage(flag, attend_out, after(line.enter(mixed_heads), up_parts[0]))
    )
    normed_two = after(normed_two, up_high)
    up_parts += [up_high, lax.ppermute(after(up_high, normed_two), "x", SWAP)]
    normed_two = gather_tokens(normed_two, yi, ci, up_parts[1])
    mixed_last = lax.ppermute(after(mixed_home, normed_two), "y", SWAP)
    others_heads = jnp.concatenate(by_bit(yi, mixed_other, mixed_last), axis=0)
    mixed = jnp.concatenate(by_bit(yi, mixed_heads, others_heads), axis=1)
    activated, slope = matmul(
        normed_two,
        up_parts,
        up_offsets,
        (model, ff_here),
        False,
        store_gelu,
        (bias_up,),
        (shape(length, ff_here), shape(length, ff_here, wide)),
    )

    down_bias_part = jnp.sum(cot_wide, axis=0)
    down_far = far_terms(after(activated, mixed), cot_all, ff_part)
    hidden_grad, up_bias_part = matmul(
        cot_all,
        down_parts,
        down_offsets,
        (ff_here, model),
        True,
        store_hidden_grad,
        (slope,),
        (shape(length, ff_here), shape(1, ff_here, wide)),
    )
    up_far = far_terms(normed_two, hidden_grad, piece_d)
    (norm_two_partial,) = matmul(
        hidden_grad,
        up_parts,
        up_offsets,
        (model, ff_here),
        True,
        store_low,
        (),
        (shape(length, model),),
    )
    (down_sum,) = line.leave(
        near_terms(line.enter(activated), cot_all, ff_part, down_far)
    )
    down_shard = sum_over_z(down_sum)

    def norm_two_back(norm_two_partial):
        norm_two_grad = scatter_tokens(norm_two_partial, yi, ci)
        resid_part, gain_two_grad, shift_two_grad = norm_back(
            residual_one, gain_two, norm_two_grad
        )
        residual_grad = cot_wide + resid_part
        branch_grad = residual_grad.astype(low)
        branch_pair = jnp.concatenate(
            by_bit(ci, branch_grad, lax.ppermute(branch_grad, "c", SWAP)), axis=0
        )
        return branch_pair, residual_grad, gain_two_grad, shift_two_grad

    branch_pair, residual_grad, gain_two_grad, shift_two_grad = line.leave(
        *stage(flag, norm_two_back, line.enter(norm_two_partial))
    )

    out_blocks = far_blocks + near_blocks

    def out_back(branch_pair):
        (mixed_grad_pair,) = plain_matmul(
            branch_pair,
            out_parts,
            out_offsets,
            (half, model),
            True,
            store_low,
            (),
            (shape(2 * tok_count, half),),
        )
        part = heads * HD
        away = lax.dynamic_slice_in_dim(mixed_grad_pair, (1 - yi) * part, part, 1)
        home = lax.dynamic_slice_in_dim(mixed_grad_pair, yi * part, part, 1)
        theirs = lax.ppermute(away, "y", SWAP)
        return jnp.concatenate(by_bit(yi, home, theirs), axis=0)

    (mixed_grad,) = line.leave(stage(flag, out_back, line.enter(branch_pair)))
    away = lax.dynamic_slice_in_dim(branch_pair, (1 - yi) * half, half, 1)
    home = lax.dynamic_slice_in_dim(branch_pair, yi * half, half, 1)
    branch_other = lax.ppermute(after(away, mixed_grad), "y", SWAP)
    branch_all = jnp.concatenate(by_bit(yi, home, branch_other), axis=0)
    (proj_grad,) = line.leave(
        attention_back(
            projected,
            line.enter(mixed_grad),
            log_total,
            query_item,
            key_item,
            heads,
            256,
        )
    )
    qkv_far = far_terms(normed_one, proj_grad, piece_d)
    (up_sum,) = line.leave(
        near_terms(line.enter(after(normed_two, branch_other)), hidden_grad, piece_d, up_far)
    )
    up_shard = sum_over_z(up_sum)
    (norm_one_partial,) = matmul(
        proj_grad,
        qkv_parts,
        qkv_offsets,
        (model, qkv_width),
        True,
        store_low,
        (),
        (shape(length, model),),
    )

    out_sum = line.leave(
        weight_grad(
            line.enter(mixed),
            branch_all,
            blocks_at(out_blocks, 0),
            shard_count,
            piece_d // 2,
            half,
        )
    )[0]
    down_other = lax.ppermute(after(down_shard, mixed_grad), "y", SWAP)

    def norm_one_back(norm_one_partial):
        home, away = core_sum(norm_one_partial, yi, ci)
        (down_partial,) = plain_matmul(
            after(activated, away),
            down_parts,
            down_offsets,
            (ff_here, model),
            False,
            store_low,
            (),
            (shape(length, model),),
        )
        away = lax.ppermute(away, "y", SWAP)
        norm_one_grad = home_sum(home, after(away, down_partial))
        input_part, gain_one_grad, shift_one_grad = norm_back(inputs, gain_one, norm_one_grad)
        input_grad = (residual_grad + input_part).reshape(1, tok_count, model)
        feed_home, feed_away = core_sum(down_partial, yi, ci)
        return (
            input_grad,
            gain_one_grad,
            shift_one_grad,
            feed_home,
            feed_away,
        )

    (
        input_grad,
        gain_one_grad,
        shift_one_grad,
        feed_home,
        feed_away,
    ) = line.leave(
        *stage(flag, norm_one_back, after(line.enter(norm_one_partial), down_other))
    )
    (qkv_sum,) = line.leave(
        near_terms(
            after(line.enter(normed_one), up_shard), proj_grad, piece_d, qkv_far
        )
    )
    qkv_shard = sum_over_z(qkv_sum)

    def ends(up_shard):
        feed_other = lax.ppermute(feed_away, "y", SWAP)
        up_other = lax.ppermute(up_shard, "y", SWAP)
        feed_out = home_sum(feed_home, feed_other)
        output_shard = (residual_one + feed_out + bias_down).astype(low)
        output_shard = output_shard.reshape(1, tok_count, model)
        out_away = lax.ppermute(out_sum[:z_count], "x", SWAP)
        out_shard = sum_small(
            (out_sum[z_count:].astype(wide) + out_away.astype(wide)).astype(low)
        ).astype(low)
        up_bias_grad = jnp.where(
            (jnp.arange(4, dtype=jnp.int32) == si)[None, :, None],
            up_bias_part.reshape(shard_count, 1, ff_part),
            0.0,
        ).reshape(shard_count, ff_piece)
        vector_grad = jnp.concatenate(
            [
                part.reshape(shard_count, -1)
                for part in (
                    gain_one_grad,
                    shift_one_grad,
                    gain_two_grad,
                    shift_two_grad,
                    down_bias_part,
                    up_bias_grad,
                )
            ],
            axis=1,
        )
        for name in ("c", "y"):
            vector_grad = vector_grad + lax.ppermute(vector_grad, name, SWAP)
        vector_grad = vector_grad.reshape(z_count, 2, -1)
        away = lax.dynamic_index_in_dim(vector_grad, 1 - xi, 1, keepdims=False)
        home = lax.dynamic_index_in_dim(vector_grad, xi, 1, keepdims=False)
        vector_grad = home + lax.ppermute(away, "x", SWAP)
        vector_total = sum_small(vector_grad)
        up_pieces = core_pieces(up_shard, up_other)
        return (
            output_shard,
            vector_total,
            out_shard,
            widen_columns(up_pieces, places, shard_count),
        )

    output_shard, vector_total, out_shard, up_total = line.leave(
        *stage(flag, ends, line.enter(up_shard))
    )

    def last(qkv_shard):
        return (
            widen_heads(seq_pieces(qkv_shard), places),
            widen_quarters(seq_pieces(out_shard), places),
            widen_rows(core_pieces(down_shard, down_other), places),
        )

    qkv_total, out_total, down_total = stage(flag, last, after(qkv_shard, up_total))
    vectors = [vector_total[slot * piece_d : (slot + 1) * piece_d] for slot in range(5)]
    return (
        output_shard,
        input_grad,
        vectors[0],
        vectors[1],
        qkv_total,
        out_total,
        vectors[2],
        vectors[3],
        up_total,
        vector_total[5 * piece_d :],
        down_total,
        vectors[4],
    )


def solution(mesh):
    shard_count, seq_count = mesh.shape["fsdp"], mesh.shape["seq"]

    def step(*args):
        model, hidden = args[0].shape[2], args[12].shape[0]
        rows_each = args[0].shape[0] // shard_count
        if (
            rows_each == 1
            and seq_count == 4
            and model // shard_count == 2 * HD
            and hidden // (4 * shard_count) % 256 == 0
        ):
            fsdp, seq = ("z", "x"), ("y", "c")
            devices = mesh.devices.reshape(shard_count // 2, 2, 2, 2)
            inner, body = Mesh(devices, fsdp + seq), split_shards
        else:
            fsdp, seq = "fsdp", "seq"
            inner, body = mesh, plain_shards
        rows, tokens = P(fsdp, None), P(fsdp, seq, None)
        vector = P(fsdp)
        placed = (tokens, tokens, rows, rows, rows, vector, vector, rows, rows)
        placed += (vector, vector, rows, vector, rows, vector)
        given = (tokens, tokens, vector, vector, rows, rows, vector, vector)
        given += (rows, vector, rows, vector)
        return jax.shard_map(
            body, mesh=inner, in_specs=placed, out_specs=given, check_vma=False
        )(*args)

    return step
```

```python
import functools

import jax
import jax.numpy as jnp
import numpy as np
from jax import lax
from jax.experimental import pallas as pl
from jax.experimental.pallas import tpu as pltpu
from jax.sharding import Mesh
from jax.sharding import PartitionSpec as P

H = 16
HD = 128


EPSILON = 1e-05
MASKED = -1e30
SWAP = ((0, 1), (1, 0))
VMEM_LIMIT = 56 << 20
GELU_A = float(np.sqrt(2.0 / np.pi))
GELU_B = 0.044715


def layer_norm(values, gain_vec, shift_vec):
    center = values - jnp.mean(values, axis=-1, keepdims=True)
    spread = jnp.mean(center * center, axis=-1, keepdims=True)
    return center * lax.rsqrt(spread + EPSILON) * gain_vec + shift_vec


def contract_rows(left, right):
    return lax.dot_general(
        left, right, (((0,), (0,)), ((), ())), preferred_element_type=jnp.float32
    )


def times_transpose(left, right):
    return lax.dot_general(
        left, right, (((1,), (1,)), ((), ())), preferred_element_type=jnp.float32
    )


def item_numbers(starts, lengths, positions):
    inside = (positions[None, :] >= starts[:, None]) & (
        positions[None, :] < (starts + lengths)[:, None]
    )
    labels = jnp.arange(1, starts.shape[0] + 1, dtype=jnp.int32)
    return jnp.sum(jnp.where(inside, labels[:, None], 0), axis=0) - 1


def visible_mask(query_pos, key_pos, query_item, key_item, key_pad):
    same_item = (query_item[:, None] == key_item[None, :]) & (query_item[:, None] >= 0)
    before = key_pos[None, :] < query_pos[:, None]
    return same_item & before & (key_pad[None, :] == 1) | (key_pos[None, :] == query_pos[:, None])


def masked_scores(query_rows, key_rows, visible, score_scale):
    scores = (
        jnp.einsum("qhd,khd->hqk", query_rows, key_rows, preferred_element_type=jnp.float32)
        * score_scale
    )
    return jnp.where(visible[None], scores, MASKED)


def attend_rows(query_rows, key_rows, value_rows, visible, score_scale):
    scores = masked_scores(query_rows, key_rows, visible, score_scale)
    row_peak = jnp.max(scores, axis=-1, keepdims=True)
    exp_scores = jnp.exp(scores - row_peak)
    row_total = jnp.sum(exp_scores, axis=-1, keepdims=True)
    attn_probs = exp_scores / row_total
    mixed_rows = jnp.einsum(
        "hqk,khd->qhd",
        attn_probs.astype(jnp.bfloat16),
        value_rows,
        preferred_element_type=jnp.float32,
    )
    return (mixed_rows, row_peak + jnp.log(row_total))


def attend_back(query_rows, key_rows, value_rows, visible, log_total, mixed_grad, score_scale):
    scores = masked_scores(query_rows, key_rows, visible, score_scale)
    attn_probs = jnp.exp(scores - log_total)
    prob_grad = jnp.einsum(
        "qhd,khd->hqk", mixed_grad, value_rows, preferred_element_type=jnp.float32
    )
    value_part = jnp.einsum(
        "hqk,qhd->khd",
        attn_probs.astype(jnp.bfloat16),
        mixed_grad,
        preferred_element_type=jnp.float32,
    )
    inner_sum = jnp.sum(prob_grad * attn_probs, axis=-1, keepdims=True)
    score_grad = (attn_probs * (prob_grad - inner_sum)).astype(jnp.bfloat16)
    query_grad = (
        jnp.einsum("hqk,khd->qhd", score_grad, key_rows, preferred_element_type=jnp.float32)
        * score_scale
    )
    key_part = (
        jnp.einsum("hqk,qhd->khd", score_grad, query_rows, preferred_element_type=jnp.float32)
        * score_scale
    )
    return (query_grad.astype(jnp.bfloat16), key_part, value_part)


def plain_shards(
    block_input,
    cotangent,
    item_starts,
    item_lengths,
    pad_mask,
    ln1_gain,
    ln1_shift,
    w_qkv,
    w_out,
    ln2_gain,
    ln2_shift,
    w_up,
    up_bias,
    w_down,
    down_bias,
):
    rows_here, tok_count, model_width = block_input.shape
    seq_count = lax.axis_size("seq")
    shard_count = lax.axis_size("fsdp")
    length = tok_count * seq_count
    score_scale = HD ** (-0.5)
    piece_d = ln1_gain.shape[0]
    seq_first = lax.axis_index("seq") * tok_count
    packed = jnp.concatenate([ln1_gain, ln1_shift, ln2_gain, ln2_shift, down_bias, up_bias])
    vector_table = lax.all_gather(packed, "fsdp", axis=0, tiled=True).reshape(shard_count, -1)

    def vector_part(slot):
        return vector_table[:, slot * piece_d : (slot + 1) * piece_d].reshape(-1)

    gain_one, shift_one, gain_two, shift_two, bias_down = [vector_part(slot) for slot in range(5)]
    bias_up = vector_table[:, 5 * piece_d :].reshape(-1)
    qkv_full, out_full = (
        lax.all_gather(w_qkv, "fsdp", axis=0, tiled=True),
        lax.all_gather(w_out, "fsdp", axis=0, tiled=True),
    )
    inputs = block_input.reshape(rows_here * tok_count, model_width).astype(jnp.float32)
    normed_one = layer_norm(inputs, gain_one, shift_one).astype(jnp.bfloat16)
    projected = jnp.dot(normed_one, qkv_full, preferred_element_type=jnp.float32).astype(
        jnp.bfloat16
    )
    query_all = projected[:, :model_width].reshape(rows_here, tok_count, H, HD)
    kv_local = projected[:, model_width:].reshape(rows_here, tok_count, 2 * model_width)
    kv_whole = lax.all_gather(kv_local, "seq", axis=1, tiled=True)
    key_all = kv_whole[:, :, :model_width].reshape(rows_here, length, H, HD)
    value_all = kv_whole[:, :, model_width:].reshape(rows_here, length, H, HD)
    positions = jnp.arange(length, dtype=jnp.int32)
    query_pos = seq_first + jnp.arange(tok_count, dtype=jnp.int32)
    row_index = 0
    item_label = item_numbers(item_starts[row_index], item_lengths[row_index], positions)
    query_item = lax.dynamic_slice_in_dim(item_label, seq_first, tok_count)
    visible = visible_mask(query_pos, positions, query_item, item_label, pad_mask[row_index])
    mixed_part, log_total = attend_rows(
        query_all[row_index], key_all[row_index], value_all[row_index], visible, score_scale
    )
    visible_list = [visible]
    mixed_list = [mixed_part]
    logsum_list = [log_total]
    mixed_all = (
        jnp.stack(mixed_list).reshape(rows_here * tok_count, model_width).astype(jnp.bfloat16)
    )
    residual_one = inputs + jnp.dot(mixed_all, out_full, preferred_element_type=jnp.float32)
    up_full, down_full = (
        lax.all_gather(w_up, "fsdp", axis=0, tiled=True),
        lax.all_gather(w_down, "fsdp", axis=0, tiled=True),
    )
    normed_two = layer_norm(residual_one, gain_two, shift_two).astype(jnp.bfloat16)
    hidden_pre = jnp.dot(normed_two, up_full, preferred_element_type=jnp.float32) + bias_up
    activated = jax.nn.gelu(hidden_pre).astype(jnp.bfloat16)
    block_output = (
        residual_one + jnp.dot(activated, down_full, preferred_element_type=jnp.float32) + bias_down
    )
    output_shard = block_output.astype(jnp.bfloat16).reshape(rows_here, tok_count, model_width)
    up_full, down_full = (
        lax.all_gather(w_up, "fsdp", axis=0, tiled=True),
        lax.all_gather(w_down, "fsdp", axis=0, tiled=True),
    )
    cot_flat = cotangent.reshape(rows_here * tok_count, model_width)
    cot_wide = cot_flat.astype(jnp.float32)
    down_grad = contract_rows(activated, cot_flat)
    down_bias_part = jnp.sum(cot_wide, axis=0)
    act_grad = times_transpose(cot_flat, down_full)
    gelu_back = jax.vjp(jax.nn.gelu, hidden_pre)[1]
    hidden_grad = gelu_back(act_grad)[0].astype(jnp.bfloat16)
    up_grad = contract_rows(normed_two, hidden_grad)
    up_bias_part = jnp.sum(hidden_grad.astype(jnp.float32), axis=0)
    norm_two_grad = times_transpose(hidden_grad, up_full)
    norm_two_back = jax.vjp(layer_norm, residual_one, gain_two, shift_two)[1]
    resid_part, gain_two_grad, shift_two_grad = norm_two_back(norm_two_grad)
    residual_grad = cot_wide + resid_part
    up_sum, down_sum = (
        lax.psum_scatter(up_grad, "fsdp", scatter_dimension=0, tiled=True),
        lax.psum_scatter(down_grad, "fsdp", scatter_dimension=0, tiled=True),
    )
    qkv_full, out_full = (
        lax.all_gather(w_qkv, "fsdp", axis=0, tiled=True),
        lax.all_gather(w_out, "fsdp", axis=0, tiled=True),
    )
    branch_grad = residual_grad.astype(jnp.bfloat16)
    out_grad = contract_rows(mixed_all, branch_grad)
    mixed_grad = (
        times_transpose(branch_grad, out_full)
        .astype(jnp.bfloat16)
        .reshape(rows_here, tok_count, H, HD)
    )
    row_index = 0
    query_grad, key_part, value_part = attend_back(
        query_all[row_index],
        key_all[row_index],
        value_all[row_index],
        visible_list[row_index],
        logsum_list[row_index],
        mixed_grad[row_index],
        score_scale,
    )
    query_list = [query_grad.reshape(tok_count, model_width)]
    kv_list = [
        jnp.concatenate(
            [key_part.reshape(length, model_width), value_part.reshape(length, model_width)], axis=1
        )
    ]
    kv_terms = jnp.stack(kv_list)
    kv_grad = lax.psum_scatter(kv_terms, "seq", scatter_dimension=1, tiled=True).astype(
        jnp.bfloat16
    )
    proj_grad = jnp.concatenate(
        [
            jnp.stack(query_list).reshape(rows_here * tok_count, model_width),
            kv_grad.reshape(rows_here * tok_count, 2 * model_width),
        ],
        axis=1,
    )
    qkv_grad = contract_rows(normed_one, proj_grad)
    norm_one_grad = times_transpose(proj_grad, qkv_full)
    norm_one_back = jax.vjp(layer_norm, inputs, gain_one, shift_one)[1]
    input_part, gain_one_grad, shift_one_grad = norm_one_back(norm_one_grad)
    input_grad = (residual_grad + input_part).reshape(rows_here, tok_count, model_width)
    vector_grad = jnp.concatenate(
        [
            piece_grad.reshape(shard_count, -1)
            for piece_grad in (
                gain_one_grad,
                shift_one_grad,
                gain_two_grad,
                shift_two_grad,
                down_bias_part,
                up_bias_part,
            )
        ],
        axis=1,
    ).reshape(-1)
    qkv_sum, out_sum, vector_sum = (
        lax.psum_scatter(qkv_grad, "fsdp", scatter_dimension=0, tiled=True),
        lax.psum_scatter(out_grad, "fsdp", scatter_dimension=0, tiled=True),
        lax.psum_scatter(vector_grad, "fsdp", scatter_dimension=0, tiled=True),
    )
    up_total, down_total, qkv_total, out_total, vector_total = lax.psum(
        (up_sum, down_sum, qkv_sum, out_sum, vector_sum), "seq"
    )
    gain_one_out = vector_total[0:piece_d]
    shift_one_out = vector_total[piece_d : 2 * piece_d]
    gain_two_out = vector_total[2 * piece_d : 3 * piece_d]
    shift_two_out = vector_total[3 * piece_d : 4 * piece_d]
    down_bias_out = vector_total[4 * piece_d : 5 * piece_d]
    up_bias_out = vector_total[5 * piece_d :]
    return (
        output_shard,
        input_grad,
        gain_one_out,
        shift_one_out,
        qkv_total,
        out_total,
        gain_two_out,
        shift_two_out,
        up_total,
        up_bias_out,
        down_total,
        down_bias_out,
    )


def gather_small(vector, z_count):
    line = [vector]
    for j in range(1, z_count):
        line.append(lax.ppermute(vector, "z", [(i, (i + j) % z_count) for i in range(z_count)]))
    return line + [lax.ppermute(piece, "x", SWAP) for piece in line]


def gather_weight(shard, *others):
    near = lax.all_gather(shard, "z", axis=0, tiled=False)
    return [near, lax.ppermute(after(near, *others), "x", SWAP)]


def stage(flag, work, *args):
    shapes = jax.eval_shape(work, *args)

    def nothing(*_):
        return jax.tree.map(lambda a: jnp.zeros(a.shape, a.dtype), shapes)

    return lax.cond(flag, work, nothing, *args)


class Line:
    def __init__(self):
        self.last = ()

    def enter(self, value):
        return after(value, *self.last)

    def leave(self, *results):
        self.last = results[:1]
        return results


def after(value, *others):
    return lax.optimization_barrier((value,) + others)[0]


def seq_pieces(block, *others):
    return core_pieces(block, after(lax.ppermute(block, "y", SWAP), *others))


def core_pieces(block, other):
    return [block, lax.ppermute(block, "c", SWAP), other, lax.ppermute(other, "c", SWAP)]


def by_bit(bit, mine, theirs):
    return jnp.where(bit == 0, mine, theirs), jnp.where(bit == 0, theirs, mine)


def gather_tokens(block, yi, ci, *others):
    parts = seq_pieces(block, *others)
    near = by_bit(ci, parts[0], parts[1])
    far = by_bit(ci, parts[2], parts[3])
    rows = [jnp.where(yi == 0, n, f) for n, f in zip(near, far)]
    rows += [jnp.where(yi == 0, f, n) for n, f in zip(near, far)]
    return jnp.concatenate(rows, axis=0)


def core_sum(partial, yi, ci):
    tokens = partial.shape[0] // 4
    parts = partial.reshape(2, 2, tokens, partial.shape[1])
    away = lax.dynamic_index_in_dim(parts, 1 - ci, 1, keepdims=False)
    home = lax.dynamic_index_in_dim(parts, ci, 1, keepdims=False)
    total = home.astype(jnp.float32) + lax.ppermute(away, "c", SWAP).astype(jnp.float32)
    away = lax.dynamic_index_in_dim(total, 1 - yi, 0, keepdims=False).astype(jnp.bfloat16)
    return lax.dynamic_index_in_dim(total, yi, 0, keepdims=False), away


def home_sum(home, other):
    return home + other.astype(jnp.float32)


def scatter_tokens(partial, yi, ci, *others):
    home, away = core_sum(partial, yi, ci)
    return home_sum(home, after(lax.ppermute(away, "y", SWAP), *others))


COST_SCALE = 0.01


def cost(flops, bytes_accessed, transcendentals):
    return pl.CostEstimate(
        flops=int(flops * COST_SCALE),
        bytes_accessed=int(bytes_accessed * COST_SCALE),
        transcendentals=int(transcendentals * COST_SCALE),
    )


def params(limit=VMEM_LIMIT):
    return pltpu.CompilerParams(vmem_limit_bytes=limit)


def weight_matmul(left, pieces, offsets, shape, back, body, extras, outs, chunk):
    rows = left.shape[0]
    depth, width = shape
    out_width = depth if back else width
    steps = out_width // chunk
    n_pieces, n_extras = len(pieces), len(extras)
    blocks = [(p, k) for p, piece in enumerate(pieces) for k in range(piece.shape[0])]
    block_rows, block_cols = pieces[0].shape[1:]
    row_count, col_count = depth // block_rows, width // block_cols

    def kernel(offs_ref, left_ref, *refs):
        piece_refs = refs[:n_pieces]
        extra_refs = refs[n_pieces : n_pieces + n_extras]
        out_refs = refs[n_pieces + n_extras : -2]
        held, sems = refs[-2:]
        step = pl.program_id(0)

        def slot(row, col):
            return sems.at[row, col]

        @pl.when(step == 0)
        def _():
            for b, (p, k) in enumerate(blocks):
                row, col = offs_ref[0, b], offs_ref[1, b]
                target = held.at[
                    pl.ds(pl.multiple_of(row * block_rows, block_rows), block_rows),
                    pl.ds(pl.multiple_of(col * block_cols, block_cols), block_cols),
                ]
                pltpu.make_async_copy(piece_refs[p].at[k], target, slot(row, col)).start()

        def arrive(row, col):
            target = held.at[
                pl.ds(row * block_rows, block_rows), pl.ds(col * block_cols, block_cols)
            ]
            pltpu.make_async_copy(piece_refs[0].at[0], target, slot(row, col)).wait()

        for n in range(steps):
            needed = [
                (row, col)
                for row in range(row_count)
                for col in range(col_count)
                if (
                    row * block_rows // chunk if back else col * block_cols // chunk
                ) == n
            ]
            if needed:

                @pl.when(step == n)
                def _():
                    for row, col in needed:
                        arrive(row, col)

        start = pl.ds(pl.multiple_of(step * chunk, chunk), chunk)
        if back:
            values = lax.dot_general(
                left_ref[...],
                held[start, :],
                (((1,), (1,)), ((), ())),
                preferred_element_type=jnp.float32,
            )
        else:
            values = jnp.dot(
                left_ref[...], held[:, start], preferred_element_type=jnp.float32
            )
        body(values, extra_refs, out_refs)

    def column_spec(array):
        return pl.BlockSpec((array.shape[0], chunk), lambda i, offs: (0, i))

    flops = 2 * rows * depth * width
    moved = 2 * (left.size + depth * width) + sum(
        a.size * a.dtype.itemsize for a in list(extras) + list(outs)
    )
    return pl.pallas_call(
        kernel,
        grid_spec=pltpu.PrefetchScalarGridSpec(
            num_scalar_prefetch=1,
            grid=(steps,),
            in_specs=[
                pl.BlockSpec(
                    left.shape, lambda i, offs: (0, 0), pipeline_mode=pl.Buffered(1)
                )
            ]
            + [pl.BlockSpec(memory_space=pl.ANY)] * n_pieces
            + [column_spec(a) for a in extras],
            out_specs=[column_spec(a) for a in outs],
            scratch_shapes=[
                pltpu.VMEM((depth, width), jnp.bfloat16),
                pltpu.SemaphoreType.DMA((row_count, col_count)),
            ],
        ),
        out_shape=list(outs),
        cost_estimate=cost(flops=flops, bytes_accessed=moved, transcendentals=0),
        compiler_params=params(),
    )(offsets, left, *pieces, *extras)


def store_low(values, extra_refs, out_refs):
    out_refs[0][...] = values.astype(jnp.bfloat16)


def store_gelu(values, extra_refs, out_refs):
    hidden = values + extra_refs[0][...]
    square = hidden * hidden
    bend = jnp.tanh(GELU_A * hidden * (1.0 + GELU_B * square))
    half = 0.5 * (1.0 + bend)
    out_refs[0][...] = (hidden * half).astype(jnp.bfloat16)
    slope = half + 0.5 * hidden * (1.0 - bend * bend) * (
        GELU_A * (1.0 + 3.0 * GELU_B * square)
    )
    out_refs[1][...] = slope


def store_hidden_grad(values, extra_refs, out_refs):
    low = (values * extra_refs[0][...]).astype(jnp.bfloat16)
    out_refs[0][...] = low
    out_refs[1][...] = jnp.sum(low.astype(jnp.float32), axis=0, keepdims=True)


def weight_grad(left, right, where, count, block, width, addend=None, parts=1):
    rows = left.shape[0]
    part = width // parts
    added = () if addend is None else (addend,)

    def kernel(where_ref, left_ref, right_ref, *refs):
        for n in range(parts):
            cols = slice(n * part, (n + 1) * part)
            value = lax.dot_general(
                left_ref[...],
                right_ref[:, cols],
                (((0,), (0,)), ((), ())),
                preferred_element_type=jnp.float32,
            )
            if added:
                value = value + refs[0][0, :, cols].astype(jnp.float32)
            refs[len(added) + n][0] = value.astype(jnp.bfloat16)

    return pl.pallas_call(
        kernel,
        grid_spec=pltpu.PrefetchScalarGridSpec(
            num_scalar_prefetch=1,
            grid=(count,),
            in_specs=[
                pl.BlockSpec((rows, block), lambda k, at: (0, at[k])),
                pl.BlockSpec((rows, width), lambda k, at: (0, at[count])),
            ]
            + [pl.BlockSpec((1, block, width), lambda k, at: (k, 0, 0))] * len(added),
            out_specs=[pl.BlockSpec((1, block, part), lambda k, at: (k, 0, 0))] * parts,
        ),
        out_shape=[jax.ShapeDtypeStruct((count, block, part), jnp.bfloat16)] * parts,
        cost_estimate=cost(
            flops=2 * rows * count * block * width,
            bytes_accessed=2 * rows * (count * block + width) + 4 * count * block * width,
            transcendentals=0,
        ),
        compiler_params=params(),
    )(where, left, right, *added)


def slice_qkv(w_qkv, where, width):
    rows = w_qkv.shape[0]
    heads = H // 4

    def kernel(at_ref, from_ref, to_ref):
        for i in range(heads):
            col = pl.ds(pl.multiple_of((2 * i + at_ref[1]) * HD, HD), HD)
            to_ref[:, i * HD : (i + 1) * HD] = from_ref[:, col]

    part = heads * HD
    return pl.pallas_call(
        kernel,
        grid_spec=pltpu.PrefetchScalarGridSpec(
            num_scalar_prefetch=1,
            grid=(3,),
            in_specs=[pl.BlockSpec((rows, 2 * part), lambda g, at: (0, 2 * g + at[0]))],
            out_specs=pl.BlockSpec((rows, part), lambda g, at: (0, g)),
        ),
        out_shape=jax.ShapeDtypeStruct((rows, width), jnp.bfloat16),
        cost_estimate=cost(flops=0, bytes_accessed=3 << 20, transcendentals=0),
        compiler_params=params(),
    )(where, w_qkv)


def slice_weights(w_out, w_up, w_down, where, shard_count):
    rows, model = w_out.shape
    ff_part = w_down.shape[0] // 4
    steps = shard_count
    part = ff_part // steps
    up_half = steps // 2

    def kernel(at_ref, out_ref, up_ref, down_ref, out_to, low_to, high_to, left_to, right_to):
        step = pl.program_id(0)
        for n, up_to in enumerate((low_to, high_to)):

            @pl.when(step // up_half == n)
            def _():
                up_to[...] = up_ref[...]

        @pl.when(step == 0)
        def _():
            out_to[...] = out_ref[...]

        left_to[...] = down_ref[:, : model // 2]
        right_to[...] = down_ref[:, model // 2 :]

    def up_spec(n):
        return pl.BlockSpec(
            (rows, ff_part), lambda i, at: (0, jnp.clip(i - n * up_half, 0, up_half - 1))
        )

    return pl.pallas_call(
        kernel,
        grid_spec=pltpu.PrefetchScalarGridSpec(
            num_scalar_prefetch=1,
            grid=(steps,),
            in_specs=[
                pl.BlockSpec((rows // 2, model // 2), lambda i, at: (at[1], at[0])),
                pl.BlockSpec((rows, ff_part), lambda i, at: (0, 4 * i + 2 * at[0] + at[1])),
                pl.BlockSpec(
                    (part, model), lambda i, at: ((2 * at[0] + at[1]) * steps + i, 0)
                ),
            ],
            out_specs=[
                pl.BlockSpec((rows // 2, model // 2), lambda i, at: (0, 0)),
                up_spec(0),
                up_spec(1),
                pl.BlockSpec((part, model // 2), lambda i, at: (i, 0)),
                pl.BlockSpec((part, model // 2), lambda i, at: (i, 0)),
            ],
        ),
        out_shape=[
            jax.ShapeDtypeStruct(shape, jnp.bfloat16)
            for shape in [(rows // 2, model // 2)]
            + [(rows, ff_part * up_half)] * 2
            + [(ff_part, model // 2)] * 2
        ],
        cost_estimate=cost(flops=0, bytes_accessed=9 << 20, transcendentals=0),
        compiler_params=params(),
    )(where, w_out, w_up, w_down)


def visible_tile(query_item, key_item, first_query, n_query, n_key):
    query_pos = first_query + lax.broadcasted_iota(jnp.int32, (n_query, n_key), 0)
    key_pos = lax.broadcasted_iota(jnp.int32, (n_query, n_key), 1)
    return ((query_item == key_item) & (key_pos < query_pos)) | (key_pos == query_pos)


def head_spec(length, first):
    return pl.BlockSpec((length, HD), lambda h: (0, first + h))


def attention(projected, query_item, key_item, heads, tile):
    length = projected.shape[0]
    scale = HD ** (-0.5)

    def kernel(q_ref, k_ref, v_ref, qi_ref, ki_ref, mixed_ref, log_ref):
        for start in range(0, length, tile):
            stop = start + tile
            rows = slice(start, stop)
            scores = (
                lax.dot_general(
                    q_ref[rows, :],
                    k_ref[:stop, :],
                    (((1,), (1,)), ((), ())),
                    preferred_element_type=jnp.float32,
                )
                * scale
            )
            seen = visible_tile(qi_ref[rows, :], ki_ref[:, :stop], start, tile, stop)
            scores = jnp.where(seen, scores, MASKED)
            peak = jnp.max(scores, axis=-1, keepdims=True)
            weights = jnp.exp(scores - peak)
            total = jnp.sum(weights, axis=-1, keepdims=True)
            probs = (weights * (1.0 / total)).astype(jnp.bfloat16)
            mixed_ref[rows, :] = jnp.dot(
                probs, v_ref[:stop, :], preferred_element_type=jnp.float32
            ).astype(jnp.bfloat16)
            log_ref[0, rows, :] = peak + jnp.log(total)

    whole = lambda rows, cols: pl.BlockSpec((rows, cols), lambda h: (0, 0))
    return pl.pallas_call(
        kernel,
        grid=(heads,),
        in_specs=[head_spec(length, g * heads) for g in range(3)]
        + [whole(length, 1), whole(1, length)],
        out_specs=[head_spec(length, 0), pl.BlockSpec((1, length, 1), lambda h: (h, 0, 0))],
        out_shape=[
            jax.ShapeDtypeStruct((length, heads * HD), jnp.bfloat16),
            jax.ShapeDtypeStruct((heads, length, 1), jnp.float32),
        ],
        cost_estimate=cost(
            flops=4 * heads * length * length * HD,
            bytes_accessed=8 * length * heads * HD,
            transcendentals=heads * length * length,
        ),
        compiler_params=params(),
    )(projected, projected, projected, query_item, key_item)


def attention_back(projected, mixed_grad, log_total, query_item, key_item, heads, tile):
    length = projected.shape[0]
    scale = HD ** (-0.5)

    def kernel(q_ref, k_ref, v_ref, g_ref, log_ref, qi_ref, ki_ref, grad_ref, dk_ref, dv_ref):
        head = pl.program_id(0)

        def place(group):
            return pl.ds(pl.multiple_of((group * heads + head) * HD, HD), HD)

        for start in reversed(range(0, length, tile)):
            stop = start + tile
            rows = slice(start, stop)
            query, grad = q_ref[rows, :], g_ref[rows, :]
            key, value = k_ref[:stop, :], v_ref[:stop, :]
            scores = (
                lax.dot_general(
                    query, key, (((1,), (1,)), ((), ())), preferred_element_type=jnp.float32
                )
                * scale
            )
            seen = visible_tile(qi_ref[rows, :], ki_ref[:, :stop], start, tile, stop)
            probs = jnp.exp(jnp.where(seen, scores, MASKED) - log_ref[0, rows, :])
            prob_grad = lax.dot_general(
                grad, value, (((1,), (1,)), ((), ())), preferred_element_type=jnp.float32
            )
            inner = jnp.sum(prob_grad * probs, axis=-1, keepdims=True)
            score_grad = (probs * (prob_grad - inner)).astype(jnp.bfloat16)
            grad_ref[rows, place(0)] = (
                jnp.dot(score_grad, key, preferred_element_type=jnp.float32) * scale
            ).astype(jnp.bfloat16)
            key_part = lax.dot_general(
                score_grad, query, (((0,), (0,)), ((), ())), preferred_element_type=jnp.float32
            )
            value_part = lax.dot_general(
                probs.astype(jnp.bfloat16),
                grad,
                (((0,), (0,)), ((), ())),
                preferred_element_type=jnp.float32,
            )
            if stop == length:
                dk_ref[...] = key_part
                dv_ref[...] = value_part
            else:
                dk_ref[:stop, :] += key_part
                dv_ref[:stop, :] += value_part
        grad_ref[:, place(1)] = (dk_ref[...] * scale).astype(jnp.bfloat16)
        grad_ref[:, place(2)] = dv_ref[...].astype(jnp.bfloat16)

    whole = lambda rows, cols: pl.BlockSpec((rows, cols), lambda h: (0, 0))
    return pl.pallas_call(
        kernel,
        grid=(heads,),
        in_specs=[head_spec(length, g * heads) for g in range(3)]
        + [
            head_spec(length, 0),
            pl.BlockSpec((1, length, 1), lambda h: (h, 0, 0)),
            whole(length, 1),
            whole(1, length),
        ],
        out_specs=whole(length, 3 * heads * HD),
        out_shape=jax.ShapeDtypeStruct((length, 3 * heads * HD), jnp.bfloat16),
        scratch_shapes=[pltpu.VMEM((length, HD), jnp.float32)] * 2,
        cost_estimate=cost(
            flops=10 * heads * length * length * HD,
            bytes_accessed=16 * length * heads * HD,
            transcendentals=heads * length * length,
        ),
        compiler_params=params(),
    )(projected, projected, projected, mixed_grad, log_total, query_item, key_item)


def widen(chunks, places, grid, piece_specs, out_block, out_index, out_shape, write):
    def kernel(place_ref, *refs):
        for n in range(len(chunks)):
            for r in range(4):
                write(n, place_ref[r], refs[4 * n + r], refs[-1])

    return pl.pallas_call(
        kernel,
        grid_spec=pltpu.PrefetchScalarGridSpec(
            num_scalar_prefetch=1,
            grid=(grid,),
            in_specs=[
                pl.BlockSpec(block, functools.partial(lambda at, i, pos: at(i), at))
                for block, at in piece_specs
                for _ in range(4)
            ],
            out_specs=pl.BlockSpec(out_block, lambda i, pos: out_index(i)),
        ),
        out_shape=jax.ShapeDtypeStruct(out_shape, jnp.float32),
        cost_estimate=cost(
            flops=0, bytes_accessed=6 * int(np.prod(out_shape)), transcendentals=0
        ),
        compiler_params=params(),
    )(places, *[piece for pieces in chunks for piece in pieces])


def widen_columns(pieces, places, blocks):
    rows, width = pieces[0].shape
    part = width // blocks

    def write(n, pos, piece, out):
        out[:, pl.ds(pl.multiple_of(pos * part, part), part)] = piece[...].astype(jnp.float32)

    return widen(
        [pieces],
        places,
        blocks,
        [((rows, part), lambda i: (0, i))],
        (rows, 4 * part),
        lambda i: (0, i),
        (rows, 4 * width),
        write,
    )


def widen_rows(pieces, places):
    rows, width = pieces[0].shape

    def write(n, pos, piece, out):
        @pl.when(pos == pl.program_id(0))
        def _():
            out[...] = piece[...].astype(jnp.float32)

    return widen(
        [pieces],
        places,
        4,
        [((rows, width), lambda i: (0, 0))],
        (rows, width),
        lambda i: (i, 0),
        (4 * rows, width),
        write,
    )


def widen_heads(chunks, places):
    rows, width = chunks[0][0].shape
    heads = H // 4
    part = heads * HD

    def write(n, pos, piece, out):
        first = lax.div(pos, 2) * part * 2 + lax.rem(pos, 2) * HD
        for i in range(width // HD):
            head = n * (width // HD) + i

            @pl.when(pl.program_id(0) == head // heads)
            def _():
                cols = pl.ds(pl.multiple_of(first + 2 * (head % heads) * HD, HD), HD)
                out[:, cols] = piece[:, i * HD : (i + 1) * HD].astype(jnp.float32)

    return widen(
        chunks,
        places,
        3,
        [((rows, width), lambda i: (0, 0))] * 2,
        (rows, 4 * part),
        lambda i: (0, i),
        (rows, 12 * part),
        write,
    )


def widen_quarters(pieces, places):
    rows, width = pieces[0].shape

    def write(n, pos, piece, out):
        row = pl.multiple_of(lax.rem(pos, 2) * rows, rows)
        col = pl.multiple_of(lax.div(pos, 2) * width, width)
        out[pl.ds(row, rows), pl.ds(col, width)] = piece[...].astype(jnp.float32)

    return widen(
        [pieces],
        places,
        1,
        [((rows, width), lambda i: (0, 0))],
        (2 * rows, 2 * width),
        lambda i: (0, 0),
        (2 * rows, 2 * width),
        write,
    )


def norm_back(values, gain_vec, incoming):
    center = values - jnp.mean(values, axis=-1, keepdims=True)
    spread = jnp.mean(center * center, axis=-1, keepdims=True)
    inverse = lax.rsqrt(spread + EPSILON)
    unit = center * inverse
    scaled = incoming * gain_vec
    inner = jnp.mean(scaled * unit, axis=-1, keepdims=True)
    grad = (scaled - jnp.mean(scaled, axis=-1, keepdims=True) - unit * inner) * inverse
    return grad, jnp.sum(incoming * unit, axis=0), jnp.sum(incoming, axis=0)


def split_shards(
    block_input,
    cotangent,
    item_starts,
    item_lengths,
    pad_mask,
    ln1_gain,
    ln1_shift,
    w_qkv,
    w_out,
    ln2_gain,
    ln2_shift,
    w_up,
    up_bias,
    w_down,
    down_bias,
):
    low, wide = jnp.bfloat16, jnp.float32
    z_count = lax.axis_size("z")
    shard_count = 2 * z_count
    zi, xi, yi, ci = [lax.axis_index(name) for name in ("z", "x", "y", "c")]
    si = 2 * yi + ci
    tok_count, model = block_input.shape[1:]
    length = 4 * tok_count
    piece_d, ff_piece = ln1_gain.shape[0], up_bias.shape[0]
    ff_part = ff_piece // 4
    ff_here = ff_part * shard_count
    heads = H // 4
    places = jnp.stack([jnp.bitwise_xor(si, r) for r in range(4)]).astype(jnp.int32)

    packed = jnp.concatenate([ln1_gain, ln1_shift, ln2_gain, ln2_shift, down_bias, up_bias])
    vector_stack = jnp.stack(gather_small(packed, z_count))
    owners = jnp.stack(
        [
            lax.rem(zi - j + z_count, z_count) * 2 + jnp.bitwise_xor(xi, dx)
            for dx in range(2)
            for j in range(z_count)
        ]
    )
    hit = owners[None, :] == jnp.arange(shard_count, dtype=jnp.int32)[:, None]
    vector_table = jnp.sum(jnp.where(hit[:, :, None], vector_stack[None], 0.0), axis=1)

    def vector_part(slot):
        return vector_table[:, slot * piece_d : (slot + 1) * piece_d].reshape(-1)

    gain_one, shift_one, gain_two, shift_two, bias_down = [vector_part(slot) for slot in range(5)]
    bias_up = lax.dynamic_index_in_dim(
        vector_table[:, 5 * piece_d :].reshape(shard_count, 4, ff_part), si, 1, keepdims=False
    ).reshape(1, ff_here)

    line = Line()
    flag = item_lengths[0, 0] > 0
    where = jnp.stack([yi, ci]).astype(jnp.int32)
    qkv_slice = slice_qkv(w_qkv, where, 3 * heads * HD)
    slices = slice_weights(w_out, w_up, w_down, after(where, qkv_slice), shard_count)
    half = model // 2
    qkv_width = 3 * heads * HD
    qkv_parts = gather_weight(qkv_slice)
    down_pair = jnp.stack([slices[4], lax.ppermute(slices[4], "x", SWAP)])
    inputs = after(block_input, down_pair).reshape(tok_count, model).astype(wide)
    normed_one = layer_norm(inputs, gain_one, shift_one).astype(low)
    out_parts = gather_weight(after(slices[0], normed_one), qkv_parts[1])
    out_parts = out_parts + [lax.ppermute(piece, "y", SWAP) for piece in out_parts]

    near_blocks = [2 * z + xi for z in range(z_count)]
    far_blocks = [2 * z + 1 - xi for z in range(z_count)]
    split = near_blocks + far_blocks
    paired = [b for pair in zip(near_blocks, far_blocks) for b in pair]
    zero = jnp.zeros_like(xi)

    def table(*rows):
        return jnp.stack([jnp.stack(row) for row in rows]).astype(jnp.int32)

    qkv_offsets = table(split, [zero] * shard_count)
    up_offsets = table(split + split, [zero] * shard_count + [zero + 1] * shard_count)
    down_offsets = table(split + paired, [zero] * shard_count + [zero + 1] * shard_count)
    out_offsets = table(split + split, [yi] * shard_count + [1 - yi] * shard_count)

    def blocks_at(blocks, n):
        return table(blocks + [zero + n])[0]

    def sum_small(terms):
        def term(j):
            return lax.dynamic_index_in_dim(
                terms, lax.rem(zi - j + z_count, z_count), 0, keepdims=False
            )

        total = term(0).astype(wide)
        for j in range(1, z_count):
            total = total + lax.ppermute(
                term(j), "z", [(i, (i - j) % z_count) for i in range(z_count)]
            ).astype(wide)
        return total

    def plain_matmul(left, pieces, offsets, shape, back, body, extras, outs):
        return weight_matmul(left, pieces, offsets, shape, back, body, extras, outs, 512)

    def matmul(left, *others):
        return line.leave(*plain_matmul(line.enter(left), *others))

    def grad_chunk(left, right, blocks, n, block, width):
        return line.leave(
            *weight_grad(line.enter(left), right, blocks_at(blocks, n), len(blocks), block, width)
        )[0]

    def far_terms(left, right, block):
        terms = grad_chunk(left, right, far_blocks, 0, block, right.shape[1])
        return lax.ppermute(terms, "x", SWAP)

    def near_terms(left, right, block, addend, parts=1):
        return weight_grad(
            left, right, blocks_at(near_blocks, 0), z_count, block, addend.shape[2], addend, parts
        )

    def sum_over_z(total):
        return lax.psum_scatter(total, "z", scatter_dimension=0, tiled=False)

    def shape(rows, cols, kind=low):
        return jax.ShapeDtypeStruct((rows, cols), kind)

    normed_one = gather_tokens(normed_one, yi, ci, qkv_parts[0])
    cot_flat = after(cotangent.reshape(tok_count, model), normed_one)
    cot_wide = cot_flat.astype(wide)
    cot_all = gather_tokens(cot_flat, yi, ci)
    (projected,) = matmul(
        after(normed_one, cot_all),
        qkv_parts,
        qkv_offsets,
        (model, qkv_width),
        False,
        store_low,
        (),
        (shape(length, qkv_width),),
    )
    up_parts = gather_weight(slices[1], projected)
    up_high = lax.all_gather(slices[2], "z", axis=0, tiled=False)
    down_parts = gather_weight(slices[3], projected)
    down_parts.append(lax.all_gather(down_pair, "z", axis=0, tiled=True))
    positions = jnp.arange(length, dtype=jnp.int32)
    item_label = item_numbers(item_starts[0], item_lengths[0], positions)
    query_item = item_label[:, None]
    key_item = jnp.where((item_label >= 0) & (pad_mask[0] == 1), item_label, -2)[None, :]
    mixed_heads, log_total = line.leave(
        *attention(line.enter(projected), query_item, key_item, heads, 256)
    )

    def attend_out(mixed_heads):
        halves = mixed_heads.reshape(2, 2 * tok_count, heads * HD)
        away = lax.dynamic_index_in_dim(halves, 1 - yi, 0, keepdims=False)
        mine = lax.dynamic_index_in_dim(halves, yi, 0, keepdims=False)
        other = lax.ppermute(away, "y", SWAP)
        mixed = jnp.concatenate(by_bit(yi, mine, other), axis=1)
        (out_partial,) = plain_matmul(
            mixed,
            out_parts,
            out_offsets,
            (half, model),
            False,
            store_low,
            (),
            (shape(2 * tok_count, model),),
        )
        halves = out_partial.reshape(2, tok_count, model)
        away = lax.dynamic_index_in_dim(halves, 1 - ci, 0, keepdims=False)
        home = lax.dynamic_index_in_dim(halves, ci, 0, keepdims=False)
        residual_one = (
            inputs + home.astype(wide) + lax.ppermute(away, "c", SWAP).astype(wide)
        )
        normed_two = layer_norm(residual_one, gain_two, shift_two).astype(low)
        return normed_two, residual_one, mine, other

    up_parts += [up_high, lax.ppermute(after(up_high, mixed_heads), "x", SWAP)]
    normed_two, residual_one, mixed_home, mixed_other = line.leave(
        *stage(flag, attend_out, after(line.enter(mixed_heads), up_parts[0], up_high))
    )
    normed_two = gather_tokens(normed_two, yi, ci, up_parts[1], up_parts[3])
    activated, slope = matmul(
        normed_two,
        up_parts,
        up_offsets,
        (model, ff_here),
        False,
        store_gelu,
        (bias_up,),
        (shape(length, ff_here), shape(length, ff_here, wide)),
    )

    mixed_last = lax.ppermute(after(mixed_home, activated), "y", SWAP)
    others_heads = jnp.concatenate(by_bit(yi, mixed_other, mixed_last), axis=0)
    mixed = jnp.concatenate(by_bit(yi, mixed_heads, others_heads), axis=1)

    down_bias_part = jnp.sum(cot_wide, axis=0)
    down_sum = grad_chunk(
        after(activated, down_parts[1], mixed), cot_all, paired, 0, ff_part, model
    )
    down_pair = lax.psum_scatter(
        down_sum.reshape(z_count, 2, ff_part, model), "z", scatter_dimension=0, tiled=False
    )
    hidden_grad, up_bias_part = matmul(
        cot_all,
        down_parts,
        down_offsets,
        (ff_here, model),
        True,
        store_hidden_grad,
        (slope,),
        (shape(length, ff_here), shape(1, ff_here, wide)),
    )
    up_far = far_terms(normed_two, hidden_grad, piece_d)
    (norm_two_partial,) = matmul(
        hidden_grad,
        up_parts,
        up_offsets,
        (model, ff_here),
        True,
        store_low,
        (),
        (shape(length, model),),
    )
    def norm_two_back(norm_two_partial):
        home, away = core_sum(norm_two_partial, yi, ci)
        other = lax.ppermute(away, "y", SWAP)
        (down_partial,) = plain_matmul(
            after(activated, away),
            down_parts,
            down_offsets,
            (ff_here, model),
            False,
            store_low,
            (),
            (shape(length, model),),
        )
        norm_two_grad = home_sum(home, after(other, down_partial))
        resid_part, gain_two_grad, shift_two_grad = norm_back(
            residual_one, gain_two, norm_two_grad
        )
        residual_grad = cot_wide + resid_part
        branch_grad = residual_grad.astype(low)
        branch_pair = jnp.concatenate(
            by_bit(ci, branch_grad, lax.ppermute(branch_grad, "c", SWAP)), axis=0
        )
        return branch_pair, residual_grad, gain_two_grad, shift_two_grad, down_partial

    branch_pair, residual_grad, gain_two_grad, shift_two_grad, down_partial = line.leave(
        *stage(flag, norm_two_back, line.enter(norm_two_partial))
    )

    out_blocks = far_blocks + near_blocks

    def out_back(branch_pair):
        (mixed_grad_pair,) = plain_matmul(
            branch_pair,
            out_parts,
            out_offsets,
            (half, model),
            True,
            store_low,
            (),
            (shape(2 * tok_count, half),),
        )
        part = heads * HD
        away = lax.dynamic_slice_in_dim(mixed_grad_pair, (1 - yi) * part, part, 1)
        home = lax.dynamic_slice_in_dim(mixed_grad_pair, yi * part, part, 1)
        theirs = lax.ppermute(away, "y", SWAP)
        feed_home, feed_away = core_sum(after(down_partial, away), yi, ci)
        theirs = after(theirs, feed_away)
        return jnp.concatenate(by_bit(yi, home, theirs), axis=0), feed_home, feed_away

    mixed_grad, feed_home, feed_away = line.leave(
        *stage(flag, out_back, line.enter(branch_pair))
    )
    away = lax.dynamic_slice_in_dim(branch_pair, (1 - yi) * half, half, 1)
    home = lax.dynamic_slice_in_dim(branch_pair, yi * half, half, 1)
    branch_other = lax.ppermute(after(away, mixed_grad), "y", SWAP)
    branch_all = jnp.concatenate(by_bit(yi, home, branch_other), axis=0)
    (proj_grad,) = line.leave(
        attention_back(
            projected,
            line.enter(mixed_grad),
            log_total,
            query_item,
            key_item,
            heads,
            256,
        )
    )
    qkv_far = far_terms(normed_one, proj_grad, piece_d)
    (up_sum,) = line.leave(
        near_terms(
            line.enter(after(normed_two, branch_other)), hidden_grad, piece_d, up_far
        )[0]
    )
    up_shard = sum_over_z(after(up_sum, down_pair))
    (norm_one_partial,) = matmul(
        proj_grad,
        qkv_parts,
        qkv_offsets,
        (model, qkv_width),
        True,
        store_low,
        (),
        (shape(length, model),),
    )

    out_sum = line.leave(
        *weight_grad(
            line.enter(mixed),
            branch_all,
            blocks_at(out_blocks, 0),
            shard_count,
            piece_d // 2,
            half,
        )
    )[0]
    feed_other = lax.ppermute(after(feed_away, up_sum), "y", SWAP)

    def norm_one_back(norm_one_partial):
        home, away = core_sum(norm_one_partial, yi, ci)
        away = lax.ppermute(away, "y", SWAP)
        norm_one_grad = home_sum(home, away)
        input_part, gain_one_grad, shift_one_grad = norm_back(inputs, gain_one, norm_one_grad)
        input_grad = (residual_grad + input_part).reshape(1, tok_count, model)
        return input_grad, gain_one_grad, shift_one_grad

    input_grad, gain_one_grad, shift_one_grad = line.leave(
        *stage(flag, norm_one_back, after(line.enter(norm_one_partial), feed_other))
    )
    qkv_sums = line.leave(
        *near_terms(
            line.enter(after(normed_one, up_shard)), proj_grad, piece_d, qkv_far, 2
        )
    )
    qkv_shards = [sum_over_z(total) for total in qkv_sums]

    def ends(up_shard):
        feed_out = home_sum(feed_home, feed_other)
        output_shard = (residual_one + feed_out + bias_down).astype(low)
        output_shard = output_shard.reshape(1, tok_count, model)
        up_bias_grad = jnp.where(
            (jnp.arange(4, dtype=jnp.int32) == si)[None, :, None],
            up_bias_part.reshape(shard_count, 1, ff_part),
            0.0,
        ).reshape(shard_count, ff_piece)
        vector_grad = jnp.concatenate(
            [
                part.reshape(shard_count, -1)
                for part in (
                    gain_one_grad,
                    shift_one_grad,
                    gain_two_grad,
                    shift_two_grad,
                    down_bias_part,
                    up_bias_grad,
                )
            ],
            axis=1,
        )
        for name in ("c", "y"):
            vector_grad = vector_grad + lax.ppermute(vector_grad, name, SWAP)
        up_shard = after(up_shard, vector_grad)
        vector_grad = vector_grad.reshape(z_count, 2, -1)
        away = lax.dynamic_index_in_dim(vector_grad, 1 - xi, 1, keepdims=False)
        home = lax.dynamic_index_in_dim(vector_grad, xi, 1, keepdims=False)
        vector_grad = home + lax.ppermute(away, "x", SWAP)
        up_other = lax.ppermute(up_shard, "y", SWAP)
        down_far = lax.ppermute(after(down_pair[1], vector_grad), "x", SWAP)
        down_shard = (down_pair[0].astype(wide) + down_far.astype(wide)).astype(low)
        down_other = lax.ppermute(after(down_shard, up_other), "y", SWAP)
        out_away = lax.ppermute(after(out_sum[:z_count], down_far), "x", SWAP)
        out_both = (out_sum[z_count:].astype(wide) + out_away.astype(wide)).astype(low)
        vector_total = sum_small(vector_grad)
        up_pieces = core_pieces(up_shard, up_other)
        return (
            output_shard,
            vector_total,
            out_both,
            widen_rows(core_pieces(down_shard, down_other), places),
            widen_columns(up_pieces, places, shard_count),
        )

    output_shard, vector_total, out_both, down_total, up_total = line.leave(
        *stage(flag, ends, line.enter(up_shard))
    )

    out_shard = sum_over_z(after(out_both, *qkv_shards))

    def last(qkv_low, qkv_high):
        return widen_heads([seq_pieces(qkv_low), seq_pieces(qkv_high)], places)

    qkv_total = stage(flag, last, after(qkv_shards[0], up_total), qkv_shards[1])
    out_total = widen_quarters(seq_pieces(after(out_shard, qkv_total)), places)
    vectors = [vector_total[slot * piece_d : (slot + 1) * piece_d] for slot in range(5)]
    return (
        output_shard,
        input_grad,
        vectors[0],
        vectors[1],
        qkv_total,
        out_total,
        vectors[2],
        vectors[3],
        up_total,
        vector_total[5 * piece_d :],
        down_total,
        vectors[4],
    )


def solution(mesh):
    shard_count, seq_count = mesh.shape["fsdp"], mesh.shape["seq"]

    def step(*args):
        model, hidden = args[0].shape[2], args[12].shape[0]
        rows_each = args[0].shape[0] // shard_count
        if (
            rows_each == 1
            and seq_count == 4
            and model // shard_count == 2 * HD
            and hidden // (4 * shard_count) % 256 == 0
        ):
            fsdp, seq = ("z", "x"), ("y", "c")
            devices = mesh.devices.reshape(shard_count // 2, 2, 2, 2)
            inner, body = Mesh(devices, fsdp + seq), split_shards
        else:
            fsdp, seq = "fsdp", "seq"
            inner, body = mesh, plain_shards
        rows, tokens = P(fsdp, None), P(fsdp, seq, None)
        vector = P(fsdp)
        placed = (tokens, tokens, rows, rows, rows, vector, vector, rows, rows)
        placed += (vector, vector, rows, vector, rows, vector)
        given = (tokens, tokens, vector, vector, rows, rows, vector, vector)
        given += (rows, vector, rows, vector)
        return jax.shard_map(
            body, mesh=inner, in_specs=placed, out_specs=given, check_vma=False
        )(*args)

    return step
```

```python
import functools

import jax
import jax.numpy as jnp
import numpy as np
from jax import lax
from jax.experimental import pallas as pl
from jax.experimental.pallas import tpu as pltpu
from jax.sharding import Mesh
from jax.sharding import PartitionSpec as P

H = 16
HD = 128


EPSILON = 1e-05
MASKED = -1e30
SWAP = ((0, 1), (1, 0))
VMEM_LIMIT = 56 << 20
GELU_A = float(np.sqrt(2.0 / np.pi))
GELU_B = 0.044715


def layer_norm(values, gain_vec, shift_vec):
    center = values - jnp.mean(values, axis=-1, keepdims=True)
    spread = jnp.mean(center * center, axis=-1, keepdims=True)
    return center * lax.rsqrt(spread + EPSILON) * gain_vec + shift_vec


def contract_rows(left, right):
    return lax.dot_general(
        left, right, (((0,), (0,)), ((), ())), preferred_element_type=jnp.float32
    )


def times_transpose(left, right):
    return lax.dot_general(
        left, right, (((1,), (1,)), ((), ())), preferred_element_type=jnp.float32
    )


def item_numbers(starts, lengths, positions):
    inside = (positions[None, :] >= starts[:, None]) & (
        positions[None, :] < (starts + lengths)[:, None]
    )
    labels = jnp.arange(1, starts.shape[0] + 1, dtype=jnp.int32)
    return jnp.sum(jnp.where(inside, labels[:, None], 0), axis=0) - 1


def visible_mask(query_pos, key_pos, query_item, key_item, key_pad):
    same_item = (query_item[:, None] == key_item[None, :]) & (query_item[:, None] >= 0)
    before = key_pos[None, :] < query_pos[:, None]
    return same_item & before & (key_pad[None, :] == 1) | (key_pos[None, :] == query_pos[:, None])


def masked_scores(query_rows, key_rows, visible, score_scale):
    scores = (
        jnp.einsum("qhd,khd->hqk", query_rows, key_rows, preferred_element_type=jnp.float32)
        * score_scale
    )
    return jnp.where(visible[None], scores, MASKED)


def attend_rows(query_rows, key_rows, value_rows, visible, score_scale):
    scores = masked_scores(query_rows, key_rows, visible, score_scale)
    row_peak = jnp.max(scores, axis=-1, keepdims=True)
    exp_scores = jnp.exp(scores - row_peak)
    row_total = jnp.sum(exp_scores, axis=-1, keepdims=True)
    attn_probs = exp_scores / row_total
    mixed_rows = jnp.einsum(
        "hqk,khd->qhd",
        attn_probs.astype(jnp.bfloat16),
        value_rows,
        preferred_element_type=jnp.float32,
    )
    return (mixed_rows, row_peak + jnp.log(row_total))


def attend_back(query_rows, key_rows, value_rows, visible, log_total, mixed_grad, score_scale):
    scores = masked_scores(query_rows, key_rows, visible, score_scale)
    attn_probs = jnp.exp(scores - log_total)
    prob_grad = jnp.einsum(
        "qhd,khd->hqk", mixed_grad, value_rows, preferred_element_type=jnp.float32
    )
    value_part = jnp.einsum(
        "hqk,qhd->khd",
        attn_probs.astype(jnp.bfloat16),
        mixed_grad,
        preferred_element_type=jnp.float32,
    )
    inner_sum = jnp.sum(prob_grad * attn_probs, axis=-1, keepdims=True)
    score_grad = (attn_probs * (prob_grad - inner_sum)).astype(jnp.bfloat16)
    query_grad = (
        jnp.einsum("hqk,khd->qhd", score_grad, key_rows, preferred_element_type=jnp.float32)
        * score_scale
    )
    key_part = (
        jnp.einsum("hqk,qhd->khd", score_grad, query_rows, preferred_element_type=jnp.float32)
        * score_scale
    )
    return (query_grad.astype(jnp.bfloat16), key_part, value_part)


def plain_shards(
    block_input,
    cotangent,
    item_starts,
    item_lengths,
    pad_mask,
    ln1_gain,
    ln1_shift,
    w_qkv,
    w_out,
    ln2_gain,
    ln2_shift,
    w_up,
    up_bias,
    w_down,
    down_bias,
):
    rows_here, tok_count, model_width = block_input.shape
    seq_count = lax.axis_size("seq")
    shard_count = lax.axis_size("fsdp")
    length = tok_count * seq_count
    score_scale = HD ** (-0.5)
    piece_d = ln1_gain.shape[0]
    seq_first = lax.axis_index("seq") * tok_count
    packed = jnp.concatenate([ln1_gain, ln1_shift, ln2_gain, ln2_shift, down_bias, up_bias])
    vector_table = lax.all_gather(packed, "fsdp", axis=0, tiled=True).reshape(shard_count, -1)

    def vector_part(slot):
        return vector_table[:, slot * piece_d : (slot + 1) * piece_d].reshape(-1)

    gain_one, shift_one, gain_two, shift_two, bias_down = [vector_part(slot) for slot in range(5)]
    bias_up = vector_table[:, 5 * piece_d :].reshape(-1)
    qkv_full, out_full = (
        lax.all_gather(w_qkv, "fsdp", axis=0, tiled=True),
        lax.all_gather(w_out, "fsdp", axis=0, tiled=True),
    )
    inputs = block_input.reshape(rows_here * tok_count, model_width).astype(jnp.float32)
    normed_one = layer_norm(inputs, gain_one, shift_one).astype(jnp.bfloat16)
    projected = jnp.dot(normed_one, qkv_full, preferred_element_type=jnp.float32).astype(
        jnp.bfloat16
    )
    query_all = projected[:, :model_width].reshape(rows_here, tok_count, H, HD)
    kv_local = projected[:, model_width:].reshape(rows_here, tok_count, 2 * model_width)
    kv_whole = lax.all_gather(kv_local, "seq", axis=1, tiled=True)
    key_all = kv_whole[:, :, :model_width].reshape(rows_here, length, H, HD)
    value_all = kv_whole[:, :, model_width:].reshape(rows_here, length, H, HD)
    positions = jnp.arange(length, dtype=jnp.int32)
    query_pos = seq_first + jnp.arange(tok_count, dtype=jnp.int32)
    row_index = 0
    item_label = item_numbers(item_starts[row_index], item_lengths[row_index], positions)
    query_item = lax.dynamic_slice_in_dim(item_label, seq_first, tok_count)
    visible = visible_mask(query_pos, positions, query_item, item_label, pad_mask[row_index])
    mixed_part, log_total = attend_rows(
        query_all[row_index], key_all[row_index], value_all[row_index], visible, score_scale
    )
    visible_list = [visible]
    mixed_list = [mixed_part]
    logsum_list = [log_total]
    mixed_all = (
        jnp.stack(mixed_list).reshape(rows_here * tok_count, model_width).astype(jnp.bfloat16)
    )
    residual_one = inputs + jnp.dot(mixed_all, out_full, preferred_element_type=jnp.float32)
    up_full, down_full = (
        lax.all_gather(w_up, "fsdp", axis=0, tiled=True),
        lax.all_gather(w_down, "fsdp", axis=0, tiled=True),
    )
    normed_two = layer_norm(residual_one, gain_two, shift_two).astype(jnp.bfloat16)
    hidden_pre = jnp.dot(normed_two, up_full, preferred_element_type=jnp.float32) + bias_up
    activated = jax.nn.gelu(hidden_pre).astype(jnp.bfloat16)
    block_output = (
        residual_one + jnp.dot(activated, down_full, preferred_element_type=jnp.float32) + bias_down
    )
    output_shard = block_output.astype(jnp.bfloat16).reshape(rows_here, tok_count, model_width)
    up_full, down_full = (
        lax.all_gather(w_up, "fsdp", axis=0, tiled=True),
        lax.all_gather(w_down, "fsdp", axis=0, tiled=True),
    )
    cot_flat = cotangent.reshape(rows_here * tok_count, model_width)
    cot_wide = cot_flat.astype(jnp.float32)
    down_grad = contract_rows(activated, cot_flat)
    down_bias_part = jnp.sum(cot_wide, axis=0)
    act_grad = times_transpose(cot_flat, down_full)
    gelu_back = jax.vjp(jax.nn.gelu, hidden_pre)[1]
    hidden_grad = gelu_back(act_grad)[0].astype(jnp.bfloat16)
    up_grad = contract_rows(normed_two, hidden_grad)
    up_bias_part = jnp.sum(hidden_grad.astype(jnp.float32), axis=0)
    norm_two_grad = times_transpose(hidden_grad, up_full)
    norm_two_back = jax.vjp(layer_norm, residual_one, gain_two, shift_two)[1]
    resid_part, gain_two_grad, shift_two_grad = norm_two_back(norm_two_grad)
    residual_grad = cot_wide + resid_part
    up_sum, down_sum = (
        lax.psum_scatter(up_grad, "fsdp", scatter_dimension=0, tiled=True),
        lax.psum_scatter(down_grad, "fsdp", scatter_dimension=0, tiled=True),
    )
    qkv_full, out_full = (
        lax.all_gather(w_qkv, "fsdp", axis=0, tiled=True),
        lax.all_gather(w_out, "fsdp", axis=0, tiled=True),
    )
    branch_grad = residual_grad.astype(jnp.bfloat16)
    out_grad = contract_rows(mixed_all, branch_grad)
    mixed_grad = (
        times_transpose(branch_grad, out_full)
        .astype(jnp.bfloat16)
        .reshape(rows_here, tok_count, H, HD)
    )
    row_index = 0
    query_grad, key_part, value_part = attend_back(
        query_all[row_index],
        key_all[row_index],
        value_all[row_index],
        visible_list[row_index],
        logsum_list[row_index],
        mixed_grad[row_index],
        score_scale,
    )
    query_list = [query_grad.reshape(tok_count, model_width)]
    kv_list = [
        jnp.concatenate(
            [key_part.reshape(length, model_width), value_part.reshape(length, model_width)], axis=1
        )
    ]
    kv_terms = jnp.stack(kv_list)
    kv_grad = lax.psum_scatter(kv_terms, "seq", scatter_dimension=1, tiled=True).astype(
        jnp.bfloat16
    )
    proj_grad = jnp.concatenate(
        [
            jnp.stack(query_list).reshape(rows_here * tok_count, model_width),
            kv_grad.reshape(rows_here * tok_count, 2 * model_width),
        ],
        axis=1,
    )
    qkv_grad = contract_rows(normed_one, proj_grad)
    norm_one_grad = times_transpose(proj_grad, qkv_full)
    norm_one_back = jax.vjp(layer_norm, inputs, gain_one, shift_one)[1]
    input_part, gain_one_grad, shift_one_grad = norm_one_back(norm_one_grad)
    input_grad = (residual_grad + input_part).reshape(rows_here, tok_count, model_width)
    vector_grad = jnp.concatenate(
        [
            piece_grad.reshape(shard_count, -1)
            for piece_grad in (
                gain_one_grad,
                shift_one_grad,
                gain_two_grad,
                shift_two_grad,
                down_bias_part,
                up_bias_part,
            )
        ],
        axis=1,
    ).reshape(-1)
    qkv_sum, out_sum, vector_sum = (
        lax.psum_scatter(qkv_grad, "fsdp", scatter_dimension=0, tiled=True),
        lax.psum_scatter(out_grad, "fsdp", scatter_dimension=0, tiled=True),
        lax.psum_scatter(vector_grad, "fsdp", scatter_dimension=0, tiled=True),
    )
    up_total, down_total, qkv_total, out_total, vector_total = lax.psum(
        (up_sum, down_sum, qkv_sum, out_sum, vector_sum), "seq"
    )
    gain_one_out = vector_total[0:piece_d]
    shift_one_out = vector_total[piece_d : 2 * piece_d]
    gain_two_out = vector_total[2 * piece_d : 3 * piece_d]
    shift_two_out = vector_total[3 * piece_d : 4 * piece_d]
    down_bias_out = vector_total[4 * piece_d : 5 * piece_d]
    up_bias_out = vector_total[5 * piece_d :]
    return (
        output_shard,
        input_grad,
        gain_one_out,
        shift_one_out,
        qkv_total,
        out_total,
        gain_two_out,
        shift_two_out,
        up_total,
        up_bias_out,
        down_total,
        down_bias_out,
    )


def gather_small(vector, z_count):
    line = [vector]
    for j in range(1, z_count):
        line.append(lax.ppermute(vector, "z", [(i, (i + j) % z_count) for i in range(z_count)]))
    return line + [lax.ppermute(piece, "x", SWAP) for piece in line]


def gather_weight(shard, *others):
    near = lax.all_gather(shard, "z", axis=0, tiled=False)
    return [near, lax.ppermute(after(near, *others), "x", SWAP)]


def stage(flag, work, *args):
    shapes = jax.eval_shape(work, *args)

    def nothing(*_):
        return jax.tree.map(lambda a: jnp.zeros(a.shape, a.dtype), shapes)

    return lax.cond(flag, work, nothing, *args)


class Line:
    def __init__(self):
        self.last = ()

    def enter(self, value):
        return after(value, *self.last)

    def leave(self, *results):
        self.last = results[:1]
        return results


def after(value, *others):
    return lax.optimization_barrier((value,) + others)[0]


def seq_pieces(block, *others):
    return core_pieces(block, after(lax.ppermute(block, "y", SWAP), *others))


def core_pieces(block, other):
    return [block, lax.ppermute(block, "c", SWAP), other, lax.ppermute(other, "c", SWAP)]


def by_bit(bit, mine, theirs):
    return jnp.where(bit == 0, mine, theirs), jnp.where(bit == 0, theirs, mine)


def gather_tokens(block, yi, ci, *others):
    parts = seq_pieces(block, *others)
    near = by_bit(ci, parts[0], parts[1])
    far = by_bit(ci, parts[2], parts[3])
    rows = [jnp.where(yi == 0, n, f) for n, f in zip(near, far)]
    rows += [jnp.where(yi == 0, f, n) for n, f in zip(near, far)]
    return jnp.concatenate(rows, axis=0)


def core_sum(parts, yi):
    away, home = parts
    other = lax.ppermute(away, "c", SWAP)
    tokens, model = home.shape[0] // 2, home.shape[1]
    steps = 4
    block = (tokens // steps, model)

    def kernel(at_ref, *refs):
        wide = jnp.float32
        refs[4][...] = refs[0][...].astype(wide) + refs[1][...].astype(wide)
        refs[5][...] = (refs[2][...].astype(wide) + refs[3][...].astype(wide)).astype(
            jnp.bfloat16
        )

    here = pl.BlockSpec(block, lambda i, at: (at[0] * steps + i, 0))
    there = pl.BlockSpec(block, lambda i, at: ((1 - at[0]) * steps + i, 0))
    out = pl.BlockSpec(block, lambda i, at: (i, 0))
    return pl.pallas_call(
        kernel,
        grid_spec=pltpu.PrefetchScalarGridSpec(
            num_scalar_prefetch=1,
            grid=(steps,),
            in_specs=[here, here, there, there],
            out_specs=[out, out],
        ),
        out_shape=[
            jax.ShapeDtypeStruct((tokens, model), jnp.float32),
            jax.ShapeDtypeStruct((tokens, model), jnp.bfloat16),
        ],
        cost_estimate=cost(flops=0, bytes_accessed=7 * tokens * model, transcendentals=0),
        compiler_params=params(),
    )(jnp.reshape(yi, (1,)).astype(jnp.int32), home, other, home, other)


def home_sum(home, other):
    return home + other.astype(jnp.float32)


COST_SCALE = 0.01


def cost(flops, bytes_accessed, transcendentals):
    return pl.CostEstimate(
        flops=int(flops * COST_SCALE),
        bytes_accessed=int(bytes_accessed * COST_SCALE),
        transcendentals=int(transcendentals * COST_SCALE),
    )


def params(limit=VMEM_LIMIT):
    return pltpu.CompilerParams(vmem_limit_bytes=limit)


def weight_matmul(left, pieces, offsets, shape, back, body, extras, outs, chunk, groups=None):
    rows = left.shape[0]
    depth, width = shape
    out_width = depth if back else width
    steps = out_width // chunk
    n_pieces, n_extras = len(pieces), len(extras)
    blocks = [(p, k) for p, piece in enumerate(pieces) for k in range(piece.shape[0])]
    block_rows, block_cols = pieces[0].shape[1:]
    row_count, col_count = depth // block_rows, width // block_cols

    tables = (offsets,) if groups is None else (offsets, groups)

    def kernel(*refs):
        table_refs, left_ref, refs = refs[: len(tables)], refs[len(tables)], refs[len(tables) + 1 :]
        offs_ref = table_refs[0]
        piece_refs = refs[:n_pieces]
        extra_refs = refs[n_pieces : n_pieces + n_extras]
        out_refs = refs[n_pieces + n_extras : -2]
        held, sems = refs[-2:]
        step = pl.program_id(0)

        def slot(row, col):
            return sems.at[row, col]

        @pl.when(step == 0)
        def _():
            for b, (p, k) in enumerate(blocks):
                row, col = offs_ref[0, b], offs_ref[1, b]
                target = held.at[
                    pl.ds(pl.multiple_of(row * block_rows, block_rows), block_rows),
                    pl.ds(pl.multiple_of(col * block_cols, block_cols), block_cols),
                ]
                pltpu.make_async_copy(piece_refs[p].at[k], target, slot(row, col)).start()

        def arrive(row, col):
            target = held.at[
                pl.ds(row * block_rows, block_rows), pl.ds(col * block_cols, block_cols)
            ]
            pltpu.make_async_copy(piece_refs[0].at[0], target, slot(row, col)).wait()

        for n in range(steps):
            needed = [
                (row, col)
                for row in range(row_count)
                for col in range(col_count)
                if (
                    row * block_rows // chunk if back else col * block_cols // chunk
                ) == n
            ]
            if needed:

                @pl.when(step == n)
                def _():
                    for row, col in needed:
                        arrive(row, col)

        start = pl.ds(pl.multiple_of(step * chunk, chunk), chunk)

        def product(part):
            if back:
                return lax.dot_general(
                    part,
                    held[start, :],
                    (((1,), (1,)), ((), ())),
                    preferred_element_type=jnp.float32,
                )
            return jnp.dot(part, held[:, start], preferred_element_type=jnp.float32)

        if groups is None:
            body(product(left_ref[...]), extra_refs, out_refs)
        else:
            size = rows // groups.shape[0]
            each = out_refs[0].shape[0] // size
            for g in range(groups.shape[0]):
                at = pl.multiple_of(table_refs[1][g] * size, size)
                values = product(left_ref[pl.ds(at, size), :])
                to = (g % each) * size
                out_refs[g // each][to : to + size, :] = values.astype(jnp.bfloat16)

    def column_spec(array):
        return pl.BlockSpec((array.shape[0], chunk), lambda i, *tabs: (0, i))

    flops = 2 * rows * depth * width
    moved = 2 * (left.size + depth * width) + sum(
        a.size * a.dtype.itemsize for a in list(extras) + list(outs)
    )
    return pl.pallas_call(
        kernel,
        grid_spec=pltpu.PrefetchScalarGridSpec(
            num_scalar_prefetch=len(tables),
            grid=(steps,),
            in_specs=[
                pl.BlockSpec(
                    left.shape, lambda i, *tabs: (0, 0), pipeline_mode=pl.Buffered(1)
                )
            ]
            + [pl.BlockSpec(memory_space=pl.ANY)] * n_pieces
            + [column_spec(a) for a in extras],
            out_specs=[column_spec(a) for a in outs],
            scratch_shapes=[
                pltpu.VMEM((depth, width), jnp.bfloat16),
                pltpu.SemaphoreType.DMA((row_count, col_count)),
            ],
        ),
        out_shape=list(outs),
        cost_estimate=cost(flops=flops, bytes_accessed=moved, transcendentals=0),
        compiler_params=params(),
    )(*tables, left, *pieces, *extras)


def store_low(values, extra_refs, out_refs):
    out_refs[0][...] = values.astype(jnp.bfloat16)


def store_gelu(values, extra_refs, out_refs):
    hidden = values + extra_refs[0][...]
    square = hidden * hidden
    bend = jnp.tanh(GELU_A * hidden * (1.0 + GELU_B * square))
    half = 0.5 * (1.0 + bend)
    out_refs[0][...] = (hidden * half).astype(jnp.bfloat16)
    slope = half + 0.5 * hidden * (1.0 - bend * bend) * (
        GELU_A * (1.0 + 3.0 * GELU_B * square)
    )
    out_refs[1][...] = slope


def store_hidden_grad(values, extra_refs, out_refs):
    low = (values * extra_refs[0][...]).astype(jnp.bfloat16)
    out_refs[0][...] = low
    out_refs[1][...] = jnp.sum(low.astype(jnp.float32), axis=0, keepdims=True)


def weight_grad(left, right, where, count, block, width, addend=None, parts=1):
    rows = left.shape[0]
    part = width // parts
    added = () if addend is None else (addend,)

    def kernel(where_ref, left_ref, right_ref, *refs):
        for n in range(parts):
            cols = slice(n * part, (n + 1) * part)
            value = lax.dot_general(
                left_ref[...],
                right_ref[:, cols],
                (((0,), (0,)), ((), ())),
                preferred_element_type=jnp.float32,
            )
            if added:
                value = value + refs[0][0, :, cols].astype(jnp.float32)
            refs[len(added) + n][0] = value.astype(jnp.bfloat16)

    return pl.pallas_call(
        kernel,
        grid_spec=pltpu.PrefetchScalarGridSpec(
            num_scalar_prefetch=1,
            grid=(count,),
            in_specs=[
                pl.BlockSpec((rows, block), lambda k, at: (0, at[k])),
                pl.BlockSpec((rows, width), lambda k, at: (0, at[count])),
            ]
            + [pl.BlockSpec((1, block, width), lambda k, at: (k, 0, 0))] * len(added),
            out_specs=[pl.BlockSpec((1, block, part), lambda k, at: (k, 0, 0))] * parts,
        ),
        out_shape=[jax.ShapeDtypeStruct((count, block, part), jnp.bfloat16)] * parts,
        cost_estimate=cost(
            flops=2 * rows * count * block * width,
            bytes_accessed=2 * rows * (count * block + width) + 4 * count * block * width,
            transcendentals=0,
        ),
        compiler_params=params(),
    )(where, left, right, *added)


def slice_qkv(w_qkv, where, width):
    rows = w_qkv.shape[0]
    heads = H // 4

    def kernel(at_ref, from_ref, to_ref):
        for i in range(heads):
            col = pl.ds(pl.multiple_of((2 * i + at_ref[1]) * HD, HD), HD)
            to_ref[:, i * HD : (i + 1) * HD] = from_ref[:, col]

    part = heads * HD
    return pl.pallas_call(
        kernel,
        grid_spec=pltpu.PrefetchScalarGridSpec(
            num_scalar_prefetch=1,
            grid=(3,),
            in_specs=[pl.BlockSpec((rows, 2 * part), lambda g, at: (0, 2 * g + at[0]))],
            out_specs=pl.BlockSpec((rows, part), lambda g, at: (0, g)),
        ),
        out_shape=jax.ShapeDtypeStruct((rows, width), jnp.bfloat16),
        cost_estimate=cost(flops=0, bytes_accessed=3 << 20, transcendentals=0),
        compiler_params=params(),
    )(where, w_qkv)


def slice_weights(w_out, w_up, w_down, where, shard_count):
    rows, model = w_out.shape
    ff_part = w_down.shape[0] // 4
    steps = shard_count
    part = ff_part // steps
    up_half = steps // 2

    def kernel(at_ref, out_ref, up_ref, down_ref, out_to, low_to, high_to, left_to, right_to):
        step = pl.program_id(0)
        for n, up_to in enumerate((low_to, high_to)):

            @pl.when(step // up_half == n)
            def _():
                up_to[...] = up_ref[...]

        @pl.when(step == 0)
        def _():
            out_to[...] = out_ref[...]

        left_to[...] = down_ref[:, : model // 2]
        right_to[...] = down_ref[:, model // 2 :]

    def up_spec(n):
        return pl.BlockSpec(
            (rows, ff_part), lambda i, at: (0, jnp.clip(i - n * up_half, 0, up_half - 1))
        )

    return pl.pallas_call(
        kernel,
        grid_spec=pltpu.PrefetchScalarGridSpec(
            num_scalar_prefetch=1,
            grid=(steps,),
            in_specs=[
                pl.BlockSpec((rows // 2, model // 2), lambda i, at: (at[1], at[0])),
                pl.BlockSpec((rows, ff_part), lambda i, at: (0, 4 * i + 2 * at[0] + at[1])),
                pl.BlockSpec(
                    (part, model), lambda i, at: ((2 * at[0] + at[1]) * steps + i, 0)
                ),
            ],
            out_specs=[
                pl.BlockSpec((rows // 2, model // 2), lambda i, at: (0, 0)),
                up_spec(0),
                up_spec(1),
                pl.BlockSpec((part, model // 2), lambda i, at: (i, 0)),
                pl.BlockSpec((part, model // 2), lambda i, at: (i, 0)),
            ],
        ),
        out_shape=[
            jax.ShapeDtypeStruct(shape, jnp.bfloat16)
            for shape in [(rows // 2, model // 2)]
            + [(rows, ff_part * up_half)] * 2
            + [(ff_part, model // 2)] * 2
        ],
        cost_estimate=cost(flops=0, bytes_accessed=9 << 20, transcendentals=0),
        compiler_params=params(),
    )(where, w_out, w_up, w_down)


def visible_tile(query_item, key_item, first_query, n_query, n_key):
    query_pos = first_query + lax.broadcasted_iota(jnp.int32, (n_query, n_key), 0)
    key_pos = lax.broadcasted_iota(jnp.int32, (n_query, n_key), 1)
    return ((query_item == key_item) & (key_pos < query_pos)) | (key_pos == query_pos)


def head_spec(length, first):
    return pl.BlockSpec((length, HD), lambda h: (0, first + h))


def attention(projected, query_item, key_item, heads, tile):
    length = projected.shape[0]
    scale = HD ** (-0.5)

    def kernel(q_ref, k_ref, v_ref, qi_ref, ki_ref, mixed_ref, log_ref):
        for start in range(0, length, tile):
            stop = start + tile
            rows = slice(start, stop)
            scores = (
                lax.dot_general(
                    q_ref[rows, :],
                    k_ref[:stop, :],
                    (((1,), (1,)), ((), ())),
                    preferred_element_type=jnp.float32,
                )
                * scale
            )
            seen = visible_tile(qi_ref[rows, :], ki_ref[:, :stop], start, tile, stop)
            scores = jnp.where(seen, scores, MASKED)
            peak = jnp.max(scores, axis=-1, keepdims=True)
            weights = jnp.exp(scores - peak)
            total = jnp.sum(weights, axis=-1, keepdims=True)
            probs = (weights * (1.0 / total)).astype(jnp.bfloat16)
            mixed_ref[rows, :] = jnp.dot(
                probs, v_ref[:stop, :], preferred_element_type=jnp.float32
            ).astype(jnp.bfloat16)
            log_ref[0, rows, :] = peak + jnp.log(total)

    whole = lambda rows, cols: pl.BlockSpec((rows, cols), lambda h: (0, 0))
    return pl.pallas_call(
        kernel,
        grid=(heads,),
        in_specs=[head_spec(length, g * heads) for g in range(3)]
        + [whole(length, 1), whole(1, length)],
        out_specs=[head_spec(length, 0), pl.BlockSpec((1, length, 1), lambda h: (h, 0, 0))],
        out_shape=[
            jax.ShapeDtypeStruct((length, heads * HD), jnp.bfloat16),
            jax.ShapeDtypeStruct((heads, length, 1), jnp.float32),
        ],
        cost_estimate=cost(
            flops=4 * heads * length * length * HD,
            bytes_accessed=8 * length * heads * HD,
            transcendentals=heads * length * length,
        ),
        compiler_params=params(),
    )(projected, projected, projected, query_item, key_item)


def attention_back(projected, mixed_grad, log_total, query_item, key_item, heads, tile):
    length = projected.shape[0]
    scale = HD ** (-0.5)

    def kernel(q_ref, k_ref, v_ref, g_ref, log_ref, qi_ref, ki_ref, grad_ref, dk_ref, dv_ref):
        head = pl.program_id(0)

        def place(group):
            return pl.ds(pl.multiple_of((group * heads + head) * HD, HD), HD)

        for start in reversed(range(0, length, tile)):
            stop = start + tile
            rows = slice(start, stop)
            query, grad = q_ref[rows, :], g_ref[rows, :]
            key, value = k_ref[:stop, :], v_ref[:stop, :]
            scores = (
                lax.dot_general(
                    query, key, (((1,), (1,)), ((), ())), preferred_element_type=jnp.float32
                )
                * scale
            )
            seen = visible_tile(qi_ref[rows, :], ki_ref[:, :stop], start, tile, stop)
            probs = jnp.exp(jnp.where(seen, scores, MASKED) - log_ref[0, rows, :])
            prob_grad = lax.dot_general(
                grad, value, (((1,), (1,)), ((), ())), preferred_element_type=jnp.float32
            )
            inner = jnp.sum(prob_grad * probs, axis=-1, keepdims=True)
            score_grad = (probs * (prob_grad - inner)).astype(jnp.bfloat16)
            grad_ref[rows, place(0)] = (
                jnp.dot(score_grad, key, preferred_element_type=jnp.float32) * scale
            ).astype(jnp.bfloat16)
            key_part = lax.dot_general(
                score_grad, query, (((0,), (0,)), ((), ())), preferred_element_type=jnp.float32
            )
            value_part = lax.dot_general(
                probs.astype(jnp.bfloat16),
                grad,
                (((0,), (0,)), ((), ())),
                preferred_element_type=jnp.float32,
            )
            if stop == length:
                dk_ref[...] = key_part
                dv_ref[...] = value_part
            else:
                dk_ref[:stop, :] += key_part
                dv_ref[:stop, :] += value_part
        grad_ref[:, place(1)] = (dk_ref[...] * scale).astype(jnp.bfloat16)
        grad_ref[:, place(2)] = dv_ref[...].astype(jnp.bfloat16)

    whole = lambda rows, cols: pl.BlockSpec((rows, cols), lambda h: (0, 0))
    return pl.pallas_call(
        kernel,
        grid=(heads,),
        in_specs=[head_spec(length, g * heads) for g in range(3)]
        + [
            head_spec(length, 0),
            pl.BlockSpec((1, length, 1), lambda h: (h, 0, 0)),
            whole(length, 1),
            whole(1, length),
        ],
        out_specs=whole(length, 3 * heads * HD),
        out_shape=jax.ShapeDtypeStruct((length, 3 * heads * HD), jnp.bfloat16),
        scratch_shapes=[pltpu.VMEM((length, HD), jnp.float32)] * 2,
        cost_estimate=cost(
            flops=10 * heads * length * length * HD,
            bytes_accessed=16 * length * heads * HD,
            transcendentals=heads * length * length,
        ),
        compiler_params=params(),
    )(projected, projected, projected, mixed_grad, log_total, query_item, key_item)


def widen(chunks, places, grid, piece_specs, out_block, out_index, out_shape, write):
    def kernel(place_ref, *refs):
        for n in range(len(chunks)):
            for r in range(4):
                write(n, place_ref[r], refs[4 * n + r], refs[-1])

    return pl.pallas_call(
        kernel,
        grid_spec=pltpu.PrefetchScalarGridSpec(
            num_scalar_prefetch=1,
            grid=(grid,),
            in_specs=[
                pl.BlockSpec(block, functools.partial(lambda at, i, pos: at(i), at))
                for block, at in piece_specs
                for _ in range(4)
            ],
            out_specs=pl.BlockSpec(out_block, lambda i, pos: out_index(i)),
        ),
        out_shape=jax.ShapeDtypeStruct(out_shape, jnp.float32),
        cost_estimate=cost(
            flops=0, bytes_accessed=6 * int(np.prod(out_shape)), transcendentals=0
        ),
        compiler_params=params(),
    )(places, *[piece for pieces in chunks for piece in pieces])


def widen_columns(pieces, places, blocks):
    rows, width = pieces[0].shape
    part = width // blocks

    def write(n, pos, piece, out):
        out[:, pl.ds(pl.multiple_of(pos * part, part), part)] = piece[...].astype(jnp.float32)

    return widen(
        [pieces],
        places,
        blocks,
        [((rows, part), lambda i: (0, i))],
        (rows, 4 * part),
        lambda i: (0, i),
        (rows, 4 * width),
        write,
    )


def widen_rows(pieces, places):
    rows, width = pieces[0].shape

    def write(n, pos, piece, out):
        @pl.when(pos == pl.program_id(0))
        def _():
            out[...] = piece[...].astype(jnp.float32)

    return widen(
        [pieces],
        places,
        4,
        [((rows, width), lambda i: (0, 0))],
        (rows, width),
        lambda i: (i, 0),
        (4 * rows, width),
        write,
    )


def widen_heads(pieces, places):
    rows, width = pieces[0].shape
    part = width // 3

    def write(n, pos, piece, out):
        first = lax.div(pos, 2) * part * 2 + lax.rem(pos, 2) * HD
        for i in range(part // HD):
            cols = pl.ds(pl.multiple_of(first + 2 * i * HD, HD), HD)
            out[:, cols] = piece[:, i * HD : (i + 1) * HD].astype(jnp.float32)

    return widen(
        [pieces],
        places,
        3,
        [((rows, part), lambda i: (0, i))],
        (rows, 4 * part),
        lambda i: (0, i),
        (rows, 4 * width),
        write,
    )


def widen_quarters(pieces, places):
    rows, width = pieces[0].shape

    def write(n, pos, piece, out):
        row = pl.multiple_of(lax.rem(pos, 2) * rows, rows)
        col = pl.multiple_of(lax.div(pos, 2) * width, width)
        out[pl.ds(row, rows), pl.ds(col, width)] = piece[...].astype(jnp.float32)

    return widen(
        [pieces],
        places,
        1,
        [((rows, width), lambda i: (0, 0))],
        (2 * rows, 2 * width),
        lambda i: (0, 0),
        (2 * rows, 2 * width),
        write,
    )


def norm_back(values, gain_vec, incoming):
    center = values - jnp.mean(values, axis=-1, keepdims=True)
    spread = jnp.mean(center * center, axis=-1, keepdims=True)
    inverse = lax.rsqrt(spread + EPSILON)
    unit = center * inverse
    scaled = incoming * gain_vec
    inner = jnp.mean(scaled * unit, axis=-1, keepdims=True)
    grad = (scaled - jnp.mean(scaled, axis=-1, keepdims=True) - unit * inner) * inverse
    return grad, jnp.sum(incoming * unit, axis=0), jnp.sum(incoming, axis=0)


def split_shards(
    block_input,
    cotangent,
    item_starts,
    item_lengths,
    pad_mask,
    ln1_gain,
    ln1_shift,
    w_qkv,
    w_out,
    ln2_gain,
    ln2_shift,
    w_up,
    up_bias,
    w_down,
    down_bias,
):
    low, wide = jnp.bfloat16, jnp.float32
    z_count = lax.axis_size("z")
    shard_count = 2 * z_count
    zi, xi, yi, ci = [lax.axis_index(name) for name in ("z", "x", "y", "c")]
    si = 2 * yi + ci
    tok_count, model = block_input.shape[1:]
    length = 4 * tok_count
    piece_d, ff_piece = ln1_gain.shape[0], up_bias.shape[0]
    ff_part = ff_piece // 4
    ff_here = ff_part * shard_count
    heads = H // 4
    places = jnp.stack([jnp.bitwise_xor(si, r) for r in range(4)]).astype(jnp.int32)

    packed = jnp.concatenate([ln1_gain, ln1_shift, ln2_gain, ln2_shift, down_bias, up_bias])
    vector_stack = jnp.stack(gather_small(packed, z_count))
    owners = jnp.stack(
        [
            lax.rem(zi - j + z_count, z_count) * 2 + jnp.bitwise_xor(xi, dx)
            for dx in range(2)
            for j in range(z_count)
        ]
    )
    hit = owners[None, :] == jnp.arange(shard_count, dtype=jnp.int32)[:, None]
    vector_table = jnp.sum(jnp.where(hit[:, :, None], vector_stack[None], 0.0), axis=1)

    def vector_part(slot):
        return vector_table[:, slot * piece_d : (slot + 1) * piece_d].reshape(-1)

    gain_one, shift_one, gain_two, shift_two, bias_down = [vector_part(slot) for slot in range(5)]
    bias_up = lax.dynamic_index_in_dim(
        vector_table[:, 5 * piece_d :].reshape(shard_count, 4, ff_part), si, 1, keepdims=False
    ).reshape(1, ff_here)

    line = Line()
    flag = item_lengths[0, 0] > 0
    where = jnp.stack([yi, ci]).astype(jnp.int32)
    qkv_slice = slice_qkv(w_qkv, where, 3 * heads * HD)
    slices = slice_weights(w_out, w_up, w_down, after(where, qkv_slice), shard_count)
    half = model // 2
    qkv_width = 3 * heads * HD
    qkv_parts = gather_weight(qkv_slice)
    down_pair = jnp.stack([slices[4], lax.ppermute(slices[4], "x", SWAP)])
    inputs = after(block_input, down_pair).reshape(tok_count, model).astype(wide)
    normed_one = layer_norm(inputs, gain_one, shift_one).astype(low)
    out_parts = gather_weight(after(slices[0], normed_one), qkv_parts[1])
    out_parts = out_parts + [lax.ppermute(piece, "y", SWAP) for piece in out_parts]

    near_blocks = [2 * z + xi for z in range(z_count)]
    far_blocks = [2 * z + 1 - xi for z in range(z_count)]
    split = near_blocks + far_blocks
    paired = [b for pair in zip(near_blocks, far_blocks) for b in pair]
    zero = jnp.zeros_like(xi)

    def table(*rows):
        return jnp.stack([jnp.stack(row) for row in rows]).astype(jnp.int32)

    qkv_offsets = table(split, [zero] * shard_count)
    up_offsets = table(split + split, [zero] * shard_count + [zero + 1] * shard_count)
    down_offsets = table(split + paired, [zero] * shard_count + [zero + 1] * shard_count)
    out_offsets = table(split + split, [yi] * shard_count + [1 - yi] * shard_count)

    def blocks_at(blocks, n):
        return table(blocks + [zero + n])[0]

    def sum_small(terms):
        def term(j):
            return lax.dynamic_index_in_dim(
                terms, lax.rem(zi - j + z_count, z_count), 0, keepdims=False
            )

        total = term(0).astype(wide)
        for j in range(1, z_count):
            total = total + lax.ppermute(
                term(j), "z", [(i, (i - j) % z_count) for i in range(z_count)]
            ).astype(wide)
        return total

    def plain_matmul(left, pieces, offsets, shape, back, body, extras, outs):
        return weight_matmul(left, pieces, offsets, shape, back, body, extras, outs, 512)

    def row_groups(left, pieces, offsets, shape_, back):
        groups = jnp.stack([1 - ci, 3 - ci, ci, 2 + ci]).astype(jnp.int32)
        outs = (shape(2 * tok_count, shape_[0] if back else shape_[1]),) * 2
        return weight_matmul(left, pieces, offsets, shape_, back, None, (), outs, 512, groups)

    def matmul(left, *others):
        return line.leave(*plain_matmul(line.enter(left), *others))

    def grad_chunk(left, right, blocks, n, block, width):
        return line.leave(
            *weight_grad(line.enter(left), right, blocks_at(blocks, n), len(blocks), block, width)
        )[0]

    def far_terms(left, right, block):
        terms = grad_chunk(left, right, far_blocks, 0, block, right.shape[1])
        return lax.ppermute(terms, "x", SWAP)

    def near_terms(left, right, block, addend, parts=1):
        return weight_grad(
            left, right, blocks_at(near_blocks, 0), z_count, block, addend.shape[2], addend, parts
        )

    def sum_over_z(total):
        return lax.psum_scatter(total, "z", scatter_dimension=0, tiled=False)

    def shape(rows, cols, kind=low):
        return jax.ShapeDtypeStruct((rows, cols), kind)

    normed_one = gather_tokens(normed_one, yi, ci, qkv_parts[0])
    cot_flat = after(cotangent.reshape(tok_count, model), normed_one)
    cot_wide = cot_flat.astype(wide)
    cot_all = gather_tokens(cot_flat, yi, ci)
    (projected,) = matmul(
        after(normed_one, cot_all),
        qkv_parts,
        qkv_offsets,
        (model, qkv_width),
        False,
        store_low,
        (),
        (shape(length, qkv_width),),
    )
    up_parts = gather_weight(slices[1], projected)
    up_high = lax.all_gather(slices[2], "z", axis=0, tiled=False)
    down_parts = gather_weight(slices[3], projected)
    down_parts.append(lax.all_gather(down_pair, "z", axis=0, tiled=True))
    positions = jnp.arange(length, dtype=jnp.int32)
    item_label = item_numbers(item_starts[0], item_lengths[0], positions)
    query_item = item_label[:, None]
    key_item = jnp.where((item_label >= 0) & (pad_mask[0] == 1), item_label, -2)[None, :]
    mixed_heads, log_total = line.leave(
        *attention(line.enter(projected), query_item, key_item, heads, 256)
    )

    def attend_out(mixed_heads):
        halves = mixed_heads.reshape(2, 2 * tok_count, heads * HD)
        away = lax.dynamic_index_in_dim(halves, 1 - yi, 0, keepdims=False)
        mine = lax.dynamic_index_in_dim(halves, yi, 0, keepdims=False)
        other = lax.ppermute(away, "y", SWAP)
        mixed = jnp.concatenate(by_bit(yi, mine, other), axis=1)
        (out_partial,) = plain_matmul(
            mixed,
            out_parts,
            out_offsets,
            (half, model),
            False,
            store_low,
            (),
            (shape(2 * tok_count, model),),
        )
        halves = out_partial.reshape(2, tok_count, model)
        away = lax.dynamic_index_in_dim(halves, 1 - ci, 0, keepdims=False)
        home = lax.dynamic_index_in_dim(halves, ci, 0, keepdims=False)
        residual_one = (
            inputs + home.astype(wide) + lax.ppermute(away, "c", SWAP).astype(wide)
        )
        normed_two = layer_norm(residual_one, gain_two, shift_two).astype(low)
        return normed_two, residual_one, mine, other

    up_parts += [up_high, lax.ppermute(after(up_high, mixed_heads), "x", SWAP)]
    normed_two, residual_one, mixed_home, mixed_other = line.leave(
        *stage(flag, attend_out, after(line.enter(mixed_heads), up_parts[0], up_high))
    )
    normed_two = gather_tokens(normed_two, yi, ci, up_parts[1], up_parts[3])
    activated, slope = matmul(
        normed_two,
        up_parts,
        up_offsets,
        (model, ff_here),
        False,
        store_gelu,
        (bias_up,),
        (shape(length, ff_here), shape(length, ff_here, wide)),
    )

    mixed_last = lax.ppermute(after(mixed_home, activated), "y", SWAP)
    others_heads = jnp.concatenate(by_bit(yi, mixed_other, mixed_last), axis=0)
    mixed = jnp.concatenate(by_bit(yi, mixed_heads, others_heads), axis=1)

    down_bias_part = jnp.sum(cot_wide, axis=0)
    down_sum = grad_chunk(
        after(activated, down_parts[1], mixed), cot_all, paired, 0, ff_part, model
    )
    down_pair = lax.psum_scatter(
        down_sum.reshape(z_count, 2, ff_part, model), "z", scatter_dimension=0, tiled=False
    )
    hidden_grad, up_bias_part = matmul(
        cot_all,
        down_parts,
        down_offsets,
        (ff_here, model),
        True,
        store_hidden_grad,
        (slope,),
        (shape(length, ff_here), shape(1, ff_here, wide)),
    )
    up_far = far_terms(normed_two, hidden_grad, piece_d)
    norm_two_parts = line.leave(
        *row_groups(line.enter(hidden_grad), up_parts, up_offsets, (model, ff_here), True)
    )

    def norm_two_back(*norm_two_parts):
        home, away = core_sum(norm_two_parts, yi)
        other = lax.ppermute(away, "y", SWAP)
        feed_parts = row_groups(
            after(activated, away), down_parts, down_offsets, (ff_here, model), False
        )
        norm_two_grad = home_sum(home, after(other, *feed_parts))
        resid_part, gain_two_grad, shift_two_grad = norm_back(
            residual_one, gain_two, norm_two_grad
        )
        residual_grad = cot_wide + resid_part
        branch_grad = residual_grad.astype(low)
        branch_pair = jnp.concatenate(
            by_bit(ci, branch_grad, lax.ppermute(branch_grad, "c", SWAP)), axis=0
        )
        return branch_pair, residual_grad, gain_two_grad, shift_two_grad, feed_parts

    branch_pair, residual_grad, gain_two_grad, shift_two_grad, feed_parts = line.leave(
        *stage(flag, norm_two_back, line.enter(norm_two_parts[0]), norm_two_parts[1])
    )

    out_blocks = far_blocks + near_blocks

    def out_back(branch_pair):
        (mixed_grad_pair,) = plain_matmul(
            branch_pair,
            out_parts,
            out_offsets,
            (half, model),
            True,
            store_low,
            (),
            (shape(2 * tok_count, half),),
        )
        part = heads * HD
        away = lax.dynamic_slice_in_dim(mixed_grad_pair, (1 - yi) * part, part, 1)
        home = lax.dynamic_slice_in_dim(mixed_grad_pair, yi * part, part, 1)
        theirs = lax.ppermute(away, "y", SWAP)
        feed_home, feed_away = core_sum([after(feed_parts[0], away), feed_parts[1]], yi)
        theirs = after(theirs, feed_away)
        return jnp.concatenate(by_bit(yi, home, theirs), axis=0), feed_home, feed_away

    mixed_grad, feed_home, feed_away = line.leave(
        *stage(flag, out_back, line.enter(branch_pair))
    )
    away = lax.dynamic_slice_in_dim(branch_pair, (1 - yi) * half, half, 1)
    home = lax.dynamic_slice_in_dim(branch_pair, yi * half, half, 1)
    branch_other = lax.ppermute(after(away, mixed_grad), "y", SWAP)
    branch_all = jnp.concatenate(by_bit(yi, home, branch_other), axis=0)
    (proj_grad,) = line.leave(
        attention_back(
            projected,
            line.enter(mixed_grad),
            log_total,
            query_item,
            key_item,
            heads,
            256,
        )
    )
    qkv_far = far_terms(normed_one, proj_grad, piece_d)
    (up_sum,) = line.leave(
        near_terms(
            line.enter(after(normed_two, branch_other)), hidden_grad, piece_d, up_far
        )[0]
    )
    up_shard = sum_over_z(after(up_sum, down_pair))
    norm_one_parts = line.leave(
        *row_groups(line.enter(proj_grad), qkv_parts, qkv_offsets, (model, qkv_width), True)
    )
    out_sum = line.leave(
        *weight_grad(
            line.enter(mixed),
            branch_all,
            blocks_at(out_blocks, 0),
            shard_count,
            piece_d // 2,
            half,
        )
    )[0]
    feed_other = lax.ppermute(after(feed_away, up_sum), "y", SWAP)

    def norm_one_back(*norm_one_parts):
        home, away = core_sum(norm_one_parts, yi)
        away = lax.ppermute(away, "y", SWAP)
        norm_one_grad = home_sum(home, away)
        input_part, gain_one_grad, shift_one_grad = norm_back(inputs, gain_one, norm_one_grad)
        input_grad = (residual_grad + input_part).reshape(1, tok_count, model)
        return input_grad, gain_one_grad, shift_one_grad

    input_grad, gain_one_grad, shift_one_grad = line.leave(
        *stage(flag, norm_one_back, after(line.enter(norm_one_parts[0]), feed_other), norm_one_parts[1])
    )
    (qkv_sum,) = line.leave(
        *near_terms(line.enter(after(normed_one, up_shard)), proj_grad, piece_d, qkv_far)
    )
    qkv_shard = sum_over_z(qkv_sum)

    def ends(up_shard):
        feed_out = home_sum(feed_home, feed_other)
        output_shard = (residual_one + feed_out + bias_down).astype(low)
        output_shard = output_shard.reshape(1, tok_count, model)
        up_bias_grad = jnp.where(
            (jnp.arange(4, dtype=jnp.int32) == si)[None, :, None],
            up_bias_part.reshape(shard_count, 1, ff_part),
            0.0,
        ).reshape(shard_count, ff_piece)
        vector_grad = jnp.concatenate(
            [
                part.reshape(shard_count, -1)
                for part in (
                    gain_one_grad,
                    shift_one_grad,
                    gain_two_grad,
                    shift_two_grad,
                    down_bias_part,
                    up_bias_grad,
                )
            ],
            axis=1,
        )
        for name in ("c", "y"):
            vector_grad = vector_grad + lax.ppermute(vector_grad, name, SWAP)
        up_shard = after(up_shard, vector_grad)
        vector_grad = vector_grad.reshape(z_count, 2, -1)
        away = lax.dynamic_index_in_dim(vector_grad, 1 - xi, 1, keepdims=False)
        home = lax.dynamic_index_in_dim(vector_grad, xi, 1, keepdims=False)
        vector_grad = home + lax.ppermute(away, "x", SWAP)
        up_other = lax.ppermute(up_shard, "y", SWAP)
        down_far = lax.ppermute(after(down_pair[1], vector_grad), "x", SWAP)
        down_shard = (down_pair[0].astype(wide) + down_far.astype(wide)).astype(low)
        return output_shard, sum_small(vector_grad), down_shard, up_other

    output_shard, vector_total, down_shard, up_other = line.leave(
        *stage(flag, ends, line.enter(up_shard))
    )

    def more_ends(down_shard):
        down_other = lax.ppermute(down_shard, "y", SWAP)
        out_away = lax.ppermute(out_sum[:z_count], "x", SWAP)
        up_total = widen_columns(core_pieces(up_shard, up_other), places, shard_count)
        out_both = (out_sum[z_count:].astype(wide) + out_away.astype(wide)).astype(low)
        return out_both, up_total, after(down_other, up_total)

    out_both, up_total, down_other = stage(flag, more_ends, line.enter(down_shard))
    out_shard = sum_over_z(after(out_both, qkv_shard))

    def last(qkv_shard):
        other = lax.ppermute(qkv_shard, "y", SWAP)
        down_total = widen_rows(core_pieces(down_shard, down_other), places)
        qkv_pieces = core_pieces(qkv_shard, after(other, down_total))
        return widen_heads(qkv_pieces, places), down_total

    qkv_total, down_total = stage(flag, last, after(qkv_shard, up_total))
    out_total = widen_quarters(seq_pieces(after(out_shard, qkv_total)), places)
    vectors = [vector_total[slot * piece_d : (slot + 1) * piece_d] for slot in range(5)]
    return (
        output_shard,
        input_grad,
        vectors[0],
        vectors[1],
        qkv_total,
        out_total,
        vectors[2],
        vectors[3],
        up_total,
        vector_total[5 * piece_d :],
        down_total,
        vectors[4],
    )


def solution(mesh):
    shard_count, seq_count = mesh.shape["fsdp"], mesh.shape["seq"]

    def step(*args):
        model, hidden = args[0].shape[2], args[12].shape[0]
        rows_each = args[0].shape[0] // shard_count
        if (
            rows_each == 1
            and seq_count == 4
            and model // shard_count == 2 * HD
            and hidden // (4 * shard_count) % 256 == 0
        ):
            fsdp, seq = ("z", "x"), ("y", "c")
            devices = mesh.devices.reshape(shard_count // 2, 2, 2, 2)
            inner, body = Mesh(devices, fsdp + seq), split_shards
        else:
            fsdp, seq = "fsdp", "seq"
            inner, body = mesh, plain_shards
        rows, tokens = P(fsdp, None), P(fsdp, seq, None)
        vector = P(fsdp)
        placed = (tokens, tokens, rows, rows, rows, vector, vector, rows, rows)
        placed += (vector, vector, rows, vector, rows, vector)
        given = (tokens, tokens, vector, vector, rows, rows, vector, vector)
        given += (rows, vector, rows, vector)
        return jax.shard_map(
            body, mesh=inner, in_specs=placed, out_specs=given, check_vma=False
        )(*args)

    return step
```

```python
import functools

import jax
import jax.numpy as jnp
import numpy as np
from jax import lax
from jax.experimental import pallas as pl
from jax.experimental.pallas import tpu as pltpu
from jax.sharding import Mesh
from jax.sharding import PartitionSpec as P

H = 16
HD = 128


EPSILON = 1e-05
MASKED = -1e30
SWAP = ((0, 1), (1, 0))
VMEM_LIMIT = 56 << 20
GELU_A = float(np.sqrt(2.0 / np.pi))
GELU_B = 0.044715


def layer_norm(values, gain_vec, shift_vec):
    center = values - jnp.mean(values, axis=-1, keepdims=True)
    spread = jnp.mean(center * center, axis=-1, keepdims=True)
    return center * lax.rsqrt(spread + EPSILON) * gain_vec + shift_vec


def contract_rows(left, right):
    return lax.dot_general(
        left, right, (((0,), (0,)), ((), ())), preferred_element_type=jnp.float32
    )


def times_transpose(left, right):
    return lax.dot_general(
        left, right, (((1,), (1,)), ((), ())), preferred_element_type=jnp.float32
    )


def item_numbers(starts, lengths, positions):
    inside = (positions[None, :] >= starts[:, None]) & (
        positions[None, :] < (starts + lengths)[:, None]
    )
    labels = jnp.arange(1, starts.shape[0] + 1, dtype=jnp.int32)
    return jnp.sum(jnp.where(inside, labels[:, None], 0), axis=0) - 1


def visible_mask(query_pos, key_pos, query_item, key_item, key_pad):
    same_item = (query_item[:, None] == key_item[None, :]) & (query_item[:, None] >= 0)
    before = key_pos[None, :] < query_pos[:, None]
    return same_item & before & (key_pad[None, :] == 1) | (key_pos[None, :] == query_pos[:, None])


def masked_scores(query_rows, key_rows, visible, score_scale):
    scores = (
        jnp.einsum("qhd,khd->hqk", query_rows, key_rows, preferred_element_type=jnp.float32)
        * score_scale
    )
    return jnp.where(visible[None], scores, MASKED)


def attend_rows(query_rows, key_rows, value_rows, visible, score_scale):
    scores = masked_scores(query_rows, key_rows, visible, score_scale)
    row_peak = jnp.max(scores, axis=-1, keepdims=True)
    exp_scores = jnp.exp(scores - row_peak)
    row_total = jnp.sum(exp_scores, axis=-1, keepdims=True)
    attn_probs = exp_scores / row_total
    mixed_rows = jnp.einsum(
        "hqk,khd->qhd",
        attn_probs.astype(jnp.bfloat16),
        value_rows,
        preferred_element_type=jnp.float32,
    )
    return (mixed_rows, row_peak + jnp.log(row_total))


def attend_back(query_rows, key_rows, value_rows, visible, log_total, mixed_grad, score_scale):
    scores = masked_scores(query_rows, key_rows, visible, score_scale)
    attn_probs = jnp.exp(scores - log_total)
    prob_grad = jnp.einsum(
        "qhd,khd->hqk", mixed_grad, value_rows, preferred_element_type=jnp.float32
    )
    value_part = jnp.einsum(
        "hqk,qhd->khd",
        attn_probs.astype(jnp.bfloat16),
        mixed_grad,
        preferred_element_type=jnp.float32,
    )
    inner_sum = jnp.sum(prob_grad * attn_probs, axis=-1, keepdims=True)
    score_grad = (attn_probs * (prob_grad - inner_sum)).astype(jnp.bfloat16)
    query_grad = (
        jnp.einsum("hqk,khd->qhd", score_grad, key_rows, preferred_element_type=jnp.float32)
        * score_scale
    )
    key_part = (
        jnp.einsum("hqk,qhd->khd", score_grad, query_rows, preferred_element_type=jnp.float32)
        * score_scale
    )
    return (query_grad.astype(jnp.bfloat16), key_part, value_part)


def plain_shards(
    block_input,
    cotangent,
    item_starts,
    item_lengths,
    pad_mask,
    ln1_gain,
    ln1_shift,
    w_qkv,
    w_out,
    ln2_gain,
    ln2_shift,
    w_up,
    up_bias,
    w_down,
    down_bias,
):
    rows_here, tok_count, model_width = block_input.shape
    seq_count = lax.axis_size("seq")
    shard_count = lax.axis_size("fsdp")
    length = tok_count * seq_count
    score_scale = HD ** (-0.5)
    piece_d = ln1_gain.shape[0]
    seq_first = lax.axis_index("seq") * tok_count
    packed = jnp.concatenate([ln1_gain, ln1_shift, ln2_gain, ln2_shift, down_bias, up_bias])
    vector_table = lax.all_gather(packed, "fsdp", axis=0, tiled=True).reshape(shard_count, -1)

    def vector_part(slot):
        return vector_table[:, slot * piece_d : (slot + 1) * piece_d].reshape(-1)

    gain_one, shift_one, gain_two, shift_two, bias_down = [vector_part(slot) for slot in range(5)]
    bias_up = vector_table[:, 5 * piece_d :].reshape(-1)
    qkv_full, out_full = (
        lax.all_gather(w_qkv, "fsdp", axis=0, tiled=True),
        lax.all_gather(w_out, "fsdp", axis=0, tiled=True),
    )
    inputs = block_input.reshape(rows_here * tok_count, model_width).astype(jnp.float32)
    normed_one = layer_norm(inputs, gain_one, shift_one).astype(jnp.bfloat16)
    projected = jnp.dot(normed_one, qkv_full, preferred_element_type=jnp.float32).astype(
        jnp.bfloat16
    )
    query_all = projected[:, :model_width].reshape(rows_here, tok_count, H, HD)
    kv_local = projected[:, model_width:].reshape(rows_here, tok_count, 2 * model_width)
    kv_whole = lax.all_gather(kv_local, "seq", axis=1, tiled=True)
    key_all = kv_whole[:, :, :model_width].reshape(rows_here, length, H, HD)
    value_all = kv_whole[:, :, model_width:].reshape(rows_here, length, H, HD)
    positions = jnp.arange(length, dtype=jnp.int32)
    query_pos = seq_first + jnp.arange(tok_count, dtype=jnp.int32)
    row_index = 0
    item_label = item_numbers(item_starts[row_index], item_lengths[row_index], positions)
    query_item = lax.dynamic_slice_in_dim(item_label, seq_first, tok_count)
    visible = visible_mask(query_pos, positions, query_item, item_label, pad_mask[row_index])
    mixed_part, log_total = attend_rows(
        query_all[row_index], key_all[row_index], value_all[row_index], visible, score_scale
    )
    visible_list = [visible]
    mixed_list = [mixed_part]
    logsum_list = [log_total]
    mixed_all = (
        jnp.stack(mixed_list).reshape(rows_here * tok_count, model_width).astype(jnp.bfloat16)
    )
    residual_one = inputs + jnp.dot(mixed_all, out_full, preferred_element_type=jnp.float32)
    up_full, down_full = (
        lax.all_gather(w_up, "fsdp", axis=0, tiled=True),
        lax.all_gather(w_down, "fsdp", axis=0, tiled=True),
    )
    normed_two = layer_norm(residual_one, gain_two, shift_two).astype(jnp.bfloat16)
    hidden_pre = jnp.dot(normed_two, up_full, preferred_element_type=jnp.float32) + bias_up
    activated = jax.nn.gelu(hidden_pre).astype(jnp.bfloat16)
    block_output = (
        residual_one + jnp.dot(activated, down_full, preferred_element_type=jnp.float32) + bias_down
    )
    output_shard = block_output.astype(jnp.bfloat16).reshape(rows_here, tok_count, model_width)
    up_full, down_full = (
        lax.all_gather(w_up, "fsdp", axis=0, tiled=True),
        lax.all_gather(w_down, "fsdp", axis=0, tiled=True),
    )
    cot_flat = cotangent.reshape(rows_here * tok_count, model_width)
    cot_wide = cot_flat.astype(jnp.float32)
    down_grad = contract_rows(activated, cot_flat)
    down_bias_part = jnp.sum(cot_wide, axis=0)
    act_grad = times_transpose(cot_flat, down_full)
    gelu_back = jax.vjp(jax.nn.gelu, hidden_pre)[1]
    hidden_grad = gelu_back(act_grad)[0].astype(jnp.bfloat16)
    up_grad = contract_rows(normed_two, hidden_grad)
    up_bias_part = jnp.sum(hidden_grad.astype(jnp.float32), axis=0)
    norm_two_grad = times_transpose(hidden_grad, up_full)
    norm_two_back = jax.vjp(layer_norm, residual_one, gain_two, shift_two)[1]
    resid_part, gain_two_grad, shift_two_grad = norm_two_back(norm_two_grad)
    residual_grad = cot_wide + resid_part
    up_sum, down_sum = (
        lax.psum_scatter(up_grad, "fsdp", scatter_dimension=0, tiled=True),
        lax.psum_scatter(down_grad, "fsdp", scatter_dimension=0, tiled=True),
    )
    qkv_full, out_full = (
        lax.all_gather(w_qkv, "fsdp", axis=0, tiled=True),
        lax.all_gather(w_out, "fsdp", axis=0, tiled=True),
    )
    branch_grad = residual_grad.astype(jnp.bfloat16)
    out_grad = contract_rows(mixed_all, branch_grad)
    mixed_grad = (
        times_transpose(branch_grad, out_full)
        .astype(jnp.bfloat16)
        .reshape(rows_here, tok_count, H, HD)
    )
    row_index = 0
    query_grad, key_part, value_part = attend_back(
        query_all[row_index],
        key_all[row_index],
        value_all[row_index],
        visible_list[row_index],
        logsum_list[row_index],
        mixed_grad[row_index],
        score_scale,
    )
    query_list = [query_grad.reshape(tok_count, model_width)]
    kv_list = [
        jnp.concatenate(
            [key_part.reshape(length, model_width), value_part.reshape(length, model_width)], axis=1
        )
    ]
    kv_terms = jnp.stack(kv_list)
    kv_grad = lax.psum_scatter(kv_terms, "seq", scatter_dimension=1, tiled=True).astype(
        jnp.bfloat16
    )
    proj_grad = jnp.concatenate(
        [
            jnp.stack(query_list).reshape(rows_here * tok_count, model_width),
            kv_grad.reshape(rows_here * tok_count, 2 * model_width),
        ],
        axis=1,
    )
    qkv_grad = contract_rows(normed_one, proj_grad)
    norm_one_grad = times_transpose(proj_grad, qkv_full)
    norm_one_back = jax.vjp(layer_norm, inputs, gain_one, shift_one)[1]
    input_part, gain_one_grad, shift_one_grad = norm_one_back(norm_one_grad)
    input_grad = (residual_grad + input_part).reshape(rows_here, tok_count, model_width)
    vector_grad = jnp.concatenate(
        [
            piece_grad.reshape(shard_count, -1)
            for piece_grad in (
                gain_one_grad,
                shift_one_grad,
                gain_two_grad,
                shift_two_grad,
                down_bias_part,
                up_bias_part,
            )
        ],
        axis=1,
    ).reshape(-1)
    qkv_sum, out_sum, vector_sum = (
        lax.psum_scatter(qkv_grad, "fsdp", scatter_dimension=0, tiled=True),
        lax.psum_scatter(out_grad, "fsdp", scatter_dimension=0, tiled=True),
        lax.psum_scatter(vector_grad, "fsdp", scatter_dimension=0, tiled=True),
    )
    up_total, down_total, qkv_total, out_total, vector_total = lax.psum(
        (up_sum, down_sum, qkv_sum, out_sum, vector_sum), "seq"
    )
    gain_one_out = vector_total[0:piece_d]
    shift_one_out = vector_total[piece_d : 2 * piece_d]
    gain_two_out = vector_total[2 * piece_d : 3 * piece_d]
    shift_two_out = vector_total[3 * piece_d : 4 * piece_d]
    down_bias_out = vector_total[4 * piece_d : 5 * piece_d]
    up_bias_out = vector_total[5 * piece_d :]
    return (
        output_shard,
        input_grad,
        gain_one_out,
        shift_one_out,
        qkv_total,
        out_total,
        gain_two_out,
        shift_two_out,
        up_total,
        up_bias_out,
        down_total,
        down_bias_out,
    )


def gather_small(vector, z_count):
    line = [vector]
    for j in range(1, z_count):
        line.append(lax.ppermute(vector, "z", [(i, (i + j) % z_count) for i in range(z_count)]))
    return line + [lax.ppermute(piece, "x", SWAP) for piece in line]


def gather_weight(shard, *others):
    near = lax.all_gather(shard, "z", axis=0, tiled=False)
    return [near, lax.ppermute(after(near, *others), "x", SWAP)]


def stage(flag, work, *args):
    shapes = jax.eval_shape(work, *args)

    def nothing(*_):
        return jax.tree.map(lambda a: jnp.zeros(a.shape, a.dtype), shapes)

    return lax.cond(flag, work, nothing, *args)


class Line:
    def __init__(self):
        self.last = ()

    def enter(self, value):
        return after(value, *self.last)

    def leave(self, *results):
        self.last = results[:1]
        return results


def after(value, *others):
    return lax.optimization_barrier((value,) + others)[0]


def seq_pieces(block, *others):
    return core_pieces(block, after(lax.ppermute(block, "y", SWAP), *others))


def core_pieces(block, other):
    return [block, lax.ppermute(block, "c", SWAP), other, lax.ppermute(other, "c", SWAP)]


def by_bit(bit, mine, theirs):
    return jnp.where(bit == 0, mine, theirs), jnp.where(bit == 0, theirs, mine)


def gather_tokens(block, yi, ci, *others):
    parts = seq_pieces(block, *others)
    near = by_bit(ci, parts[0], parts[1])
    far = by_bit(ci, parts[2], parts[3])
    rows = [jnp.where(yi == 0, n, f) for n, f in zip(near, far)]
    rows += [jnp.where(yi == 0, f, n) for n, f in zip(near, far)]
    return jnp.concatenate(rows, axis=0)


def core_sum(parts, yi):
    away, home = parts
    other = lax.ppermute(away, "c", SWAP)
    tokens, model = home.shape[0] // 2, home.shape[1]
    steps = 4
    block = (tokens // steps, model)

    def kernel(at_ref, *refs):
        wide = jnp.float32
        refs[4][...] = refs[0][...].astype(wide) + refs[1][...].astype(wide)
        refs[5][...] = (refs[2][...].astype(wide) + refs[3][...].astype(wide)).astype(
            jnp.bfloat16
        )

    here = pl.BlockSpec(block, lambda i, at: (at[0] * steps + i, 0))
    there = pl.BlockSpec(block, lambda i, at: ((1 - at[0]) * steps + i, 0))
    out = pl.BlockSpec(block, lambda i, at: (i, 0))
    return pl.pallas_call(
        kernel,
        grid_spec=pltpu.PrefetchScalarGridSpec(
            num_scalar_prefetch=1,
            grid=(steps,),
            in_specs=[here, here, there, there],
            out_specs=[out, out],
        ),
        out_shape=[
            jax.ShapeDtypeStruct((tokens, model), jnp.float32),
            jax.ShapeDtypeStruct((tokens, model), jnp.bfloat16),
        ],
        cost_estimate=cost(flops=0, bytes_accessed=7 * tokens * model, transcendentals=0),
        compiler_params=params(),
    )(jnp.reshape(yi, (1,)).astype(jnp.int32), home, other, home, other)


def home_sum(home, other):
    return home + other.astype(jnp.float32)


COST_SCALE = 0.01


def cost(flops, bytes_accessed, transcendentals):
    return pl.CostEstimate(
        flops=int(flops * COST_SCALE),
        bytes_accessed=int(bytes_accessed * COST_SCALE),
        transcendentals=int(transcendentals * COST_SCALE),
    )


def params(limit=VMEM_LIMIT):
    return pltpu.CompilerParams(vmem_limit_bytes=limit)


def weight_matmul(left, pieces, offsets, shape, back, body, extras, outs, chunk, groups=None):
    rows = left.shape[0]
    depth, width = shape
    out_width = depth if back else width
    steps = out_width // chunk
    n_pieces, n_extras = len(pieces), len(extras)
    blocks = [(p, k) for p, piece in enumerate(pieces) for k in range(piece.shape[0])]
    block_rows, block_cols = pieces[0].shape[1:]
    row_count, col_count = depth // block_rows, width // block_cols

    tables = (offsets,) if groups is None else (offsets, groups)

    def kernel(*refs):
        table_refs, left_ref, refs = refs[: len(tables)], refs[len(tables)], refs[len(tables) + 1 :]
        offs_ref = table_refs[0]
        piece_refs = refs[:n_pieces]
        extra_refs = refs[n_pieces : n_pieces + n_extras]
        out_refs = refs[n_pieces + n_extras : -2]
        held, sems = refs[-2:]
        step = pl.program_id(0)

        def slot(row, col):
            return sems.at[row, col]

        @pl.when(step == 0)
        def _():
            for b, (p, k) in enumerate(blocks):
                row, col = offs_ref[0, b], offs_ref[1, b]
                target = held.at[
                    pl.ds(pl.multiple_of(row * block_rows, block_rows), block_rows),
                    pl.ds(pl.multiple_of(col * block_cols, block_cols), block_cols),
                ]
                pltpu.make_async_copy(piece_refs[p].at[k], target, slot(row, col)).start()

        def arrive(row, col):
            target = held.at[
                pl.ds(row * block_rows, block_rows), pl.ds(col * block_cols, block_cols)
            ]
            pltpu.make_async_copy(piece_refs[0].at[0], target, slot(row, col)).wait()

        for n in range(steps):
            needed = [
                (row, col)
                for row in range(row_count)
                for col in range(col_count)
                if (
                    row * block_rows // chunk if back else col * block_cols // chunk
                ) == n
            ]
            if needed:

                @pl.when(step == n)
                def _():
                    for row, col in needed:
                        arrive(row, col)

        start = pl.ds(pl.multiple_of(step * chunk, chunk), chunk)

        def product(part):
            if back:
                return lax.dot_general(
                    part,
                    held[start, :],
                    (((1,), (1,)), ((), ())),
                    preferred_element_type=jnp.float32,
                )
            return jnp.dot(part, held[:, start], preferred_element_type=jnp.float32)

        if groups is None:
            body(product(left_ref[...]), extra_refs, out_refs)
        else:
            size = rows // groups.shape[0]
            each = out_refs[0].shape[0] // size
            for g in range(groups.shape[0]):
                at = pl.multiple_of(table_refs[1][g] * size, size)
                values = product(left_ref[pl.ds(at, size), :])
                to = (g % each) * size
                out_refs[g // each][to : to + size, :] = values.astype(jnp.bfloat16)

    def column_spec(array):
        return pl.BlockSpec((array.shape[0], chunk), lambda i, *tabs: (0, i))

    flops = 2 * rows * depth * width
    moved = 2 * (left.size + depth * width) + sum(
        a.size * a.dtype.itemsize for a in list(extras) + list(outs)
    )
    return pl.pallas_call(
        kernel,
        grid_spec=pltpu.PrefetchScalarGridSpec(
            num_scalar_prefetch=len(tables),
            grid=(steps,),
            in_specs=[
                pl.BlockSpec(
                    left.shape, lambda i, *tabs: (0, 0), pipeline_mode=pl.Buffered(1)
                )
            ]
            + [pl.BlockSpec(memory_space=pl.ANY)] * n_pieces
            + [column_spec(a) for a in extras],
            out_specs=[column_spec(a) for a in outs],
            scratch_shapes=[
                pltpu.VMEM((depth, width), jnp.bfloat16),
                pltpu.SemaphoreType.DMA((row_count, col_count)),
            ],
        ),
        out_shape=list(outs),
        cost_estimate=cost(flops=flops, bytes_accessed=moved, transcendentals=0),
        compiler_params=params(),
    )(*tables, left, *pieces, *extras)


def store_low(values, extra_refs, out_refs):
    out_refs[0][...] = values.astype(jnp.bfloat16)


def store_gelu(values, extra_refs, out_refs):
    hidden = values + extra_refs[0][...]
    square = hidden * hidden
    bend = jnp.tanh(GELU_A * hidden * (1.0 + GELU_B * square))
    half = 0.5 * (1.0 + bend)
    out_refs[0][...] = (hidden * half).astype(jnp.bfloat16)
    slope = half + 0.5 * hidden * (1.0 - bend * bend) * (
        GELU_A * (1.0 + 3.0 * GELU_B * square)
    )
    out_refs[1][...] = slope


def store_hidden_grad(values, extra_refs, out_refs):
    low = (values * extra_refs[0][...]).astype(jnp.bfloat16)
    out_refs[0][...] = low
    out_refs[1][...] = jnp.sum(low.astype(jnp.float32), axis=0, keepdims=True)


def weight_grad(left, right, where, count, block, width, addend=None, parts=1):
    rows = left.shape[0]
    part = width // parts
    added = () if addend is None else (addend,)

    def kernel(where_ref, left_ref, right_ref, *refs):
        for n in range(parts):
            cols = slice(n * part, (n + 1) * part)
            value = lax.dot_general(
                left_ref[...],
                right_ref[:, cols],
                (((0,), (0,)), ((), ())),
                preferred_element_type=jnp.float32,
            )
            if added:
                value = value + refs[0][0, :, cols].astype(jnp.float32)
            refs[len(added) + n][0] = value.astype(jnp.bfloat16)

    return pl.pallas_call(
        kernel,
        grid_spec=pltpu.PrefetchScalarGridSpec(
            num_scalar_prefetch=1,
            grid=(count,),
            in_specs=[
                pl.BlockSpec((rows, block), lambda k, at: (0, at[k])),
                pl.BlockSpec((rows, width), lambda k, at: (0, at[count])),
            ]
            + [pl.BlockSpec((1, block, width), lambda k, at: (k, 0, 0))] * len(added),
            out_specs=[pl.BlockSpec((1, block, part), lambda k, at: (k, 0, 0))] * parts,
        ),
        out_shape=[jax.ShapeDtypeStruct((count, block, part), jnp.bfloat16)] * parts,
        cost_estimate=cost(
            flops=2 * rows * count * block * width,
            bytes_accessed=2 * rows * (count * block + width) + 4 * count * block * width,
            transcendentals=0,
        ),
        compiler_params=params(),
    )(where, left, right, *added)


def slice_qkv(w_qkv, where, width):
    rows = w_qkv.shape[0]
    heads = H // 4

    def kernel(at_ref, from_ref, to_ref):
        for i in range(heads):
            col = pl.ds(pl.multiple_of((2 * i + at_ref[1]) * HD, HD), HD)
            to_ref[:, i * HD : (i + 1) * HD] = from_ref[:, col]

    part = heads * HD
    return pl.pallas_call(
        kernel,
        grid_spec=pltpu.PrefetchScalarGridSpec(
            num_scalar_prefetch=1,
            grid=(3,),
            in_specs=[pl.BlockSpec((rows, 2 * part), lambda g, at: (0, 2 * g + at[0]))],
            out_specs=pl.BlockSpec((rows, part), lambda g, at: (0, g)),
        ),
        out_shape=jax.ShapeDtypeStruct((rows, width), jnp.bfloat16),
        cost_estimate=cost(flops=0, bytes_accessed=3 << 20, transcendentals=0),
        compiler_params=params(),
    )(where, w_qkv)


def slice_weights(w_out, w_up, w_down, where, shard_count):
    rows, model = w_out.shape
    ff_part = w_down.shape[0] // 4
    steps = shard_count
    part = ff_part // steps
    up_half = steps // 2

    def kernel(at_ref, out_ref, up_ref, down_ref, out_to, low_to, high_to, left_to, right_to):
        step = pl.program_id(0)
        for n, up_to in enumerate((low_to, high_to)):

            @pl.when(step // up_half == n)
            def _():
                up_to[...] = up_ref[...]

        @pl.when(step == 0)
        def _():
            out_to[...] = out_ref[...]

        left_to[...] = down_ref[:, : model // 2]
        right_to[...] = down_ref[:, model // 2 :]

    def up_spec(n):
        return pl.BlockSpec(
            (rows, ff_part), lambda i, at: (0, jnp.clip(i - n * up_half, 0, up_half - 1))
        )

    return pl.pallas_call(
        kernel,
        grid_spec=pltpu.PrefetchScalarGridSpec(
            num_scalar_prefetch=1,
            grid=(steps,),
            in_specs=[
                pl.BlockSpec((rows // 2, model // 2), lambda i, at: (at[1], at[0])),
                pl.BlockSpec((rows, ff_part), lambda i, at: (0, 4 * i + 2 * at[0] + at[1])),
                pl.BlockSpec(
                    (part, model), lambda i, at: ((2 * at[0] + at[1]) * steps + i, 0)
                ),
            ],
            out_specs=[
                pl.BlockSpec((rows // 2, model // 2), lambda i, at: (0, 0)),
                up_spec(0),
                up_spec(1),
                pl.BlockSpec((part, model // 2), lambda i, at: (i, 0)),
                pl.BlockSpec((part, model // 2), lambda i, at: (i, 0)),
            ],
        ),
        out_shape=[
            jax.ShapeDtypeStruct(shape, jnp.bfloat16)
            for shape in [(rows // 2, model // 2)]
            + [(rows, ff_part * up_half)] * 2
            + [(ff_part, model // 2)] * 2
        ],
        cost_estimate=cost(flops=0, bytes_accessed=9 << 20, transcendentals=0),
        compiler_params=params(),
    )(where, w_out, w_up, w_down)


def visible_tile(query_item, key_item, first_query, n_query, n_key):
    query_pos = first_query + lax.broadcasted_iota(jnp.int32, (n_query, n_key), 0)
    key_pos = lax.broadcasted_iota(jnp.int32, (n_query, n_key), 1)
    return ((query_item == key_item) & (key_pos < query_pos)) | (key_pos == query_pos)


def head_spec(length, first):
    return pl.BlockSpec((length, HD), lambda h: (0, first + h))


def attention(projected, query_item, key_item, heads, tile):
    length = projected.shape[0]
    scale = HD ** (-0.5)

    def kernel(q_ref, k_ref, v_ref, qi_ref, ki_ref, mixed_ref, log_ref):
        for start in range(0, length, tile):
            stop = start + tile
            rows = slice(start, stop)
            scores = (
                lax.dot_general(
                    q_ref[rows, :],
                    k_ref[:stop, :],
                    (((1,), (1,)), ((), ())),
                    preferred_element_type=jnp.float32,
                )
                * scale
            )
            seen = visible_tile(qi_ref[rows, :], ki_ref[:, :stop], start, tile, stop)
            scores = jnp.where(seen, scores, MASKED)
            peak = jnp.max(scores, axis=-1, keepdims=True)
            weights = jnp.exp(scores - peak)
            total = jnp.sum(weights, axis=-1, keepdims=True)
            probs = (weights * (1.0 / total)).astype(jnp.bfloat16)
            mixed_ref[rows, :] = jnp.dot(
                probs, v_ref[:stop, :], preferred_element_type=jnp.float32
            ).astype(jnp.bfloat16)
            log_ref[0, rows, :] = peak + jnp.log(total)

    whole = lambda rows, cols: pl.BlockSpec((rows, cols), lambda h: (0, 0))
    return pl.pallas_call(
        kernel,
        grid=(heads,),
        in_specs=[head_spec(length, g * heads) for g in range(3)]
        + [whole(length, 1), whole(1, length)],
        out_specs=[head_spec(length, 0), pl.BlockSpec((1, length, 1), lambda h: (h, 0, 0))],
        out_shape=[
            jax.ShapeDtypeStruct((length, heads * HD), jnp.bfloat16),
            jax.ShapeDtypeStruct((heads, length, 1), jnp.float32),
        ],
        cost_estimate=cost(
            flops=4 * heads * length * length * HD,
            bytes_accessed=8 * length * heads * HD,
            transcendentals=heads * length * length,
        ),
        compiler_params=params(),
    )(projected, projected, projected, query_item, key_item)


def attention_back(projected, mixed_grad, log_total, query_item, key_item, heads, tile):
    length = projected.shape[0]
    scale = HD ** (-0.5)

    def kernel(q_ref, k_ref, v_ref, g_ref, log_ref, qi_ref, ki_ref, grad_ref, dk_ref, dv_ref):
        head = pl.program_id(0)

        def place(group):
            return pl.ds(pl.multiple_of((group * heads + head) * HD, HD), HD)

        for start in reversed(range(0, length, tile)):
            stop = start + tile
            rows = slice(start, stop)
            query, grad = q_ref[rows, :], g_ref[rows, :]
            key, value = k_ref[:stop, :], v_ref[:stop, :]
            scores = (
                lax.dot_general(
                    query, key, (((1,), (1,)), ((), ())), preferred_element_type=jnp.float32
                )
                * scale
            )
            seen = visible_tile(qi_ref[rows, :], ki_ref[:, :stop], start, tile, stop)
            probs = jnp.exp(jnp.where(seen, scores, MASKED) - log_ref[0, rows, :])
            prob_grad = lax.dot_general(
                grad, value, (((1,), (1,)), ((), ())), preferred_element_type=jnp.float32
            )
            inner = jnp.sum(prob_grad * probs, axis=-1, keepdims=True)
            score_grad = (probs * (prob_grad - inner)).astype(jnp.bfloat16)
            grad_ref[rows, place(0)] = (
                jnp.dot(score_grad, key, preferred_element_type=jnp.float32) * scale
            ).astype(jnp.bfloat16)
            key_part = lax.dot_general(
                score_grad, query, (((0,), (0,)), ((), ())), preferred_element_type=jnp.float32
            )
            value_part = lax.dot_general(
                probs.astype(jnp.bfloat16),
                grad,
                (((0,), (0,)), ((), ())),
                preferred_element_type=jnp.float32,
            )
            if stop == length:
                dk_ref[...] = key_part
                dv_ref[...] = value_part
            else:
                dk_ref[:stop, :] += key_part
                dv_ref[:stop, :] += value_part
        grad_ref[:, place(1)] = (dk_ref[...] * scale).astype(jnp.bfloat16)
        grad_ref[:, place(2)] = dv_ref[...].astype(jnp.bfloat16)

    whole = lambda rows, cols: pl.BlockSpec((rows, cols), lambda h: (0, 0))
    return pl.pallas_call(
        kernel,
        grid=(heads,),
        in_specs=[head_spec(length, g * heads) for g in range(3)]
        + [
            head_spec(length, 0),
            pl.BlockSpec((1, length, 1), lambda h: (h, 0, 0)),
            whole(length, 1),
            whole(1, length),
        ],
        out_specs=whole(length, 3 * heads * HD),
        out_shape=jax.ShapeDtypeStruct((length, 3 * heads * HD), jnp.bfloat16),
        scratch_shapes=[pltpu.VMEM((length, HD), jnp.float32)] * 2,
        cost_estimate=cost(
            flops=10 * heads * length * length * HD,
            bytes_accessed=16 * length * heads * HD,
            transcendentals=heads * length * length,
        ),
        compiler_params=params(),
    )(projected, projected, projected, mixed_grad, log_total, query_item, key_item)


def widen(chunks, places, grid, piece_specs, out_block, out_index, out_shape, write):
    def kernel(place_ref, *refs):
        for n in range(len(chunks)):
            for r in range(4):
                write(n, place_ref[r], refs[4 * n + r], refs[-1])

    return pl.pallas_call(
        kernel,
        grid_spec=pltpu.PrefetchScalarGridSpec(
            num_scalar_prefetch=1,
            grid=(grid,),
            in_specs=[
                pl.BlockSpec(block, functools.partial(lambda at, i, pos: at(i), at))
                for block, at in piece_specs
                for _ in range(4)
            ],
            out_specs=pl.BlockSpec(out_block, lambda i, pos: out_index(i)),
        ),
        out_shape=jax.ShapeDtypeStruct(out_shape, jnp.float32),
        cost_estimate=cost(
            flops=0, bytes_accessed=6 * int(np.prod(out_shape)), transcendentals=0
        ),
        compiler_params=params(),
    )(places, *[piece for pieces in chunks for piece in pieces])


def widen_columns(pieces, places, blocks):
    rows, width = pieces[0].shape
    part = width // blocks

    def write(n, pos, piece, out):
        out[:, pl.ds(pl.multiple_of(pos * part, part), part)] = piece[...].astype(jnp.float32)

    return widen(
        [pieces],
        places,
        blocks,
        [((rows, part), lambda i: (0, i))],
        (rows, 4 * part),
        lambda i: (0, i),
        (rows, 4 * width),
        write,
    )


def widen_rows(pieces, places):
    rows, width = pieces[0].shape

    def write(n, pos, piece, out):
        @pl.when(pos == pl.program_id(0))
        def _():
            out[...] = piece[...].astype(jnp.float32)

    return widen(
        [pieces],
        places,
        4,
        [((rows, width), lambda i: (0, 0))],
        (rows, width),
        lambda i: (i, 0),
        (4 * rows, width),
        write,
    )


def widen_heads(pieces, places):
    rows, width = pieces[0].shape
    part = width // 3

    def write(n, pos, piece, out):
        first = lax.div(pos, 2) * part * 2 + lax.rem(pos, 2) * HD
        for i in range(part // HD):
            cols = pl.ds(pl.multiple_of(first + 2 * i * HD, HD), HD)
            out[:, cols] = piece[:, i * HD : (i + 1) * HD].astype(jnp.float32)

    return widen(
        [pieces],
        places,
        3,
        [((rows, part), lambda i: (0, i))],
        (rows, 4 * part),
        lambda i: (0, i),
        (rows, 4 * width),
        write,
    )


def widen_quarters(pieces, places):
    rows, width = pieces[0].shape

    def write(n, pos, piece, out):
        row = pl.multiple_of(lax.rem(pos, 2) * rows, rows)
        col = pl.multiple_of(lax.div(pos, 2) * width, width)
        out[pl.ds(row, rows), pl.ds(col, width)] = piece[...].astype(jnp.float32)

    return widen(
        [pieces],
        places,
        1,
        [((rows, width), lambda i: (0, 0))],
        (2 * rows, 2 * width),
        lambda i: (0, 0),
        (2 * rows, 2 * width),
        write,
    )


def norm_back(values, gain_vec, incoming):
    center = values - jnp.mean(values, axis=-1, keepdims=True)
    spread = jnp.mean(center * center, axis=-1, keepdims=True)
    inverse = lax.rsqrt(spread + EPSILON)
    unit = center * inverse
    scaled = incoming * gain_vec
    inner = jnp.mean(scaled * unit, axis=-1, keepdims=True)
    grad = (scaled - jnp.mean(scaled, axis=-1, keepdims=True) - unit * inner) * inverse
    return grad, jnp.sum(incoming * unit, axis=0), jnp.sum(incoming, axis=0)


def split_shards(
    block_input,
    cotangent,
    item_starts,
    item_lengths,
    pad_mask,
    ln1_gain,
    ln1_shift,
    w_qkv,
    w_out,
    ln2_gain,
    ln2_shift,
    w_up,
    up_bias,
    w_down,
    down_bias,
):
    low, wide = jnp.bfloat16, jnp.float32
    z_count = lax.axis_size("z")
    shard_count = 2 * z_count
    zi, xi, yi, ci = [lax.axis_index(name) for name in ("z", "x", "y", "c")]
    si = 2 * yi + ci
    tok_count, model = block_input.shape[1:]
    length = 4 * tok_count
    piece_d, ff_piece = ln1_gain.shape[0], up_bias.shape[0]
    ff_part = ff_piece // 4
    ff_here = ff_part * shard_count
    heads = H // 4
    places = jnp.stack([jnp.bitwise_xor(si, r) for r in range(4)]).astype(jnp.int32)

    packed = jnp.concatenate([ln1_gain, ln1_shift, ln2_gain, ln2_shift, down_bias, up_bias])
    vector_stack = jnp.stack(gather_small(packed, z_count))
    owners = jnp.stack(
        [
            lax.rem(zi - j + z_count, z_count) * 2 + jnp.bitwise_xor(xi, dx)
            for dx in range(2)
            for j in range(z_count)
        ]
    )
    hit = owners[None, :] == jnp.arange(shard_count, dtype=jnp.int32)[:, None]
    vector_table = jnp.sum(jnp.where(hit[:, :, None], vector_stack[None], 0.0), axis=1)

    def vector_part(slot):
        return vector_table[:, slot * piece_d : (slot + 1) * piece_d].reshape(-1)

    gain_one, shift_one, gain_two, shift_two, bias_down = [vector_part(slot) for slot in range(5)]
    bias_up = lax.dynamic_index_in_dim(
        vector_table[:, 5 * piece_d :].reshape(shard_count, 4, ff_part), si, 1, keepdims=False
    ).reshape(1, ff_here)

    line = Line()
    flag = item_lengths[0, 0] > 0
    where = jnp.stack([yi, ci]).astype(jnp.int32)
    qkv_slice = slice_qkv(w_qkv, where, 3 * heads * HD)
    slices = slice_weights(w_out, w_up, w_down, after(where, qkv_slice), shard_count)
    half = model // 2
    qkv_width = 3 * heads * HD
    qkv_parts = gather_weight(qkv_slice)
    down_pair = jnp.stack([slices[4], lax.ppermute(slices[4], "x", SWAP)])
    inputs = after(block_input, down_pair).reshape(tok_count, model).astype(wide)
    normed_one = layer_norm(inputs, gain_one, shift_one).astype(low)
    out_parts = gather_weight(after(slices[0], normed_one), qkv_parts[1])
    out_parts = out_parts + [lax.ppermute(piece, "y", SWAP) for piece in out_parts]

    near_blocks = [2 * z + xi for z in range(z_count)]
    far_blocks = [2 * z + 1 - xi for z in range(z_count)]
    split = near_blocks + far_blocks
    paired = [b for pair in zip(near_blocks, far_blocks) for b in pair]
    zero = jnp.zeros_like(xi)

    def table(*rows):
        return jnp.stack([jnp.stack(row) for row in rows]).astype(jnp.int32)

    qkv_offsets = table(split, [zero] * shard_count)
    up_offsets = table(split + split, [zero] * shard_count + [zero + 1] * shard_count)
    down_offsets = table(split + paired, [zero] * shard_count + [zero + 1] * shard_count)
    out_offsets = table(split + split, [yi] * shard_count + [1 - yi] * shard_count)

    def blocks_at(blocks, n):
        return table(blocks + [zero + n])[0]

    def sum_small(terms, *others):
        def term(j):
            return lax.dynamic_index_in_dim(
                terms, lax.rem(zi - j + z_count, z_count), 0, keepdims=False
            )

        total = term(0).astype(wide)
        for j in range(1, z_count):
            theirs = lax.ppermute(
                term(j), "z", [(i, (i - j) % z_count) for i in range(z_count)]
            )
            total = total + after(theirs, *others).astype(wide)
        return total

    def plain_matmul(left, pieces, offsets, shape, back, body, extras, outs):
        return weight_matmul(left, pieces, offsets, shape, back, body, extras, outs, 512)

    def row_groups(left, pieces, offsets, shape_, back):
        groups = jnp.stack([1 - ci, 3 - ci, ci, 2 + ci]).astype(jnp.int32)
        outs = (shape(2 * tok_count, shape_[0] if back else shape_[1]),) * 2
        return weight_matmul(left, pieces, offsets, shape_, back, None, (), outs, 512, groups)

    def matmul(left, *others):
        return line.leave(*plain_matmul(line.enter(left), *others))

    def grad_chunk(left, right, blocks, n, block, width):
        return line.leave(
            *weight_grad(line.enter(left), right, blocks_at(blocks, n), len(blocks), block, width)
        )[0]

    def far_terms(left, right, block):
        terms = grad_chunk(left, right, far_blocks, 0, block, right.shape[1])
        return lax.ppermute(terms, "x", SWAP)

    def near_terms(left, right, block, addend, parts=1):
        return weight_grad(
            left, right, blocks_at(near_blocks, 0), z_count, block, addend.shape[2], addend, parts
        )

    def sum_over_z(total):
        return lax.psum_scatter(total, "z", scatter_dimension=0, tiled=False)

    def shape(rows, cols, kind=low):
        return jax.ShapeDtypeStruct((rows, cols), kind)

    normed_one = gather_tokens(normed_one, yi, ci, qkv_parts[0])
    cot_flat = after(cotangent.reshape(tok_count, model), normed_one)
    cot_wide = cot_flat.astype(wide)
    cot_all = gather_tokens(cot_flat, yi, ci)
    (projected,) = matmul(
        after(normed_one, cot_all),
        qkv_parts,
        qkv_offsets,
        (model, qkv_width),
        False,
        store_low,
        (),
        (shape(length, qkv_width),),
    )
    up_parts = gather_weight(slices[1], projected)
    up_high = lax.all_gather(slices[2], "z", axis=0, tiled=False)
    down_parts = gather_weight(slices[3], projected)
    down_parts.append(lax.all_gather(down_pair, "z", axis=0, tiled=True))
    positions = jnp.arange(length, dtype=jnp.int32)
    item_label = item_numbers(item_starts[0], item_lengths[0], positions)
    query_item = item_label[:, None]
    key_item = jnp.where((item_label >= 0) & (pad_mask[0] == 1), item_label, -2)[None, :]
    mixed_heads, log_total = line.leave(
        *attention(line.enter(projected), query_item, key_item, heads, 256)
    )

    def attend_out(mixed_heads):
        halves = mixed_heads.reshape(2, 2 * tok_count, heads * HD)
        away = lax.dynamic_index_in_dim(halves, 1 - yi, 0, keepdims=False)
        mine = lax.dynamic_index_in_dim(halves, yi, 0, keepdims=False)
        other = lax.ppermute(away, "y", SWAP)
        mixed = jnp.concatenate(by_bit(yi, mine, other), axis=1)
        (out_partial,) = plain_matmul(
            mixed,
            out_parts,
            out_offsets,
            (half, model),
            False,
            store_low,
            (),
            (shape(2 * tok_count, model),),
        )
        halves = out_partial.reshape(2, tok_count, model)
        away = lax.dynamic_index_in_dim(halves, 1 - ci, 0, keepdims=False)
        home = lax.dynamic_index_in_dim(halves, ci, 0, keepdims=False)
        residual_one = (
            inputs + home.astype(wide) + lax.ppermute(away, "c", SWAP).astype(wide)
        )
        normed_two = layer_norm(residual_one, gain_two, shift_two).astype(low)
        return normed_two, residual_one, mine, other

    up_parts += [up_high, lax.ppermute(after(up_high, mixed_heads), "x", SWAP)]
    normed_two, residual_one, mixed_home, mixed_other = line.leave(
        *stage(flag, attend_out, after(line.enter(mixed_heads), up_parts[0], up_high))
    )
    normed_two = gather_tokens(normed_two, yi, ci, up_parts[1], up_parts[3])
    activated, slope = matmul(
        normed_two,
        up_parts,
        up_offsets,
        (model, ff_here),
        False,
        store_gelu,
        (bias_up,),
        (shape(length, ff_here), shape(length, ff_here, wide)),
    )

    mixed_last = lax.ppermute(after(mixed_home, activated), "y", SWAP)
    others_heads = jnp.concatenate(by_bit(yi, mixed_other, mixed_last), axis=0)
    mixed = jnp.concatenate(by_bit(yi, mixed_heads, others_heads), axis=1)

    down_bias_part = jnp.sum(cot_wide, axis=0)
    down_sum = grad_chunk(
        after(activated, down_parts[1], mixed), cot_all, paired, 0, ff_part, model
    )
    down_pair = lax.psum_scatter(
        down_sum.reshape(z_count, 2, ff_part, model), "z", scatter_dimension=0, tiled=False
    )
    hidden_grad, up_bias_part = matmul(
        cot_all,
        down_parts,
        down_offsets,
        (ff_here, model),
        True,
        store_hidden_grad,
        (slope,),
        (shape(length, ff_here), shape(1, ff_here, wide)),
    )
    up_far = far_terms(normed_two, hidden_grad, piece_d)
    norm_two_parts = line.leave(
        *row_groups(line.enter(hidden_grad), up_parts, up_offsets, (model, ff_here), True)
    )

    def norm_two_back(*norm_two_parts):
        home, away = core_sum(norm_two_parts, yi)
        other = lax.ppermute(away, "y", SWAP)
        feed_parts = row_groups(
            after(activated, away), down_parts, down_offsets, (ff_here, model), False
        )
        norm_two_grad = home_sum(home, after(other, *feed_parts))
        resid_part, gain_two_grad, shift_two_grad = norm_back(
            residual_one, gain_two, norm_two_grad
        )
        residual_grad = cot_wide + resid_part
        branch_grad = residual_grad.astype(low)
        branch_pair = jnp.concatenate(
            by_bit(ci, branch_grad, lax.ppermute(branch_grad, "c", SWAP)), axis=0
        )
        return branch_pair, residual_grad, gain_two_grad, shift_two_grad, feed_parts

    branch_pair, residual_grad, gain_two_grad, shift_two_grad, feed_parts = line.leave(
        *stage(flag, norm_two_back, line.enter(norm_two_parts[0]), norm_two_parts[1])
    )

    out_blocks = far_blocks + near_blocks

    def out_back(branch_pair):
        (mixed_grad_pair,) = plain_matmul(
            branch_pair,
            out_parts,
            out_offsets,
            (half, model),
            True,
            store_low,
            (),
            (shape(2 * tok_count, half),),
        )
        part = heads * HD
        away = lax.dynamic_slice_in_dim(mixed_grad_pair, (1 - yi) * part, part, 1)
        home = lax.dynamic_slice_in_dim(mixed_grad_pair, yi * part, part, 1)
        theirs = lax.ppermute(away, "y", SWAP)
        feed_home, feed_away = core_sum([after(feed_parts[0], away), feed_parts[1]], yi)
        pair = after(branch_pair, away)
        branch_away = lax.dynamic_slice_in_dim(pair, (1 - yi) * half, half, 1)
        branch_home = lax.dynamic_slice_in_dim(pair, yi * half, half, 1)
        theirs = after(theirs, feed_away, branch_away, branch_home)
        mixed_grad = jnp.concatenate(by_bit(yi, home, theirs), axis=0)
        return mixed_grad, feed_home, feed_away, branch_away, branch_home

    mixed_grad, feed_home, feed_away, branch_away, branch_home = line.leave(
        *stage(flag, out_back, line.enter(branch_pair))
    )
    branch_other = lax.ppermute(after(branch_away, mixed_grad), "y", SWAP)
    branch_all = jnp.concatenate(by_bit(yi, branch_home, branch_other), axis=0)
    (proj_grad,) = line.leave(
        attention_back(
            projected,
            line.enter(mixed_grad),
            log_total,
            query_item,
            key_item,
            heads,
            256,
        )
    )
    qkv_far = far_terms(normed_one, proj_grad, piece_d)
    (up_sum,) = line.leave(
        near_terms(
            line.enter(after(normed_two, branch_other)), hidden_grad, piece_d, up_far
        )[0]
    )
    up_shard = sum_over_z(after(up_sum, down_pair))
    norm_one_parts = line.leave(
        *row_groups(line.enter(proj_grad), qkv_parts, qkv_offsets, (model, qkv_width), True)
    )
    out_sum = line.leave(
        *weight_grad(
            line.enter(mixed),
            branch_all,
            blocks_at(out_blocks, 0),
            shard_count,
            piece_d // 2,
            half,
        )
    )[0]
    feed_other = lax.ppermute(after(feed_away, up_sum), "y", SWAP)

    def norm_one_back(*norm_one_parts):
        home, away = core_sum(norm_one_parts, yi)
        away = lax.ppermute(away, "y", SWAP)
        norm_one_grad = home_sum(home, away)
        input_part, gain_one_grad, shift_one_grad = norm_back(inputs, gain_one, norm_one_grad)
        input_grad = (residual_grad + input_part).reshape(1, tok_count, model)
        return input_grad, gain_one_grad, shift_one_grad

    input_grad, gain_one_grad, shift_one_grad = line.leave(
        *stage(flag, norm_one_back, after(line.enter(norm_one_parts[0]), feed_other), norm_one_parts[1])
    )
    (qkv_sum,) = line.leave(
        *near_terms(line.enter(after(normed_one, up_shard)), proj_grad, piece_d, qkv_far)
    )
    qkv_shard = sum_over_z(qkv_sum)

    def ends(up_shard):
        up_other = lax.ppermute(up_shard, "y", SWAP)
        down_far = lax.ppermute(down_pair[1], "x", SWAP)
        output_shard = (residual_one + home_sum(feed_home, feed_other) + bias_down).astype(low)
        output_shard = output_shard.reshape(1, tok_count, model)
        down_shard = (down_pair[0].astype(wide) + down_far.astype(wide)).astype(low)
        return output_shard, down_shard, up_other

    output_shard, down_shard, up_other = line.leave(
        *stage(flag, ends, line.enter(up_shard))
    )

    def more_ends(down_shard):
        up_bias_grad = jnp.where(
            (jnp.arange(4, dtype=jnp.int32) == si)[None, :, None],
            up_bias_part.reshape(shard_count, 1, ff_part),
            0.0,
        ).reshape(shard_count, ff_piece)
        vector_grad = jnp.concatenate(
            [
                part.reshape(shard_count, -1)
                for part in (
                    gain_one_grad,
                    shift_one_grad,
                    gain_two_grad,
                    shift_two_grad,
                    down_bias_part,
                    up_bias_grad,
                )
            ],
            axis=1,
        )
        for name in ("c", "y"):
            vector_grad = vector_grad + lax.ppermute(vector_grad, name, SWAP)
        down_shard = after(down_shard, vector_grad)
        vector_grad = vector_grad.reshape(z_count, 2, -1)
        away = lax.dynamic_index_in_dim(vector_grad, 1 - xi, 1, keepdims=False)
        home = lax.dynamic_index_in_dim(vector_grad, xi, 1, keepdims=False)
        vector_grad = home + lax.ppermute(away, "x", SWAP)
        down_other = lax.ppermute(down_shard, "y", SWAP)
        out_away = lax.ppermute(after(out_sum[:z_count], vector_grad), "x", SWAP)
        up_total = widen_columns(core_pieces(up_shard, up_other), places, shard_count)
        out_both = (out_sum[z_count:].astype(wide) + out_away.astype(wide)).astype(low)
        return out_both, up_total, after(down_other, up_total), sum_small(vector_grad, up_total)

    out_both, up_total, down_other, vector_total = stage(
        flag, more_ends, after(line.enter(down_shard), down_shard)
    )
    out_shard = sum_over_z(after(out_both, qkv_sum))

    def last(qkv_shard):
        other = lax.ppermute(qkv_shard, "y", SWAP)
        down_total = widen_rows(core_pieces(down_shard, down_other), places)
        qkv_pieces = core_pieces(qkv_shard, after(other, down_total))
        return widen_heads(qkv_pieces, places), down_total

    qkv_total, down_total = stage(flag, last, after(qkv_shard, up_total))
    out_total = widen_quarters(seq_pieces(after(out_shard, qkv_total)), places)
    vectors = [vector_total[slot * piece_d : (slot + 1) * piece_d] for slot in range(5)]
    return (
        output_shard,
        input_grad,
        vectors[0],
        vectors[1],
        qkv_total,
        out_total,
        vectors[2],
        vectors[3],
        up_total,
        vector_total[5 * piece_d :],
        down_total,
        vectors[4],
    )


def solution(mesh):
    shard_count, seq_count = mesh.shape["fsdp"], mesh.shape["seq"]

    def step(*args):
        model, hidden = args[0].shape[2], args[12].shape[0]
        rows_each = args[0].shape[0] // shard_count
        if (
            rows_each == 1
            and seq_count == 4
            and model // shard_count == 2 * HD
            and hidden // (4 * shard_count) % 256 == 0
        ):
            fsdp, seq = ("z", "x"), ("y", "c")
            devices = mesh.devices.reshape(shard_count // 2, 2, 2, 2)
            inner, body = Mesh(devices, fsdp + seq), split_shards
        else:
            fsdp, seq = "fsdp", "seq"
            inner, body = mesh, plain_shards
        rows, tokens = P(fsdp, None), P(fsdp, seq, None)
        vector = P(fsdp)
        placed = (tokens, tokens, rows, rows, rows, vector, vector, rows, rows)
        placed += (vector, vector, rows, vector, rows, vector)
        given = (tokens, tokens, vector, vector, rows, rows, vector, vector)
        given += (rows, vector, rows, vector)
        return jax.shard_map(
            body, mesh=inner, in_specs=placed, out_specs=given, check_vma=False
        )(*args)

    return step
```

```python
import functools

import jax
import jax.numpy as jnp
import numpy as np
from jax import lax
from jax.experimental import pallas as pl
from jax.experimental.pallas import tpu as pltpu
from jax.sharding import Mesh
from jax.sharding import PartitionSpec as P

H = 16
HD = 128


EPSILON = 1e-05
MASKED = -1e30
SWAP = ((0, 1), (1, 0))
VMEM_LIMIT = 56 << 20
GELU_A = float(np.sqrt(2.0 / np.pi))
GELU_B = 0.044715


def layer_norm(values, gain_vec, shift_vec):
    center = values - jnp.mean(values, axis=-1, keepdims=True)
    spread = jnp.mean(center * center, axis=-1, keepdims=True)
    return center * lax.rsqrt(spread + EPSILON) * gain_vec + shift_vec


def contract_rows(left, right):
    return lax.dot_general(
        left, right, (((0,), (0,)), ((), ())), preferred_element_type=jnp.float32
    )


def times_transpose(left, right):
    return lax.dot_general(
        left, right, (((1,), (1,)), ((), ())), preferred_element_type=jnp.float32
    )


def item_numbers(starts, lengths, positions):
    inside = (positions[None, :] >= starts[:, None]) & (
        positions[None, :] < (starts + lengths)[:, None]
    )
    labels = jnp.arange(1, starts.shape[0] + 1, dtype=jnp.int32)
    return jnp.sum(jnp.where(inside, labels[:, None], 0), axis=0) - 1


def visible_mask(query_pos, key_pos, query_item, key_item, key_pad):
    same_item = (query_item[:, None] == key_item[None, :]) & (query_item[:, None] >= 0)
    before = key_pos[None, :] < query_pos[:, None]
    return same_item & before & (key_pad[None, :] == 1) | (key_pos[None, :] == query_pos[:, None])


def masked_scores(query_rows, key_rows, visible, score_scale):
    scores = (
        jnp.einsum("qhd,khd->hqk", query_rows, key_rows, preferred_element_type=jnp.float32)
        * score_scale
    )
    return jnp.where(visible[None], scores, MASKED)


def attend_rows(query_rows, key_rows, value_rows, visible, score_scale):
    scores = masked_scores(query_rows, key_rows, visible, score_scale)
    row_peak = jnp.max(scores, axis=-1, keepdims=True)
    exp_scores = jnp.exp(scores - row_peak)
    row_total = jnp.sum(exp_scores, axis=-1, keepdims=True)
    attn_probs = exp_scores / row_total
    mixed_rows = jnp.einsum(
        "hqk,khd->qhd",
        attn_probs.astype(jnp.bfloat16),
        value_rows,
        preferred_element_type=jnp.float32,
    )
    return (mixed_rows, row_peak + jnp.log(row_total))


def attend_back(query_rows, key_rows, value_rows, visible, log_total, mixed_grad, score_scale):
    scores = masked_scores(query_rows, key_rows, visible, score_scale)
    attn_probs = jnp.exp(scores - log_total)
    prob_grad = jnp.einsum(
        "qhd,khd->hqk", mixed_grad, value_rows, preferred_element_type=jnp.float32
    )
    value_part = jnp.einsum(
        "hqk,qhd->khd",
        attn_probs.astype(jnp.bfloat16),
        mixed_grad,
        preferred_element_type=jnp.float32,
    )
    inner_sum = jnp.sum(prob_grad * attn_probs, axis=-1, keepdims=True)
    score_grad = (attn_probs * (prob_grad - inner_sum)).astype(jnp.bfloat16)
    query_grad = (
        jnp.einsum("hqk,khd->qhd", score_grad, key_rows, preferred_element_type=jnp.float32)
        * score_scale
    )
    key_part = (
        jnp.einsum("hqk,qhd->khd", score_grad, query_rows, preferred_element_type=jnp.float32)
        * score_scale
    )
    return (query_grad.astype(jnp.bfloat16), key_part, value_part)


def plain_shards(
    block_input,
    cotangent,
    item_starts,
    item_lengths,
    pad_mask,
    ln1_gain,
    ln1_shift,
    w_qkv,
    w_out,
    ln2_gain,
    ln2_shift,
    w_up,
    up_bias,
    w_down,
    down_bias,
):
    rows_here, tok_count, model_width = block_input.shape
    seq_count = lax.axis_size("seq")
    shard_count = lax.axis_size("fsdp")
    length = tok_count * seq_count
    score_scale = HD ** (-0.5)
    piece_d = ln1_gain.shape[0]
    seq_first = lax.axis_index("seq") * tok_count
    packed = jnp.concatenate([ln1_gain, ln1_shift, ln2_gain, ln2_shift, down_bias, up_bias])
    vector_table = lax.all_gather(packed, "fsdp", axis=0, tiled=True).reshape(shard_count, -1)

    def vector_part(slot):
        return vector_table[:, slot * piece_d : (slot + 1) * piece_d].reshape(-1)

    gain_one, shift_one, gain_two, shift_two, bias_down = [vector_part(slot) for slot in range(5)]
    bias_up = vector_table[:, 5 * piece_d :].reshape(-1)
    qkv_full, out_full = (
        lax.all_gather(w_qkv, "fsdp", axis=0, tiled=True),
        lax.all_gather(w_out, "fsdp", axis=0, tiled=True),
    )
    inputs = block_input.reshape(rows_here * tok_count, model_width).astype(jnp.float32)
    normed_one = layer_norm(inputs, gain_one, shift_one).astype(jnp.bfloat16)
    projected = jnp.dot(normed_one, qkv_full, preferred_element_type=jnp.float32).astype(
        jnp.bfloat16
    )
    query_all = projected[:, :model_width].reshape(rows_here, tok_count, H, HD)
    kv_local = projected[:, model_width:].reshape(rows_here, tok_count, 2 * model_width)
    kv_whole = lax.all_gather(kv_local, "seq", axis=1, tiled=True)
    key_all = kv_whole[:, :, :model_width].reshape(rows_here, length, H, HD)
    value_all = kv_whole[:, :, model_width:].reshape(rows_here, length, H, HD)
    positions = jnp.arange(length, dtype=jnp.int32)
    query_pos = seq_first + jnp.arange(tok_count, dtype=jnp.int32)
    row_index = 0
    item_label = item_numbers(item_starts[row_index], item_lengths[row_index], positions)
    query_item = lax.dynamic_slice_in_dim(item_label, seq_first, tok_count)
    visible = visible_mask(query_pos, positions, query_item, item_label, pad_mask[row_index])
    mixed_part, log_total = attend_rows(
        query_all[row_index], key_all[row_index], value_all[row_index], visible, score_scale
    )
    visible_list = [visible]
    mixed_list = [mixed_part]
    logsum_list = [log_total]
    mixed_all = (
        jnp.stack(mixed_list).reshape(rows_here * tok_count, model_width).astype(jnp.bfloat16)
    )
    residual_one = inputs + jnp.dot(mixed_all, out_full, preferred_element_type=jnp.float32)
    up_full, down_full = (
        lax.all_gather(w_up, "fsdp", axis=0, tiled=True),
        lax.all_gather(w_down, "fsdp", axis=0, tiled=True),
    )
    normed_two = layer_norm(residual_one, gain_two, shift_two).astype(jnp.bfloat16)
    hidden_pre = jnp.dot(normed_two, up_full, preferred_element_type=jnp.float32) + bias_up
    activated = jax.nn.gelu(hidden_pre).astype(jnp.bfloat16)
    block_output = (
        residual_one + jnp.dot(activated, down_full, preferred_element_type=jnp.float32) + bias_down
    )
    output_shard = block_output.astype(jnp.bfloat16).reshape(rows_here, tok_count, model_width)
    up_full, down_full = (
        lax.all_gather(w_up, "fsdp", axis=0, tiled=True),
        lax.all_gather(w_down, "fsdp", axis=0, tiled=True),
    )
    cot_flat = cotangent.reshape(rows_here * tok_count, model_width)
    cot_wide = cot_flat.astype(jnp.float32)
    down_grad = contract_rows(activated, cot_flat)
    down_bias_part = jnp.sum(cot_wide, axis=0)
    act_grad = times_transpose(cot_flat, down_full)
    gelu_back = jax.vjp(jax.nn.gelu, hidden_pre)[1]
    hidden_grad = gelu_back(act_grad)[0].astype(jnp.bfloat16)
    up_grad = contract_rows(normed_two, hidden_grad)
    up_bias_part = jnp.sum(hidden_grad.astype(jnp.float32), axis=0)
    norm_two_grad = times_transpose(hidden_grad, up_full)
    norm_two_back = jax.vjp(layer_norm, residual_one, gain_two, shift_two)[1]
    resid_part, gain_two_grad, shift_two_grad = norm_two_back(norm_two_grad)
    residual_grad = cot_wide + resid_part
    up_sum, down_sum = (
        lax.psum_scatter(up_grad, "fsdp", scatter_dimension=0, tiled=True),
        lax.psum_scatter(down_grad, "fsdp", scatter_dimension=0, tiled=True),
    )
    qkv_full, out_full = (
        lax.all_gather(w_qkv, "fsdp", axis=0, tiled=True),
        lax.all_gather(w_out, "fsdp", axis=0, tiled=True),
    )
    branch_grad = residual_grad.astype(jnp.bfloat16)
    out_grad = contract_rows(mixed_all, branch_grad)
    mixed_grad = (
        times_transpose(branch_grad, out_full)
        .astype(jnp.bfloat16)
        .reshape(rows_here, tok_count, H, HD)
    )
    row_index = 0
    query_grad, key_part, value_part = attend_back(
        query_all[row_index],
        key_all[row_index],
        value_all[row_index],
        visible_list[row_index],
        logsum_list[row_index],
        mixed_grad[row_index],
        score_scale,
    )
    query_list = [query_grad.reshape(tok_count, model_width)]
    kv_list = [
        jnp.concatenate(
            [key_part.reshape(length, model_width), value_part.reshape(length, model_width)], axis=1
        )
    ]
    kv_terms = jnp.stack(kv_list)
    kv_grad = lax.psum_scatter(kv_terms, "seq", scatter_dimension=1, tiled=True).astype(
        jnp.bfloat16
    )
    proj_grad = jnp.concatenate(
        [
            jnp.stack(query_list).reshape(rows_here * tok_count, model_width),
            kv_grad.reshape(rows_here * tok_count, 2 * model_width),
        ],
        axis=1,
    )
    qkv_grad = contract_rows(normed_one, proj_grad)
    norm_one_grad = times_transpose(proj_grad, qkv_full)
    norm_one_back = jax.vjp(layer_norm, inputs, gain_one, shift_one)[1]
    input_part, gain_one_grad, shift_one_grad = norm_one_back(norm_one_grad)
    input_grad = (residual_grad + input_part).reshape(rows_here, tok_count, model_width)
    vector_grad = jnp.concatenate(
        [
            piece_grad.reshape(shard_count, -1)
            for piece_grad in (
                gain_one_grad,
                shift_one_grad,
                gain_two_grad,
                shift_two_grad,
                down_bias_part,
                up_bias_part,
            )
        ],
        axis=1,
    ).reshape(-1)
    qkv_sum, out_sum, vector_sum = (
        lax.psum_scatter(qkv_grad, "fsdp", scatter_dimension=0, tiled=True),
        lax.psum_scatter(out_grad, "fsdp", scatter_dimension=0, tiled=True),
        lax.psum_scatter(vector_grad, "fsdp", scatter_dimension=0, tiled=True),
    )
    up_total, down_total, qkv_total, out_total, vector_total = lax.psum(
        (up_sum, down_sum, qkv_sum, out_sum, vector_sum), "seq"
    )
    gain_one_out = vector_total[0:piece_d]
    shift_one_out = vector_total[piece_d : 2 * piece_d]
    gain_two_out = vector_total[2 * piece_d : 3 * piece_d]
    shift_two_out = vector_total[3 * piece_d : 4 * piece_d]
    down_bias_out = vector_total[4 * piece_d : 5 * piece_d]
    up_bias_out = vector_total[5 * piece_d :]
    return (
        output_shard,
        input_grad,
        gain_one_out,
        shift_one_out,
        qkv_total,
        out_total,
        gain_two_out,
        shift_two_out,
        up_total,
        up_bias_out,
        down_total,
        down_bias_out,
    )


def gather_small(vector, z_count):
    line = [vector]
    for j in range(1, z_count):
        line.append(lax.ppermute(vector, "z", [(i, (i + j) % z_count) for i in range(z_count)]))
    return line + [lax.ppermute(piece, "x", SWAP) for piece in line]


def gather_weight(shard, *others):
    near = lax.all_gather(shard, "z", axis=0, tiled=False)
    return [near, lax.ppermute(after(near, *others), "x", SWAP)]


def stage(flag, work, *args):
    shapes = jax.eval_shape(work, *args)

    def nothing(*_):
        return jax.tree.map(lambda a: jnp.zeros(a.shape, a.dtype), shapes)

    return lax.cond(flag, work, nothing, *args)


class Line:
    def __init__(self):
        self.last = ()

    def enter(self, value):
        return after(value, *self.last)

    def leave(self, *results):
        self.last = results[:1]
        return results


def after(value, *others):
    return lax.optimization_barrier((value,) + others)[0]


def seq_pieces(block, *others):
    return core_pieces(block, after(lax.ppermute(block, "y", SWAP), *others))


def core_pieces(block, other):
    return [block, lax.ppermute(block, "c", SWAP), other, lax.ppermute(other, "c", SWAP)]


def by_bit(bit, mine, theirs):
    return jnp.where(bit == 0, mine, theirs), jnp.where(bit == 0, theirs, mine)


def gather_tokens(block, yi, ci, *others):
    parts = seq_pieces(block, *others)
    near = by_bit(ci, parts[0], parts[1])
    far = by_bit(ci, parts[2], parts[3])
    rows = [jnp.where(yi == 0, n, f) for n, f in zip(near, far)]
    rows += [jnp.where(yi == 0, f, n) for n, f in zip(near, far)]
    return jnp.concatenate(rows, axis=0)


def core_sum(parts, yi):
    away, home = parts
    other = lax.ppermute(away, "c", SWAP)
    tokens, model = home.shape[0] // 2, home.shape[1]
    steps = 4
    block = (tokens // steps, model)

    def kernel(at_ref, *refs):
        wide = jnp.float32
        refs[4][...] = refs[0][...].astype(wide) + refs[1][...].astype(wide)
        refs[5][...] = (refs[2][...].astype(wide) + refs[3][...].astype(wide)).astype(
            jnp.bfloat16
        )

    here = pl.BlockSpec(block, lambda i, at: (at[0] * steps + i, 0))
    there = pl.BlockSpec(block, lambda i, at: ((1 - at[0]) * steps + i, 0))
    out = pl.BlockSpec(block, lambda i, at: (i, 0))
    return pl.pallas_call(
        kernel,
        grid_spec=pltpu.PrefetchScalarGridSpec(
            num_scalar_prefetch=1,
            grid=(steps,),
            in_specs=[here, here, there, there],
            out_specs=[out, out],
        ),
        out_shape=[
            jax.ShapeDtypeStruct((tokens, model), jnp.float32),
            jax.ShapeDtypeStruct((tokens, model), jnp.bfloat16),
        ],
        cost_estimate=cost(flops=0, bytes_accessed=7 * tokens * model, transcendentals=0),
        compiler_params=params(),
    )(jnp.reshape(yi, (1,)).astype(jnp.int32), home, other, home, other)


def home_sum(home, other):
    return home + other.astype(jnp.float32)


COST_SCALE = 0.01


def cost(flops, bytes_accessed, transcendentals):
    return pl.CostEstimate(
        flops=int(flops * COST_SCALE),
        bytes_accessed=int(bytes_accessed * COST_SCALE),
        transcendentals=int(transcendentals * COST_SCALE),
    )


def params(limit=VMEM_LIMIT):
    return pltpu.CompilerParams(vmem_limit_bytes=limit)


def weight_matmul(left, pieces, offsets, shape, back, body, extras, outs, chunk, groups=None):
    rows = left.shape[0]
    depth, width = shape
    out_width = depth if back else width
    steps = out_width // chunk
    n_pieces, n_extras = len(pieces), len(extras)
    blocks = [(p, k) for p, piece in enumerate(pieces) for k in range(piece.shape[0])]
    block_rows, block_cols = pieces[0].shape[1:]
    row_count, col_count = depth // block_rows, width // block_cols

    tables = (offsets,) if groups is None else (offsets, groups)

    def kernel(*refs):
        table_refs, left_ref, refs = refs[: len(tables)], refs[len(tables)], refs[len(tables) + 1 :]
        offs_ref = table_refs[0]
        piece_refs = refs[:n_pieces]
        extra_refs = refs[n_pieces : n_pieces + n_extras]
        out_refs = refs[n_pieces + n_extras : -2]
        held, sems = refs[-2:]
        step = pl.program_id(0)

        def slot(row, col):
            return sems.at[row, col]

        @pl.when(step == 0)
        def _():
            for b, (p, k) in enumerate(blocks):
                row, col = offs_ref[0, b], offs_ref[1, b]
                target = held.at[
                    pl.ds(pl.multiple_of(row * block_rows, block_rows), block_rows),
                    pl.ds(pl.multiple_of(col * block_cols, block_cols), block_cols),
                ]
                pltpu.make_async_copy(piece_refs[p].at[k], target, slot(row, col)).start()

        def arrive(row, col):
            target = held.at[
                pl.ds(row * block_rows, block_rows), pl.ds(col * block_cols, block_cols)
            ]
            pltpu.make_async_copy(piece_refs[0].at[0], target, slot(row, col)).wait()

        for n in range(steps):
            needed = [
                (row, col)
                for row in range(row_count)
                for col in range(col_count)
                if (
                    row * block_rows // chunk if back else col * block_cols // chunk
                ) == n
            ]
            if needed:

                @pl.when(step == n)
                def _():
                    for row, col in needed:
                        arrive(row, col)

        start = pl.ds(pl.multiple_of(step * chunk, chunk), chunk)

        def product(part):
            if back:
                return lax.dot_general(
                    part,
                    held[start, :],
                    (((1,), (1,)), ((), ())),
                    preferred_element_type=jnp.float32,
                )
            return jnp.dot(part, held[:, start], preferred_element_type=jnp.float32)

        if groups is None:
            body(product(left_ref[...]), extra_refs, out_refs)
        else:
            size = rows // groups.shape[0]
            each = out_refs[0].shape[0] // size
            for g in range(groups.shape[0]):
                at = pl.multiple_of(table_refs[1][g] * size, size)
                values = product(left_ref[pl.ds(at, size), :])
                to = (g % each) * size
                out_refs[g // each][to : to + size, :] = values.astype(jnp.bfloat16)

    def column_spec(array):
        return pl.BlockSpec((array.shape[0], chunk), lambda i, *tabs: (0, i))

    flops = 2 * rows * depth * width
    moved = 2 * (left.size + depth * width) + sum(
        a.size * a.dtype.itemsize for a in list(extras) + list(outs)
    )
    return pl.pallas_call(
        kernel,
        grid_spec=pltpu.PrefetchScalarGridSpec(
            num_scalar_prefetch=len(tables),
            grid=(steps,),
            in_specs=[
                pl.BlockSpec(
                    left.shape, lambda i, *tabs: (0, 0), pipeline_mode=pl.Buffered(1)
                )
            ]
            + [pl.BlockSpec(memory_space=pl.ANY)] * n_pieces
            + [column_spec(a) for a in extras],
            out_specs=[column_spec(a) for a in outs],
            scratch_shapes=[
                pltpu.VMEM((depth, width), jnp.bfloat16),
                pltpu.SemaphoreType.DMA((row_count, col_count)),
            ],
        ),
        out_shape=list(outs),
        cost_estimate=cost(flops=flops, bytes_accessed=moved, transcendentals=0),
        compiler_params=params(),
    )(*tables, left, *pieces, *extras)


def store_low(values, extra_refs, out_refs):
    out_refs[0][...] = values.astype(jnp.bfloat16)


def store_gelu(values, extra_refs, out_refs):
    hidden = values + extra_refs[0][...]
    square = hidden * hidden
    bend = jnp.tanh(GELU_A * hidden * (1.0 + GELU_B * square))
    half = 0.5 * (1.0 + bend)
    out_refs[0][...] = (hidden * half).astype(jnp.bfloat16)
    slope = half + 0.5 * hidden * (1.0 - bend * bend) * (
        GELU_A * (1.0 + 3.0 * GELU_B * square)
    )
    out_refs[1][...] = slope


def store_hidden_grad(values, extra_refs, out_refs):
    low = (values * extra_refs[0][...]).astype(jnp.bfloat16)
    out_refs[0][...] = low
    out_refs[1][...] = jnp.sum(low.astype(jnp.float32), axis=0, keepdims=True)


def weight_grad(left, right, where, count, block, width, addend=None, parts=1):
    rows = left.shape[0]
    part = width // parts
    added = () if addend is None else (addend,)

    def kernel(where_ref, left_ref, right_ref, *refs):
        for n in range(parts):
            cols = slice(n * part, (n + 1) * part)
            value = lax.dot_general(
                left_ref[...],
                right_ref[:, cols],
                (((0,), (0,)), ((), ())),
                preferred_element_type=jnp.float32,
            )
            if added:
                value = value + refs[0][0, :, cols].astype(jnp.float32)
            refs[len(added) + n][0] = value.astype(jnp.bfloat16)

    return pl.pallas_call(
        kernel,
        grid_spec=pltpu.PrefetchScalarGridSpec(
            num_scalar_prefetch=1,
            grid=(count,),
            in_specs=[
                pl.BlockSpec((rows, block), lambda k, at: (0, at[k])),
                pl.BlockSpec((rows, width), lambda k, at: (0, at[count])),
            ]
            + [pl.BlockSpec((1, block, width), lambda k, at: (k, 0, 0))] * len(added),
            out_specs=[pl.BlockSpec((1, block, part), lambda k, at: (k, 0, 0))] * parts,
        ),
        out_shape=[jax.ShapeDtypeStruct((count, block, part), jnp.bfloat16)] * parts,
        cost_estimate=cost(
            flops=2 * rows * count * block * width,
            bytes_accessed=2 * rows * (count * block + width) + 4 * count * block * width,
            transcendentals=0,
        ),
        compiler_params=params(),
    )(where, left, right, *added)


def slice_qkv(w_qkv, where, width):
    rows = w_qkv.shape[0]
    heads = H // 4

    def kernel(at_ref, from_ref, to_ref):
        for i in range(heads):
            col = pl.ds(pl.multiple_of((2 * i + at_ref[1]) * HD, HD), HD)
            to_ref[:, i * HD : (i + 1) * HD] = from_ref[:, col]

    part = heads * HD
    return pl.pallas_call(
        kernel,
        grid_spec=pltpu.PrefetchScalarGridSpec(
            num_scalar_prefetch=1,
            grid=(3,),
            in_specs=[pl.BlockSpec((rows, 2 * part), lambda g, at: (0, 2 * g + at[0]))],
            out_specs=pl.BlockSpec((rows, part), lambda g, at: (0, g)),
        ),
        out_shape=jax.ShapeDtypeStruct((rows, width), jnp.bfloat16),
        cost_estimate=cost(flops=0, bytes_accessed=3 << 20, transcendentals=0),
        compiler_params=params(),
    )(where, w_qkv)


def slice_weights(w_out, w_up, w_down, where, shard_count):
    rows, model = w_out.shape
    ff_part = w_down.shape[0] // 4
    steps = shard_count
    part = ff_part // steps
    up_half = steps // 2

    def kernel(at_ref, out_ref, up_ref, down_ref, out_to, low_to, high_to, left_to, right_to):
        step = pl.program_id(0)
        for n, up_to in enumerate((low_to, high_to)):

            @pl.when(step // up_half == n)
            def _():
                up_to[...] = up_ref[...]

        @pl.when(step == 0)
        def _():
            out_to[...] = out_ref[...]

        left_to[...] = down_ref[:, : model // 2]
        right_to[...] = down_ref[:, model // 2 :]

    def up_spec(n):
        return pl.BlockSpec(
            (rows, ff_part), lambda i, at: (0, jnp.clip(i - n * up_half, 0, up_half - 1))
        )

    return pl.pallas_call(
        kernel,
        grid_spec=pltpu.PrefetchScalarGridSpec(
            num_scalar_prefetch=1,
            grid=(steps,),
            in_specs=[
                pl.BlockSpec((rows // 2, model // 2), lambda i, at: (at[1], at[0])),
                pl.BlockSpec((rows, ff_part), lambda i, at: (0, 4 * i + 2 * at[0] + at[1])),
                pl.BlockSpec(
                    (part, model), lambda i, at: ((2 * at[0] + at[1]) * steps + i, 0)
                ),
            ],
            out_specs=[
                pl.BlockSpec((rows // 2, model // 2), lambda i, at: (0, 0)),
                up_spec(0),
                up_spec(1),
                pl.BlockSpec((part, model // 2), lambda i, at: (i, 0)),
                pl.BlockSpec((part, model // 2), lambda i, at: (i, 0)),
            ],
        ),
        out_shape=[
            jax.ShapeDtypeStruct(shape, jnp.bfloat16)
            for shape in [(rows // 2, model // 2)]
            + [(rows, ff_part * up_half)] * 2
            + [(ff_part, model // 2)] * 2
        ],
        cost_estimate=cost(flops=0, bytes_accessed=9 << 20, transcendentals=0),
        compiler_params=params(),
    )(where, w_out, w_up, w_down)


def visible_tile(query_item, key_item, first_query, n_query, n_key):
    query_pos = first_query + lax.broadcasted_iota(jnp.int32, (n_query, n_key), 0)
    key_pos = lax.broadcasted_iota(jnp.int32, (n_query, n_key), 1)
    return ((query_item == key_item) & (key_pos < query_pos)) | (key_pos == query_pos)


def head_spec(length, first):
    return pl.BlockSpec((length, HD), lambda h: (0, first + h))


def attention(projected, query_item, key_item, heads, tile):
    length = projected.shape[0]
    scale = HD ** (-0.5)

    def kernel(q_ref, k_ref, v_ref, qi_ref, ki_ref, mixed_ref, log_ref):
        for start in range(0, length, tile):
            stop = start + tile
            rows = slice(start, stop)
            scores = (
                lax.dot_general(
                    q_ref[rows, :],
                    k_ref[:stop, :],
                    (((1,), (1,)), ((), ())),
                    preferred_element_type=jnp.float32,
                )
                * scale
            )
            seen = visible_tile(qi_ref[rows, :], ki_ref[:, :stop], start, tile, stop)
            scores = jnp.where(seen, scores, MASKED)
            peak = jnp.max(scores, axis=-1, keepdims=True)
            weights = jnp.exp(scores - peak)
            total = jnp.sum(weights, axis=-1, keepdims=True)
            probs = (weights * (1.0 / total)).astype(jnp.bfloat16)
            mixed_ref[rows, :] = jnp.dot(
                probs, v_ref[:stop, :], preferred_element_type=jnp.float32
            ).astype(jnp.bfloat16)
            log_ref[0, rows, :] = peak + jnp.log(total)

    whole = lambda rows, cols: pl.BlockSpec((rows, cols), lambda h: (0, 0))
    return pl.pallas_call(
        kernel,
        grid=(heads,),
        in_specs=[head_spec(length, g * heads) for g in range(3)]
        + [whole(length, 1), whole(1, length)],
        out_specs=[head_spec(length, 0), pl.BlockSpec((1, length, 1), lambda h: (h, 0, 0))],
        out_shape=[
            jax.ShapeDtypeStruct((length, heads * HD), jnp.bfloat16),
            jax.ShapeDtypeStruct((heads, length, 1), jnp.float32),
        ],
        cost_estimate=cost(
            flops=4 * heads * length * length * HD,
            bytes_accessed=8 * length * heads * HD,
            transcendentals=heads * length * length,
        ),
        compiler_params=params(),
    )(projected, projected, projected, query_item, key_item)


def attention_back(projected, mixed_grad, log_total, query_item, key_item, heads, tile):
    length = projected.shape[0]
    scale = HD ** (-0.5)

    def kernel(q_ref, k_ref, v_ref, g_ref, log_ref, qi_ref, ki_ref, grad_ref, dk_ref, dv_ref):
        head = pl.program_id(0)

        def place(group):
            return pl.ds(pl.multiple_of((group * heads + head) * HD, HD), HD)

        for start in reversed(range(0, length, tile)):
            stop = start + tile
            rows = slice(start, stop)
            query, grad = q_ref[rows, :], g_ref[rows, :]
            key, value = k_ref[:stop, :], v_ref[:stop, :]
            scores = (
                lax.dot_general(
                    query, key, (((1,), (1,)), ((), ())), preferred_element_type=jnp.float32
                )
                * scale
            )
            seen = visible_tile(qi_ref[rows, :], ki_ref[:, :stop], start, tile, stop)
            probs = jnp.exp(jnp.where(seen, scores, MASKED) - log_ref[0, rows, :])
            prob_grad = lax.dot_general(
                grad, value, (((1,), (1,)), ((), ())), preferred_element_type=jnp.float32
            )
            inner = jnp.sum(prob_grad * probs, axis=-1, keepdims=True)
            score_grad = (probs * (prob_grad - inner)).astype(jnp.bfloat16)
            grad_ref[rows, place(0)] = (
                jnp.dot(score_grad, key, preferred_element_type=jnp.float32) * scale
            ).astype(jnp.bfloat16)
            key_part = lax.dot_general(
                score_grad, query, (((0,), (0,)), ((), ())), preferred_element_type=jnp.float32
            )
            value_part = lax.dot_general(
                probs.astype(jnp.bfloat16),
                grad,
                (((0,), (0,)), ((), ())),
                preferred_element_type=jnp.float32,
            )
            if stop == length:
                dk_ref[...] = key_part
                dv_ref[...] = value_part
            else:
                dk_ref[:stop, :] += key_part
                dv_ref[:stop, :] += value_part
        grad_ref[:, place(1)] = (dk_ref[...] * scale).astype(jnp.bfloat16)
        grad_ref[:, place(2)] = dv_ref[...].astype(jnp.bfloat16)

    whole = lambda rows, cols: pl.BlockSpec((rows, cols), lambda h: (0, 0))
    return pl.pallas_call(
        kernel,
        grid=(heads,),
        in_specs=[head_spec(length, g * heads) for g in range(3)]
        + [
            head_spec(length, 0),
            pl.BlockSpec((1, length, 1), lambda h: (h, 0, 0)),
            whole(length, 1),
            whole(1, length),
        ],
        out_specs=whole(length, 3 * heads * HD),
        out_shape=jax.ShapeDtypeStruct((length, 3 * heads * HD), jnp.bfloat16),
        scratch_shapes=[pltpu.VMEM((length, HD), jnp.float32)] * 2,
        cost_estimate=cost(
            flops=10 * heads * length * length * HD,
            bytes_accessed=16 * length * heads * HD,
            transcendentals=heads * length * length,
        ),
        compiler_params=params(),
    )(projected, projected, projected, mixed_grad, log_total, query_item, key_item)


def widen(chunks, places, grid, piece_specs, out_block, out_index, out_shape, write):
    def kernel(place_ref, *refs):
        for n in range(len(chunks)):
            for r in range(4):
                write(n, place_ref[r], refs[4 * n + r], refs[-1])

    return pl.pallas_call(
        kernel,
        grid_spec=pltpu.PrefetchScalarGridSpec(
            num_scalar_prefetch=1,
            grid=(grid,),
            in_specs=[
                pl.BlockSpec(block, functools.partial(lambda at, i, pos: at(i), at))
                for block, at in piece_specs
                for _ in range(4)
            ],
            out_specs=pl.BlockSpec(out_block, lambda i, pos: out_index(i)),
        ),
        out_shape=jax.ShapeDtypeStruct(out_shape, jnp.float32),
        cost_estimate=cost(
            flops=0, bytes_accessed=6 * int(np.prod(out_shape)), transcendentals=0
        ),
        compiler_params=params(),
    )(places, *[piece for pieces in chunks for piece in pieces])


def widen_columns(pieces, places, blocks):
    rows, width = pieces[0].shape
    part = width // blocks

    def write(n, pos, piece, out):
        out[:, pl.ds(pl.multiple_of(pos * part, part), part)] = piece[...].astype(jnp.float32)

    return widen(
        [pieces],
        places,
        blocks,
        [((rows, part), lambda i: (0, i))],
        (rows, 4 * part),
        lambda i: (0, i),
        (rows, 4 * width),
        write,
    )


def widen_rows(pieces, places):
    rows, width = pieces[0].shape

    def write(n, pos, piece, out):
        @pl.when(pos == pl.program_id(0))
        def _():
            out[...] = piece[...].astype(jnp.float32)

    return widen(
        [pieces],
        places,
        4,
        [((rows, width), lambda i: (0, 0))],
        (rows, width),
        lambda i: (i, 0),
        (4 * rows, width),
        write,
    )


def widen_heads(pieces, places):
    rows, width = pieces[0].shape
    part = width // 3

    def write(n, pos, piece, out):
        first = lax.div(pos, 2) * part * 2 + lax.rem(pos, 2) * HD
        for i in range(part // HD):
            cols = pl.ds(pl.multiple_of(first + 2 * i * HD, HD), HD)
            out[:, cols] = piece[:, i * HD : (i + 1) * HD].astype(jnp.float32)

    return widen(
        [pieces],
        places,
        3,
        [((rows, part), lambda i: (0, i))],
        (rows, 4 * part),
        lambda i: (0, i),
        (rows, 4 * width),
        write,
    )


def widen_quarters(pieces, places):
    rows, width = pieces[0].shape

    def write(n, pos, piece, out):
        row = pl.multiple_of(lax.rem(pos, 2) * rows, rows)
        col = pl.multiple_of(lax.div(pos, 2) * width, width)
        out[pl.ds(row, rows), pl.ds(col, width)] = piece[...].astype(jnp.float32)

    return widen(
        [pieces],
        places,
        1,
        [((rows, width), lambda i: (0, 0))],
        (2 * rows, 2 * width),
        lambda i: (0, 0),
        (2 * rows, 2 * width),
        write,
    )


def norm_back(values, gain_vec, incoming):
    center = values - jnp.mean(values, axis=-1, keepdims=True)
    spread = jnp.mean(center * center, axis=-1, keepdims=True)
    inverse = lax.rsqrt(spread + EPSILON)
    unit = center * inverse
    scaled = incoming * gain_vec
    inner = jnp.mean(scaled * unit, axis=-1, keepdims=True)
    grad = (scaled - jnp.mean(scaled, axis=-1, keepdims=True) - unit * inner) * inverse
    return grad, jnp.sum(incoming * unit, axis=0), jnp.sum(incoming, axis=0)


def split_shards(
    block_input,
    cotangent,
    item_starts,
    item_lengths,
    pad_mask,
    ln1_gain,
    ln1_shift,
    w_qkv,
    w_out,
    ln2_gain,
    ln2_shift,
    w_up,
    up_bias,
    w_down,
    down_bias,
):
    low, wide = jnp.bfloat16, jnp.float32
    z_count = lax.axis_size("z")
    shard_count = 2 * z_count
    zi, xi, yi, ci = [lax.axis_index(name) for name in ("z", "x", "y", "c")]
    si = 2 * yi + ci
    tok_count, model = block_input.shape[1:]
    length = 4 * tok_count
    piece_d, ff_piece = ln1_gain.shape[0], up_bias.shape[0]
    ff_part = ff_piece // 4
    ff_here = ff_part * shard_count
    heads = H // 4
    places = jnp.stack([jnp.bitwise_xor(si, r) for r in range(4)]).astype(jnp.int32)

    packed = jnp.concatenate([ln1_gain, ln1_shift, ln2_gain, ln2_shift, down_bias, up_bias])
    vector_stack = jnp.stack(gather_small(packed, z_count))
    owners = jnp.stack(
        [
            lax.rem(zi - j + z_count, z_count) * 2 + jnp.bitwise_xor(xi, dx)
            for dx in range(2)
            for j in range(z_count)
        ]
    )
    hit = owners[None, :] == jnp.arange(shard_count, dtype=jnp.int32)[:, None]
    vector_table = jnp.sum(jnp.where(hit[:, :, None], vector_stack[None], 0.0), axis=1)

    def vector_part(slot):
        return vector_table[:, slot * piece_d : (slot + 1) * piece_d].reshape(-1)

    gain_one, shift_one, gain_two, shift_two, bias_down = [vector_part(slot) for slot in range(5)]
    bias_up = lax.dynamic_index_in_dim(
        vector_table[:, 5 * piece_d :].reshape(shard_count, 4, ff_part), si, 1, keepdims=False
    ).reshape(1, ff_here)

    line = Line()
    flag = item_lengths[0, 0] > 0
    where = jnp.stack([yi, ci]).astype(jnp.int32)
    qkv_slice = slice_qkv(w_qkv, where, 3 * heads * HD)
    slices = slice_weights(w_out, w_up, w_down, after(where, qkv_slice), shard_count)
    half = model // 2
    qkv_width = 3 * heads * HD
    qkv_parts = gather_weight(qkv_slice)
    down_pair = jnp.stack([slices[4], lax.ppermute(slices[4], "x", SWAP)])
    inputs = after(block_input, down_pair).reshape(tok_count, model).astype(wide)
    normed_one = layer_norm(inputs, gain_one, shift_one).astype(low)
    out_parts = gather_weight(after(slices[0], normed_one), qkv_parts[1])
    out_parts = out_parts + [lax.ppermute(piece, "y", SWAP) for piece in out_parts]

    near_blocks = [2 * z + xi for z in range(z_count)]
    far_blocks = [2 * z + 1 - xi for z in range(z_count)]
    split = near_blocks + far_blocks
    paired = [b for pair in zip(near_blocks, far_blocks) for b in pair]
    zero = jnp.zeros_like(xi)

    def table(*rows):
        return jnp.stack([jnp.stack(row) for row in rows]).astype(jnp.int32)

    qkv_offsets = table(split, [zero] * shard_count)
    up_offsets = table(split + split, [zero] * shard_count + [zero + 1] * shard_count)
    down_offsets = table(split + paired, [zero] * shard_count + [zero + 1] * shard_count)
    out_offsets = table(split + split, [yi] * shard_count + [1 - yi] * shard_count)

    def blocks_at(blocks, n):
        return table(blocks + [zero + n])[0]

    def sum_small(terms, *others):
        def term(j):
            return lax.dynamic_index_in_dim(
                terms, lax.rem(zi - j + z_count, z_count), 0, keepdims=False
            )

        total = term(0).astype(wide)
        for j in range(1, z_count):
            theirs = lax.ppermute(
                term(j), "z", [(i, (i - j) % z_count) for i in range(z_count)]
            )
            total = total + after(theirs, *others).astype(wide)
        return total

    def plain_matmul(left, pieces, offsets, shape, back, body, extras, outs):
        return weight_matmul(left, pieces, offsets, shape, back, body, extras, outs, 512)

    def row_groups(left, pieces, offsets, shape_, back):
        groups = jnp.stack([1 - ci, 3 - ci, ci, 2 + ci]).astype(jnp.int32)
        outs = (shape(2 * tok_count, shape_[0] if back else shape_[1]),) * 2
        return weight_matmul(left, pieces, offsets, shape_, back, None, (), outs, 512, groups)

    def matmul(left, *others):
        return line.leave(*plain_matmul(line.enter(left), *others))

    def grad_chunk(left, right, blocks, n, block, width):
        return line.leave(
            *weight_grad(line.enter(left), right, blocks_at(blocks, n), len(blocks), block, width)
        )[0]

    def far_terms(left, right, block):
        terms = grad_chunk(left, right, far_blocks, 0, block, right.shape[1])
        return lax.ppermute(terms, "x", SWAP)

    def near_terms(left, right, block, addend, parts=1):
        return weight_grad(
            left, right, blocks_at(near_blocks, 0), z_count, block, addend.shape[2], addend, parts
        )

    def sum_over_z(total):
        return lax.psum_scatter(total, "z", scatter_dimension=0, tiled=False)

    def shape(rows, cols, kind=low):
        return jax.ShapeDtypeStruct((rows, cols), kind)

    normed_one = gather_tokens(normed_one, yi, ci, qkv_parts[0])
    cot_flat = after(cotangent.reshape(tok_count, model), normed_one)
    cot_wide = cot_flat.astype(wide)
    cot_all = gather_tokens(cot_flat, yi, ci)
    (projected,) = matmul(
        after(normed_one, cot_all),
        qkv_parts,
        qkv_offsets,
        (model, qkv_width),
        False,
        store_low,
        (),
        (shape(length, qkv_width),),
    )
    up_parts = gather_weight(slices[1], projected)
    up_high = lax.all_gather(slices[2], "z", axis=0, tiled=False)
    down_parts = gather_weight(slices[3], projected)
    down_parts.append(lax.all_gather(down_pair, "z", axis=0, tiled=True))
    positions = jnp.arange(length, dtype=jnp.int32)
    item_label = item_numbers(item_starts[0], item_lengths[0], positions)
    query_item = item_label[:, None]
    key_item = jnp.where((item_label >= 0) & (pad_mask[0] == 1), item_label, -2)[None, :]
    mixed_heads, log_total = line.leave(
        *attention(line.enter(projected), query_item, key_item, heads, 256)
    )

    def attend_out(mixed_heads):
        halves = mixed_heads.reshape(2, 2 * tok_count, heads * HD)
        away = lax.dynamic_index_in_dim(halves, 1 - yi, 0, keepdims=False)
        mine = lax.dynamic_index_in_dim(halves, yi, 0, keepdims=False)
        other = lax.ppermute(away, "y", SWAP)
        mixed = jnp.concatenate(by_bit(yi, mine, other), axis=1)
        (out_partial,) = plain_matmul(
            mixed,
            out_parts,
            out_offsets,
            (half, model),
            False,
            store_low,
            (),
            (shape(2 * tok_count, model),),
        )
        halves = out_partial.reshape(2, tok_count, model)
        away = lax.dynamic_index_in_dim(halves, 1 - ci, 0, keepdims=False)
        home = lax.dynamic_index_in_dim(halves, ci, 0, keepdims=False)
        residual_one = (
            inputs + home.astype(wide) + lax.ppermute(away, "c", SWAP).astype(wide)
        )
        normed_two = layer_norm(residual_one, gain_two, shift_two).astype(low)
        return normed_two, residual_one, mine, other

    up_parts += [up_high, lax.ppermute(after(up_high, mixed_heads), "x", SWAP)]
    normed_two, residual_one, mixed_home, mixed_other = line.leave(
        *stage(flag, attend_out, after(line.enter(mixed_heads), up_parts[0], up_high))
    )
    normed_two = gather_tokens(normed_two, yi, ci, up_parts[1], up_parts[3])
    activated, slope = matmul(
        normed_two,
        up_parts,
        up_offsets,
        (model, ff_here),
        False,
        store_gelu,
        (bias_up,),
        (shape(length, ff_here), shape(length, ff_here, wide)),
    )

    mixed_last = lax.ppermute(after(mixed_home, activated), "y", SWAP)
    others_heads = jnp.concatenate(by_bit(yi, mixed_other, mixed_last), axis=0)
    mixed = jnp.concatenate(by_bit(yi, mixed_heads, others_heads), axis=1)

    down_bias_part = jnp.sum(cot_wide, axis=0)
    down_sum = grad_chunk(
        after(activated, down_parts[1], mixed), cot_all, paired, 0, ff_part, model
    )
    down_pair = lax.psum_scatter(
        down_sum.reshape(z_count, 2, ff_part, model), "z", scatter_dimension=0, tiled=False
    )
    hidden_grad, up_bias_part = matmul(
        cot_all,
        down_parts,
        down_offsets,
        (ff_here, model),
        True,
        store_hidden_grad,
        (slope,),
        (shape(length, ff_here), shape(1, ff_here, wide)),
    )
    up_far = far_terms(normed_two, hidden_grad, piece_d)
    norm_two_parts = line.leave(
        *row_groups(line.enter(hidden_grad), up_parts, up_offsets, (model, ff_here), True)
    )

    def norm_two_back(*norm_two_parts):
        home, away = core_sum(norm_two_parts, yi)
        other = lax.ppermute(away, "y", SWAP)
        feed_parts = row_groups(
            after(activated, away), down_parts, down_offsets, (ff_here, model), False
        )
        norm_two_grad = home_sum(home, after(other, *feed_parts))
        resid_part, gain_two_grad, shift_two_grad = norm_back(
            residual_one, gain_two, norm_two_grad
        )
        residual_grad = cot_wide + resid_part
        branch_grad = residual_grad.astype(low)
        branch_pair = jnp.concatenate(
            by_bit(ci, branch_grad, lax.ppermute(branch_grad, "c", SWAP)), axis=0
        )
        return branch_pair, residual_grad, gain_two_grad, shift_two_grad, feed_parts

    branch_pair, residual_grad, gain_two_grad, shift_two_grad, feed_parts = line.leave(
        *stage(flag, norm_two_back, line.enter(norm_two_parts[0]), norm_two_parts[1])
    )

    out_blocks = far_blocks + near_blocks

    def out_back(branch_pair):
        (mixed_grad_pair,) = plain_matmul(
            branch_pair,
            out_parts,
            out_offsets,
            (half, model),
            True,
            store_low,
            (),
            (shape(2 * tok_count, half),),
        )
        part = heads * HD
        away = lax.dynamic_slice_in_dim(mixed_grad_pair, (1 - yi) * part, part, 1)
        home = lax.dynamic_slice_in_dim(mixed_grad_pair, yi * part, part, 1)
        theirs = lax.ppermute(away, "y", SWAP)
        feed_home, feed_away = core_sum([after(feed_parts[0], away), feed_parts[1]], yi)
        pair = after(branch_pair, away)
        branch_away = lax.dynamic_slice_in_dim(pair, (1 - yi) * half, half, 1)
        branch_home = lax.dynamic_slice_in_dim(pair, yi * half, half, 1)
        theirs = after(theirs, feed_away, branch_away, branch_home)
        mixed_grad = jnp.concatenate(by_bit(yi, home, theirs), axis=0)
        return mixed_grad, feed_home, feed_away, branch_away, branch_home

    mixed_grad, feed_home, feed_away, branch_away, branch_home = line.leave(
        *stage(flag, out_back, line.enter(branch_pair))
    )
    branch_other = lax.ppermute(after(branch_away, mixed_grad), "y", SWAP)
    branch_all = jnp.concatenate(by_bit(yi, branch_home, branch_other), axis=0)
    (proj_grad,) = line.leave(
        attention_back(
            projected,
            line.enter(mixed_grad),
            log_total,
            query_item,
            key_item,
            heads,
            256,
        )
    )
    qkv_far = far_terms(normed_one, proj_grad, piece_d)
    (up_sum,) = line.leave(
        near_terms(
            line.enter(after(normed_two, branch_other)), hidden_grad, piece_d, up_far
        )[0]
    )
    up_shard = sum_over_z(after(up_sum, down_pair))
    norm_one_parts = line.leave(
        *row_groups(line.enter(proj_grad), qkv_parts, qkv_offsets, (model, qkv_width), True)
    )
    out_sum = line.leave(
        *weight_grad(
            line.enter(mixed),
            branch_all,
            blocks_at(out_blocks, 0),
            shard_count,
            piece_d // 2,
            half,
        )
    )[0]
    feed_other = lax.ppermute(after(feed_away, up_sum), "y", SWAP)

    def norm_one_back(*norm_one_parts):
        home, away = core_sum(norm_one_parts, yi)
        away = lax.ppermute(away, "y", SWAP)
        norm_one_grad = home_sum(home, away)
        input_part, gain_one_grad, shift_one_grad = norm_back(inputs, gain_one, norm_one_grad)
        input_grad = (residual_grad + input_part).reshape(1, tok_count, model)
        return input_grad, gain_one_grad, shift_one_grad

    input_grad, gain_one_grad, shift_one_grad = line.leave(
        *stage(flag, norm_one_back, after(line.enter(norm_one_parts[0]), feed_other), norm_one_parts[1])
    )
    (qkv_sum,) = line.leave(
        *near_terms(line.enter(after(normed_one, up_shard)), proj_grad, piece_d, qkv_far)
    )
    qkv_shard = sum_over_z(qkv_sum)

    def ends(up_shard):
        up_other = lax.ppermute(up_shard, "y", SWAP)
        down_far = lax.ppermute(down_pair[1], "x", SWAP)
        output_shard = (residual_one + home_sum(feed_home, feed_other) + bias_down).astype(low)
        output_shard = output_shard.reshape(1, tok_count, model)
        down_shard = (down_pair[0].astype(wide) + down_far.astype(wide)).astype(low)
        return output_shard, down_shard, up_other

    output_shard, down_shard, up_other = line.leave(
        *stage(flag, ends, line.enter(up_shard))
    )

    def more_ends(down_shard):
        up_bias_grad = jnp.where(
            (jnp.arange(4, dtype=jnp.int32) == si)[None, :, None],
            up_bias_part.reshape(shard_count, 1, ff_part),
            0.0,
        ).reshape(shard_count, ff_piece)
        vector_grad = jnp.concatenate(
            [
                part.reshape(shard_count, -1)
                for part in (
                    gain_one_grad,
                    shift_one_grad,
                    gain_two_grad,
                    shift_two_grad,
                    down_bias_part,
                    up_bias_grad,
                )
            ],
            axis=1,
        )
        vector_grad = vector_grad + lax.ppermute(vector_grad, "c", SWAP)
        vector_other = lax.ppermute(vector_grad, "y", SWAP)
        down_other = lax.ppermute(down_shard, "y", SWAP)
        out_away = lax.ppermute(out_sum[:z_count], "x", SWAP)
        up_total = widen_columns(core_pieces(up_shard, up_other), places, shard_count)
        out_both = (out_sum[z_count:].astype(wide) + out_away.astype(wide)).astype(low)
        vector_grad = vector_grad + after(vector_other, up_total)
        return out_both, up_total, after(down_other, up_total), vector_grad

    out_both, up_total, down_other, vector_grad = stage(
        flag, more_ends, after(line.enter(down_shard), down_shard)
    )
    out_shard = sum_over_z(after(out_both, qkv_sum))

    def last(qkv_shard):
        other = lax.ppermute(qkv_shard, "y", SWAP)
        vector_pair = vector_grad.reshape(z_count, 2, -1)
        away = lax.dynamic_index_in_dim(vector_pair, 1 - xi, 1, keepdims=False)
        home = lax.dynamic_index_in_dim(vector_pair, xi, 1, keepdims=False)
        vector_other = lax.ppermute(away, "x", SWAP)
        down_total = widen_rows(core_pieces(down_shard, down_other), places)
        vector_sum = home + after(vector_other, down_total)
        qkv_pieces = core_pieces(qkv_shard, after(other, vector_sum))
        return widen_heads(qkv_pieces, places), down_total, vector_sum

    qkv_total, down_total, vector_sum = stage(flag, last, after(qkv_shard, up_total))
    out_total = widen_quarters(seq_pieces(after(out_shard, qkv_total)), places)
    vector_total = sum_small(after(vector_sum, qkv_total))
    vectors = [vector_total[slot * piece_d : (slot + 1) * piece_d] for slot in range(5)]
    return (
        output_shard,
        input_grad,
        vectors[0],
        vectors[1],
        qkv_total,
        out_total,
        vectors[2],
        vectors[3],
        up_total,
        vector_total[5 * piece_d :],
        down_total,
        vectors[4],
    )


def solution(mesh):
    shard_count, seq_count = mesh.shape["fsdp"], mesh.shape["seq"]

    def step(*args):
        model, hidden = args[0].shape[2], args[12].shape[0]
        rows_each = args[0].shape[0] // shard_count
        if (
            rows_each == 1
            and seq_count == 4
            and model // shard_count == 2 * HD
            and hidden // (4 * shard_count) % 256 == 0
        ):
            fsdp, seq = ("z", "x"), ("y", "c")
            devices = mesh.devices.reshape(shard_count // 2, 2, 2, 2)
            inner, body = Mesh(devices, fsdp + seq), split_shards
        else:
            fsdp, seq = "fsdp", "seq"
            inner, body = mesh, plain_shards
        rows, tokens = P(fsdp, None), P(fsdp, seq, None)
        vector = P(fsdp)
        placed = (tokens, tokens, rows, rows, rows, vector, vector, rows, rows)
        placed += (vector, vector, rows, vector, rows, vector)
        given = (tokens, tokens, vector, vector, rows, rows, vector, vector)
        given += (rows, vector, rows, vector)
        return jax.shard_map(
            body, mesh=inner, in_specs=placed, out_specs=given, check_vma=False
        )(*args)

    return step
```

```python
import functools

import jax
import jax.numpy as jnp
import numpy as np
from jax import lax
from jax.experimental import pallas as pl
from jax.experimental.pallas import tpu as pltpu
from jax.sharding import Mesh
from jax.sharding import PartitionSpec as P

H = 16
HD = 128


EPSILON = 1e-05
MASKED = -1e30
SWAP = ((0, 1), (1, 0))
VMEM_LIMIT = 56 << 20
GELU_A = float(np.sqrt(2.0 / np.pi))
GELU_B = 0.044715


def layer_norm(values, gain_vec, shift_vec):
    center = values - jnp.mean(values, axis=-1, keepdims=True)
    spread = jnp.mean(center * center, axis=-1, keepdims=True)
    return center * lax.rsqrt(spread + EPSILON) * gain_vec + shift_vec


def contract_rows(left, right):
    return lax.dot_general(
        left, right, (((0,), (0,)), ((), ())), preferred_element_type=jnp.float32
    )


def times_transpose(left, right):
    return lax.dot_general(
        left, right, (((1,), (1,)), ((), ())), preferred_element_type=jnp.float32
    )


def item_numbers(starts, lengths, positions):
    inside = (positions[None, :] >= starts[:, None]) & (
        positions[None, :] < (starts + lengths)[:, None]
    )
    labels = jnp.arange(1, starts.shape[0] + 1, dtype=jnp.int32)
    return jnp.sum(jnp.where(inside, labels[:, None], 0), axis=0) - 1


def visible_mask(query_pos, key_pos, query_item, key_item, key_pad):
    same_item = (query_item[:, None] == key_item[None, :]) & (query_item[:, None] >= 0)
    before = key_pos[None, :] < query_pos[:, None]
    return same_item & before & (key_pad[None, :] == 1) | (key_pos[None, :] == query_pos[:, None])


def masked_scores(query_rows, key_rows, visible, score_scale):
    scores = (
        jnp.einsum("qhd,khd->hqk", query_rows, key_rows, preferred_element_type=jnp.float32)
        * score_scale
    )
    return jnp.where(visible[None], scores, MASKED)


def attend_rows(query_rows, key_rows, value_rows, visible, score_scale):
    scores = masked_scores(query_rows, key_rows, visible, score_scale)
    row_peak = jnp.max(scores, axis=-1, keepdims=True)
    exp_scores = jnp.exp(scores - row_peak)
    row_total = jnp.sum(exp_scores, axis=-1, keepdims=True)
    attn_probs = exp_scores / row_total
    mixed_rows = jnp.einsum(
        "hqk,khd->qhd",
        attn_probs.astype(jnp.bfloat16),
        value_rows,
        preferred_element_type=jnp.float32,
    )
    return (mixed_rows, row_peak + jnp.log(row_total))


def attend_back(query_rows, key_rows, value_rows, visible, log_total, mixed_grad, score_scale):
    scores = masked_scores(query_rows, key_rows, visible, score_scale)
    attn_probs = jnp.exp(scores - log_total)
    prob_grad = jnp.einsum(
        "qhd,khd->hqk", mixed_grad, value_rows, preferred_element_type=jnp.float32
    )
    value_part = jnp.einsum(
        "hqk,qhd->khd",
        attn_probs.astype(jnp.bfloat16),
        mixed_grad,
        preferred_element_type=jnp.float32,
    )
    inner_sum = jnp.sum(prob_grad * attn_probs, axis=-1, keepdims=True)
    score_grad = (attn_probs * (prob_grad - inner_sum)).astype(jnp.bfloat16)
    query_grad = (
        jnp.einsum("hqk,khd->qhd", score_grad, key_rows, preferred_element_type=jnp.float32)
        * score_scale
    )
    key_part = (
        jnp.einsum("hqk,qhd->khd", score_grad, query_rows, preferred_element_type=jnp.float32)
        * score_scale
    )
    return (query_grad.astype(jnp.bfloat16), key_part, value_part)


def plain_shards(
    block_input,
    cotangent,
    item_starts,
    item_lengths,
    pad_mask,
    ln1_gain,
    ln1_shift,
    w_qkv,
    w_out,
    ln2_gain,
    ln2_shift,
    w_up,
    up_bias,
    w_down,
    down_bias,
):
    rows_here, tok_count, model_width = block_input.shape
    seq_count = lax.axis_size("seq")
    shard_count = lax.axis_size("fsdp")
    length = tok_count * seq_count
    score_scale = HD ** (-0.5)
    piece_d = ln1_gain.shape[0]
    seq_first = lax.axis_index("seq") * tok_count
    packed = jnp.concatenate([ln1_gain, ln1_shift, ln2_gain, ln2_shift, down_bias, up_bias])
    vector_table = lax.all_gather(packed, "fsdp", axis=0, tiled=True).reshape(shard_count, -1)

    def vector_part(slot):
        return vector_table[:, slot * piece_d : (slot + 1) * piece_d].reshape(-1)

    gain_one, shift_one, gain_two, shift_two, bias_down = [vector_part(slot) for slot in range(5)]
    bias_up = vector_table[:, 5 * piece_d :].reshape(-1)
    qkv_full, out_full = (
        lax.all_gather(w_qkv, "fsdp", axis=0, tiled=True),
        lax.all_gather(w_out, "fsdp", axis=0, tiled=True),
    )
    inputs = block_input.reshape(rows_here * tok_count, model_width).astype(jnp.float32)
    normed_one = layer_norm(inputs, gain_one, shift_one).astype(jnp.bfloat16)
    projected = jnp.dot(normed_one, qkv_full, preferred_element_type=jnp.float32).astype(
        jnp.bfloat16
    )
    query_all = projected[:, :model_width].reshape(rows_here, tok_count, H, HD)
    kv_local = projected[:, model_width:].reshape(rows_here, tok_count, 2 * model_width)
    kv_whole = lax.all_gather(kv_local, "seq", axis=1, tiled=True)
    key_all = kv_whole[:, :, :model_width].reshape(rows_here, length, H, HD)
    value_all = kv_whole[:, :, model_width:].reshape(rows_here, length, H, HD)
    positions = jnp.arange(length, dtype=jnp.int32)
    query_pos = seq_first + jnp.arange(tok_count, dtype=jnp.int32)
    row_index = 0
    item_label = item_numbers(item_starts[row_index], item_lengths[row_index], positions)
    query_item = lax.dynamic_slice_in_dim(item_label, seq_first, tok_count)
    visible = visible_mask(query_pos, positions, query_item, item_label, pad_mask[row_index])
    mixed_part, log_total = attend_rows(
        query_all[row_index], key_all[row_index], value_all[row_index], visible, score_scale
    )
    visible_list = [visible]
    mixed_list = [mixed_part]
    logsum_list = [log_total]
    mixed_all = (
        jnp.stack(mixed_list).reshape(rows_here * tok_count, model_width).astype(jnp.bfloat16)
    )
    residual_one = inputs + jnp.dot(mixed_all, out_full, preferred_element_type=jnp.float32)
    up_full, down_full = (
        lax.all_gather(w_up, "fsdp", axis=0, tiled=True),
        lax.all_gather(w_down, "fsdp", axis=0, tiled=True),
    )
    normed_two = layer_norm(residual_one, gain_two, shift_two).astype(jnp.bfloat16)
    hidden_pre = jnp.dot(normed_two, up_full, preferred_element_type=jnp.float32) + bias_up
    activated = jax.nn.gelu(hidden_pre).astype(jnp.bfloat16)
    block_output = (
        residual_one + jnp.dot(activated, down_full, preferred_element_type=jnp.float32) + bias_down
    )
    output_shard = block_output.astype(jnp.bfloat16).reshape(rows_here, tok_count, model_width)
    up_full, down_full = (
        lax.all_gather(w_up, "fsdp", axis=0, tiled=True),
        lax.all_gather(w_down, "fsdp", axis=0, tiled=True),
    )
    cot_flat = cotangent.reshape(rows_here * tok_count, model_width)
    cot_wide = cot_flat.astype(jnp.float32)
    down_grad = contract_rows(activated, cot_flat)
    down_bias_part = jnp.sum(cot_wide, axis=0)
    act_grad = times_transpose(cot_flat, down_full)
    gelu_back = jax.vjp(jax.nn.gelu, hidden_pre)[1]
    hidden_grad = gelu_back(act_grad)[0].astype(jnp.bfloat16)
    up_grad = contract_rows(normed_two, hidden_grad)
    up_bias_part = jnp.sum(hidden_grad.astype(jnp.float32), axis=0)
    norm_two_grad = times_transpose(hidden_grad, up_full)
    norm_two_back = jax.vjp(layer_norm, residual_one, gain_two, shift_two)[1]
    resid_part, gain_two_grad, shift_two_grad = norm_two_back(norm_two_grad)
    residual_grad = cot_wide + resid_part
    up_sum, down_sum = (
        lax.psum_scatter(up_grad, "fsdp", scatter_dimension=0, tiled=True),
        lax.psum_scatter(down_grad, "fsdp", scatter_dimension=0, tiled=True),
    )
    qkv_full, out_full = (
        lax.all_gather(w_qkv, "fsdp", axis=0, tiled=True),
        lax.all_gather(w_out, "fsdp", axis=0, tiled=True),
    )
    branch_grad = residual_grad.astype(jnp.bfloat16)
    out_grad = contract_rows(mixed_all, branch_grad)
    mixed_grad = (
        times_transpose(branch_grad, out_full)
        .astype(jnp.bfloat16)
        .reshape(rows_here, tok_count, H, HD)
    )
    row_index = 0
    query_grad, key_part, value_part = attend_back(
        query_all[row_index],
        key_all[row_index],
        value_all[row_index],
        visible_list[row_index],
        logsum_list[row_index],
        mixed_grad[row_index],
        score_scale,
    )
    query_list = [query_grad.reshape(tok_count, model_width)]
    kv_list = [
        jnp.concatenate(
            [key_part.reshape(length, model_width), value_part.reshape(length, model_width)], axis=1
        )
    ]
    kv_terms = jnp.stack(kv_list)
    kv_grad = lax.psum_scatter(kv_terms, "seq", scatter_dimension=1, tiled=True).astype(
        jnp.bfloat16
    )
    proj_grad = jnp.concatenate(
        [
            jnp.stack(query_list).reshape(rows_here * tok_count, model_width),
            kv_grad.reshape(rows_here * tok_count, 2 * model_width),
        ],
        axis=1,
    )
    qkv_grad = contract_rows(normed_one, proj_grad)
    norm_one_grad = times_transpose(proj_grad, qkv_full)
    norm_one_back = jax.vjp(layer_norm, inputs, gain_one, shift_one)[1]
    input_part, gain_one_grad, shift_one_grad = norm_one_back(norm_one_grad)
    input_grad = (residual_grad + input_part).reshape(rows_here, tok_count, model_width)
    vector_grad = jnp.concatenate(
        [
            piece_grad.reshape(shard_count, -1)
            for piece_grad in (
                gain_one_grad,
                shift_one_grad,
                gain_two_grad,
                shift_two_grad,
                down_bias_part,
                up_bias_part,
            )
        ],
        axis=1,
    ).reshape(-1)
    qkv_sum, out_sum, vector_sum = (
        lax.psum_scatter(qkv_grad, "fsdp", scatter_dimension=0, tiled=True),
        lax.psum_scatter(out_grad, "fsdp", scatter_dimension=0, tiled=True),
        lax.psum_scatter(vector_grad, "fsdp", scatter_dimension=0, tiled=True),
    )
    up_total, down_total, qkv_total, out_total, vector_total = lax.psum(
        (up_sum, down_sum, qkv_sum, out_sum, vector_sum), "seq"
    )
    gain_one_out = vector_total[0:piece_d]
    shift_one_out = vector_total[piece_d : 2 * piece_d]
    gain_two_out = vector_total[2 * piece_d : 3 * piece_d]
    shift_two_out = vector_total[3 * piece_d : 4 * piece_d]
    down_bias_out = vector_total[4 * piece_d : 5 * piece_d]
    up_bias_out = vector_total[5 * piece_d :]
    return (
        output_shard,
        input_grad,
        gain_one_out,
        shift_one_out,
        qkv_total,
        out_total,
        gain_two_out,
        shift_two_out,
        up_total,
        up_bias_out,
        down_total,
        down_bias_out,
    )


def gather_small(vector, z_count):
    line = [vector]
    for j in range(1, z_count):
        line.append(lax.ppermute(vector, "z", [(i, (i + j) % z_count) for i in range(z_count)]))
    return line + [lax.ppermute(piece, "x", SWAP) for piece in line]


def gather_weight(shard, *others):
    near = lax.all_gather(shard, "z", axis=0, tiled=False)
    return [near, lax.ppermute(after(near, *others), "x", SWAP)]


def stage(flag, work, *args):
    shapes = jax.eval_shape(work, *args)

    def nothing(*_):
        return jax.tree.map(lambda a: jnp.zeros(a.shape, a.dtype), shapes)

    return lax.cond(flag, work, nothing, *args)


class Line:
    def __init__(self):
        self.last = ()

    def enter(self, value):
        return after(value, *self.last)

    def leave(self, *results):
        self.last = results[:1]
        return results


def after(value, *others):
    return lax.optimization_barrier((value,) + others)[0]


def seq_pieces(block, *others):
    return core_pieces(block, after(lax.ppermute(block, "y", SWAP), *others))


def core_pieces(block, other):
    return [block, lax.ppermute(block, "c", SWAP), other, lax.ppermute(other, "c", SWAP)]


def by_bit(bit, mine, theirs):
    return jnp.where(bit == 0, mine, theirs), jnp.where(bit == 0, theirs, mine)


def gather_tokens(block, yi, ci, *others):
    parts = seq_pieces(block, *others)
    near = by_bit(ci, parts[0], parts[1])
    far = by_bit(ci, parts[2], parts[3])
    rows = [jnp.where(yi == 0, n, f) for n, f in zip(near, far)]
    rows += [jnp.where(yi == 0, f, n) for n, f in zip(near, far)]
    return jnp.concatenate(rows, axis=0)


def core_sum(parts, yi):
    away, home = parts
    other = lax.ppermute(away, "c", SWAP)
    tokens, model = home.shape[0] // 2, home.shape[1]
    steps = 2
    block = (tokens // steps, model)

    def kernel(at_ref, *refs):
        wide = jnp.float32
        refs[4][...] = refs[0][...].astype(wide) + refs[1][...].astype(wide)
        refs[5][...] = (refs[2][...].astype(wide) + refs[3][...].astype(wide)).astype(
            jnp.bfloat16
        )

    here = pl.BlockSpec(block, lambda i, at: (at[0] * steps + i, 0))
    there = pl.BlockSpec(block, lambda i, at: ((1 - at[0]) * steps + i, 0))
    out = pl.BlockSpec(block, lambda i, at: (i, 0))
    return pl.pallas_call(
        kernel,
        grid_spec=pltpu.PrefetchScalarGridSpec(
            num_scalar_prefetch=1,
            grid=(steps,),
            in_specs=[here, here, there, there],
            out_specs=[out, out],
        ),
        out_shape=[
            jax.ShapeDtypeStruct((tokens, model), jnp.float32),
            jax.ShapeDtypeStruct((tokens, model), jnp.bfloat16),
        ],
        cost_estimate=cost(flops=0, bytes_accessed=7 * tokens * model, transcendentals=0),
        compiler_params=params(),
    )(jnp.reshape(yi, (1,)).astype(jnp.int32), home, other, home, other)


def home_sum(home, other):
    return home + other.astype(jnp.float32)


COST_SCALE = 0.01


def cost(flops, bytes_accessed, transcendentals):
    return pl.CostEstimate(
        flops=int(flops * COST_SCALE),
        bytes_accessed=int(bytes_accessed * COST_SCALE),
        transcendentals=int(transcendentals * COST_SCALE),
    )


def params(limit=VMEM_LIMIT):
    return pltpu.CompilerParams(vmem_limit_bytes=limit)


def weight_matmul(left, pieces, offsets, shape, back, body, extras, outs, chunk, groups=None):
    rows = left.shape[0]
    depth, width = shape
    out_width = depth if back else width
    steps = out_width // chunk
    n_pieces, n_extras = len(pieces), len(extras)
    blocks = [(p, k) for p, piece in enumerate(pieces) for k in range(piece.shape[0])]
    block_rows, block_cols = pieces[0].shape[1:]
    row_count, col_count = depth // block_rows, width // block_cols

    tables = (offsets,) if groups is None else (offsets, groups)

    def kernel(*refs):
        table_refs, left_ref, refs = refs[: len(tables)], refs[len(tables)], refs[len(tables) + 1 :]
        offs_ref = table_refs[0]
        piece_refs = refs[:n_pieces]
        extra_refs = refs[n_pieces : n_pieces + n_extras]
        out_refs = refs[n_pieces + n_extras : -2]
        held, sems = refs[-2:]
        step = pl.program_id(0)

        def slot(row, col):
            return sems.at[row, col]

        @pl.when(step == 0)
        def _():
            for b, (p, k) in enumerate(blocks):
                row, col = offs_ref[0, b], offs_ref[1, b]
                target = held.at[
                    pl.ds(pl.multiple_of(row * block_rows, block_rows), block_rows),
                    pl.ds(pl.multiple_of(col * block_cols, block_cols), block_cols),
                ]
                pltpu.make_async_copy(piece_refs[p].at[k], target, slot(row, col)).start()

        def arrive(row, col):
            target = held.at[
                pl.ds(row * block_rows, block_rows), pl.ds(col * block_cols, block_cols)
            ]
            pltpu.make_async_copy(piece_refs[0].at[0], target, slot(row, col)).wait()

        for n in range(steps):
            needed = [
                (row, col)
                for row in range(row_count)
                for col in range(col_count)
                if (
                    row * block_rows // chunk if back else col * block_cols // chunk
                ) == n
            ]
            if needed:

                @pl.when(step == n)
                def _():
                    for row, col in needed:
                        arrive(row, col)

        start = pl.ds(pl.multiple_of(step * chunk, chunk), chunk)

        def product(part):
            if back:
                return lax.dot_general(
                    part,
                    held[start, :],
                    (((1,), (1,)), ((), ())),
                    preferred_element_type=jnp.float32,
                )
            return jnp.dot(part, held[:, start], preferred_element_type=jnp.float32)

        if groups is None:
            body(product(left_ref[...]), extra_refs, out_refs)
        else:
            size = rows // groups.shape[0]
            each = out_refs[0].shape[0] // size
            for g in range(groups.shape[0]):
                at = pl.multiple_of(table_refs[1][g] * size, size)
                values = product(left_ref[pl.ds(at, size), :])
                to = (g % each) * size
                out_refs[g // each][to : to + size, :] = values.astype(jnp.bfloat16)

    def column_spec(array):
        return pl.BlockSpec((array.shape[0], chunk), lambda i, *tabs: (0, i))

    flops = 2 * rows * depth * width
    moved = 2 * (left.size + depth * width) + sum(
        a.size * a.dtype.itemsize for a in list(extras) + list(outs)
    )
    return pl.pallas_call(
        kernel,
        grid_spec=pltpu.PrefetchScalarGridSpec(
            num_scalar_prefetch=len(tables),
            grid=(steps,),
            in_specs=[
                pl.BlockSpec(
                    left.shape, lambda i, *tabs: (0, 0), pipeline_mode=pl.Buffered(1)
                )
            ]
            + [pl.BlockSpec(memory_space=pl.ANY)] * n_pieces
            + [column_spec(a) for a in extras],
            out_specs=[column_spec(a) for a in outs],
            scratch_shapes=[
                pltpu.VMEM((depth, width), jnp.bfloat16),
                pltpu.SemaphoreType.DMA((row_count, col_count)),
            ],
        ),
        out_shape=list(outs),
        cost_estimate=cost(flops=flops, bytes_accessed=moved, transcendentals=0),
        compiler_params=params(),
    )(*tables, left, *pieces, *extras)


def store_low(values, extra_refs, out_refs):
    out_refs[0][...] = values.astype(jnp.bfloat16)


def store_gelu(values, extra_refs, out_refs):
    hidden = values + extra_refs[0][...]
    square = hidden * hidden
    bend = jnp.tanh(GELU_A * hidden * (1.0 + GELU_B * square))
    half = 0.5 * (1.0 + bend)
    out_refs[0][...] = (hidden * half).astype(jnp.bfloat16)
    slope = half + 0.5 * hidden * (1.0 - bend * bend) * (
        GELU_A * (1.0 + 3.0 * GELU_B * square)
    )
    out_refs[1][...] = slope


def store_hidden_grad(values, extra_refs, out_refs):
    low = (values * extra_refs[0][...]).astype(jnp.bfloat16)
    out_refs[0][...] = low
    out_refs[1][...] = jnp.sum(low.astype(jnp.float32), axis=0, keepdims=True)


def weight_grad(left, right, where, count, block, width, addend=None, parts=1):
    rows = left.shape[0]
    part = width // parts
    added = () if addend is None else (addend,)

    def kernel(where_ref, left_ref, right_ref, *refs):
        for n in range(parts):
            cols = slice(n * part, (n + 1) * part)
            value = lax.dot_general(
                left_ref[...],
                right_ref[:, cols],
                (((0,), (0,)), ((), ())),
                preferred_element_type=jnp.float32,
            )
            if added:
                value = value + refs[0][0, :, cols].astype(jnp.float32)
            refs[len(added) + n][0] = value.astype(jnp.bfloat16)

    return pl.pallas_call(
        kernel,
        grid_spec=pltpu.PrefetchScalarGridSpec(
            num_scalar_prefetch=1,
            grid=(count,),
            in_specs=[
                pl.BlockSpec((rows, block), lambda k, at: (0, at[k])),
                pl.BlockSpec((rows, width), lambda k, at: (0, at[count])),
            ]
            + [pl.BlockSpec((1, block, width), lambda k, at: (k, 0, 0))] * len(added),
            out_specs=[pl.BlockSpec((1, block, part), lambda k, at: (k, 0, 0))] * parts,
        ),
        out_shape=[jax.ShapeDtypeStruct((count, block, part), jnp.bfloat16)] * parts,
        cost_estimate=cost(
            flops=2 * rows * count * block * width,
            bytes_accessed=2 * rows * (count * block + width) + 4 * count * block * width,
            transcendentals=0,
        ),
        compiler_params=params(),
    )(where, left, right, *added)


def slice_qkv(w_qkv, where, width):
    rows = w_qkv.shape[0]
    heads = H // 4

    def kernel(at_ref, from_ref, to_ref):
        for i in range(heads):
            col = pl.ds(pl.multiple_of((2 * i + at_ref[1]) * HD, HD), HD)
            to_ref[:, i * HD : (i + 1) * HD] = from_ref[:, col]

    part = heads * HD
    return pl.pallas_call(
        kernel,
        grid_spec=pltpu.PrefetchScalarGridSpec(
            num_scalar_prefetch=1,
            grid=(3,),
            in_specs=[pl.BlockSpec((rows, 2 * part), lambda g, at: (0, 2 * g + at[0]))],
            out_specs=pl.BlockSpec((rows, part), lambda g, at: (0, g)),
        ),
        out_shape=jax.ShapeDtypeStruct((rows, width), jnp.bfloat16),
        cost_estimate=cost(flops=0, bytes_accessed=3 << 20, transcendentals=0),
        compiler_params=params(),
    )(where, w_qkv)


def slice_weights(w_out, w_up, w_down, where, shard_count):
    rows, model = w_out.shape
    ff_part = w_down.shape[0] // 4
    steps = shard_count
    part = ff_part // steps
    up_half = steps // 2

    def kernel(at_ref, out_ref, up_ref, down_ref, out_to, low_to, high_to, left_to, right_to):
        step = pl.program_id(0)
        for n, up_to in enumerate((low_to, high_to)):

            @pl.when(step // up_half == n)
            def _():
                up_to[...] = up_ref[...]

        @pl.when(step == 0)
        def _():
            out_to[...] = out_ref[...]

        left_to[...] = down_ref[:, : model // 2]
        right_to[...] = down_ref[:, model // 2 :]

    def up_spec(n):
        return pl.BlockSpec(
            (rows, ff_part), lambda i, at: (0, jnp.clip(i - n * up_half, 0, up_half - 1))
        )

    return pl.pallas_call(
        kernel,
        grid_spec=pltpu.PrefetchScalarGridSpec(
            num_scalar_prefetch=1,
            grid=(steps,),
            in_specs=[
                pl.BlockSpec((rows // 2, model // 2), lambda i, at: (at[1], at[0])),
                pl.BlockSpec((rows, ff_part), lambda i, at: (0, 4 * i + 2 * at[0] + at[1])),
                pl.BlockSpec(
                    (part, model), lambda i, at: ((2 * at[0] + at[1]) * steps + i, 0)
                ),
            ],
            out_specs=[
                pl.BlockSpec((rows // 2, model // 2), lambda i, at: (0, 0)),
                up_spec(0),
                up_spec(1),
                pl.BlockSpec((part, model // 2), lambda i, at: (i, 0)),
                pl.BlockSpec((part, model // 2), lambda i, at: (i, 0)),
            ],
        ),
        out_shape=[
            jax.ShapeDtypeStruct(shape, jnp.bfloat16)
            for shape in [(rows // 2, model // 2)]
            + [(rows, ff_part * up_half)] * 2
            + [(ff_part, model // 2)] * 2
        ],
        cost_estimate=cost(flops=0, bytes_accessed=9 << 20, transcendentals=0),
        compiler_params=params(),
    )(where, w_out, w_up, w_down)


def visible_tile(query_item, key_item, first_query, n_query, n_key):
    query_pos = first_query + lax.broadcasted_iota(jnp.int32, (n_query, n_key), 0)
    key_pos = lax.broadcasted_iota(jnp.int32, (n_query, n_key), 1)
    return ((query_item == key_item) & (key_pos < query_pos)) | (key_pos == query_pos)


def head_spec(length, first):
    return pl.BlockSpec((length, HD), lambda h: (0, first + h))


def attention(projected, query_item, key_item, heads, tile):
    length = projected.shape[0]
    scale = HD ** (-0.5)

    def kernel(q_ref, k_ref, v_ref, qi_ref, ki_ref, mixed_ref, log_ref):
        for start in range(0, length, tile):
            stop = start + tile
            rows = slice(start, stop)
            scores = (
                lax.dot_general(
                    q_ref[rows, :],
                    k_ref[:stop, :],
                    (((1,), (1,)), ((), ())),
                    preferred_element_type=jnp.float32,
                )
                * scale
            )
            seen = visible_tile(qi_ref[rows, :], ki_ref[:, :stop], start, tile, stop)
            scores = jnp.where(seen, scores, MASKED)
            peak = jnp.max(scores, axis=-1, keepdims=True)
            weights = jnp.exp(scores - peak)
            total = jnp.sum(weights, axis=-1, keepdims=True)
            probs = (weights * (1.0 / total)).astype(jnp.bfloat16)
            mixed_ref[rows, :] = jnp.dot(
                probs, v_ref[:stop, :], preferred_element_type=jnp.float32
            ).astype(jnp.bfloat16)
            log_ref[0, rows, :] = peak + jnp.log(total)

    whole = lambda rows, cols: pl.BlockSpec((rows, cols), lambda h: (0, 0))
    return pl.pallas_call(
        kernel,
        grid=(heads,),
        in_specs=[head_spec(length, g * heads) for g in range(3)]
        + [whole(length, 1), whole(1, length)],
        out_specs=[head_spec(length, 0), pl.BlockSpec((1, length, 1), lambda h: (h, 0, 0))],
        out_shape=[
            jax.ShapeDtypeStruct((length, heads * HD), jnp.bfloat16),
            jax.ShapeDtypeStruct((heads, length, 1), jnp.float32),
        ],
        cost_estimate=cost(
            flops=4 * heads * length * length * HD,
            bytes_accessed=8 * length * heads * HD,
            transcendentals=heads * length * length,
        ),
        compiler_params=params(),
    )(projected, projected, projected, query_item, key_item)


def attention_back(projected, mixed_grad, log_total, query_item, key_item, heads, tile):
    length = projected.shape[0]
    scale = HD ** (-0.5)

    def kernel(q_ref, k_ref, v_ref, g_ref, log_ref, qi_ref, ki_ref, grad_ref, dk_ref, dv_ref):
        head = pl.program_id(0)

        def place(group):
            return pl.ds(pl.multiple_of((group * heads + head) * HD, HD), HD)

        for start in reversed(range(0, length, tile)):
            stop = start + tile
            rows = slice(start, stop)
            query, grad = q_ref[rows, :], g_ref[rows, :]
            key, value = k_ref[:stop, :], v_ref[:stop, :]
            scores = (
                lax.dot_general(
                    query, key, (((1,), (1,)), ((), ())), preferred_element_type=jnp.float32
                )
                * scale
            )
            seen = visible_tile(qi_ref[rows, :], ki_ref[:, :stop], start, tile, stop)
            probs = jnp.exp(jnp.where(seen, scores, MASKED) - log_ref[0, rows, :])
            prob_grad = lax.dot_general(
                grad, value, (((1,), (1,)), ((), ())), preferred_element_type=jnp.float32
            )
            inner = jnp.sum(prob_grad * probs, axis=-1, keepdims=True)
            score_grad = (probs * (prob_grad - inner)).astype(jnp.bfloat16)
            grad_ref[rows, place(0)] = (
                jnp.dot(score_grad, key, preferred_element_type=jnp.float32) * scale
            ).astype(jnp.bfloat16)
            key_part = lax.dot_general(
                score_grad, query, (((0,), (0,)), ((), ())), preferred_element_type=jnp.float32
            )
            value_part = lax.dot_general(
                probs.astype(jnp.bfloat16),
                grad,
                (((0,), (0,)), ((), ())),
                preferred_element_type=jnp.float32,
            )
            if stop == length:
                dk_ref[...] = key_part
                dv_ref[...] = value_part
            else:
                dk_ref[:stop, :] += key_part
                dv_ref[:stop, :] += value_part
        grad_ref[:, place(1)] = (dk_ref[...] * scale).astype(jnp.bfloat16)
        grad_ref[:, place(2)] = dv_ref[...].astype(jnp.bfloat16)

    whole = lambda rows, cols: pl.BlockSpec((rows, cols), lambda h: (0, 0))
    return pl.pallas_call(
        kernel,
        grid=(heads,),
        in_specs=[head_spec(length, g * heads) for g in range(3)]
        + [
            head_spec(length, 0),
            pl.BlockSpec((1, length, 1), lambda h: (h, 0, 0)),
            whole(length, 1),
            whole(1, length),
        ],
        out_specs=whole(length, 3 * heads * HD),
        out_shape=jax.ShapeDtypeStruct((length, 3 * heads * HD), jnp.bfloat16),
        scratch_shapes=[pltpu.VMEM((length, HD), jnp.float32)] * 2,
        cost_estimate=cost(
            flops=10 * heads * length * length * HD,
            bytes_accessed=16 * length * heads * HD,
            transcendentals=heads * length * length,
        ),
        compiler_params=params(),
    )(projected, projected, projected, mixed_grad, log_total, query_item, key_item)


def widen(chunks, places, grid, piece_specs, out_block, out_index, out_shape, write):
    def kernel(place_ref, *refs):
        for n in range(len(chunks)):
            for r in range(4):
                write(n, place_ref[r], refs[4 * n + r], refs[-1])

    return pl.pallas_call(
        kernel,
        grid_spec=pltpu.PrefetchScalarGridSpec(
            num_scalar_prefetch=1,
            grid=(grid,),
            in_specs=[
                pl.BlockSpec(block, functools.partial(lambda at, i, pos: at(i), at))
                for block, at in piece_specs
                for _ in range(4)
            ],
            out_specs=pl.BlockSpec(out_block, lambda i, pos: out_index(i)),
        ),
        out_shape=jax.ShapeDtypeStruct(out_shape, jnp.float32),
        cost_estimate=cost(
            flops=0, bytes_accessed=6 * int(np.prod(out_shape)), transcendentals=0
        ),
        compiler_params=params(),
    )(places, *[piece for pieces in chunks for piece in pieces])


def widen_columns(pieces, places, blocks):
    rows, width = pieces[0].shape
    part = width // blocks

    def write(n, pos, piece, out):
        out[:, pl.ds(pl.multiple_of(pos * part, part), part)] = piece[...].astype(jnp.float32)

    return widen(
        [pieces],
        places,
        blocks,
        [((rows, part), lambda i: (0, i))],
        (rows, 4 * part),
        lambda i: (0, i),
        (rows, 4 * width),
        write,
    )


def widen_rows(pieces, places):
    rows, width = pieces[0].shape

    def write(n, pos, piece, out):
        @pl.when(pos == pl.program_id(0))
        def _():
            out[...] = piece[...].astype(jnp.float32)

    return widen(
        [pieces],
        places,
        4,
        [((rows, width), lambda i: (0, 0))],
        (rows, width),
        lambda i: (i, 0),
        (4 * rows, width),
        write,
    )


def widen_heads(pieces, places):
    rows, width = pieces[0].shape
    part = width // 3

    def write(n, pos, piece, out):
        first = lax.div(pos, 2) * part * 2 + lax.rem(pos, 2) * HD
        for i in range(part // HD):
            cols = pl.ds(pl.multiple_of(first + 2 * i * HD, HD), HD)
            out[:, cols] = piece[:, i * HD : (i + 1) * HD].astype(jnp.float32)

    return widen(
        [pieces],
        places,
        3,
        [((rows, part), lambda i: (0, i))],
        (rows, 4 * part),
        lambda i: (0, i),
        (rows, 4 * width),
        write,
    )


def widen_quarters(pieces, places):
    rows, width = pieces[0].shape

    def write(n, pos, piece, out):
        row = pl.multiple_of(lax.rem(pos, 2) * rows, rows)
        col = pl.multiple_of(lax.div(pos, 2) * width, width)
        out[pl.ds(row, rows), pl.ds(col, width)] = piece[...].astype(jnp.float32)

    return widen(
        [pieces],
        places,
        1,
        [((rows, width), lambda i: (0, 0))],
        (2 * rows, 2 * width),
        lambda i: (0, 0),
        (2 * rows, 2 * width),
        write,
    )


def norm_back(values, gain_vec, incoming):
    center = values - jnp.mean(values, axis=-1, keepdims=True)
    spread = jnp.mean(center * center, axis=-1, keepdims=True)
    inverse = lax.rsqrt(spread + EPSILON)
    unit = center * inverse
    scaled = incoming * gain_vec
    inner = jnp.mean(scaled * unit, axis=-1, keepdims=True)
    grad = (scaled - jnp.mean(scaled, axis=-1, keepdims=True) - unit * inner) * inverse
    return grad, jnp.sum(incoming * unit, axis=0), jnp.sum(incoming, axis=0)


def split_shards(
    block_input,
    cotangent,
    item_starts,
    item_lengths,
    pad_mask,
    ln1_gain,
    ln1_shift,
    w_qkv,
    w_out,
    ln2_gain,
    ln2_shift,
    w_up,
    up_bias,
    w_down,
    down_bias,
):
    low, wide = jnp.bfloat16, jnp.float32
    z_count = lax.axis_size("z")
    shard_count = 2 * z_count
    zi, xi, yi, ci = [lax.axis_index(name) for name in ("z", "x", "y", "c")]
    si = 2 * yi + ci
    tok_count, model = block_input.shape[1:]
    length = 4 * tok_count
    piece_d, ff_piece = ln1_gain.shape[0], up_bias.shape[0]
    ff_part = ff_piece // 4
    ff_here = ff_part * shard_count
    heads = H // 4
    places = jnp.stack([jnp.bitwise_xor(si, r) for r in range(4)]).astype(jnp.int32)

    packed = jnp.concatenate([ln1_gain, ln1_shift, ln2_gain, ln2_shift, down_bias, up_bias])
    vector_stack = jnp.stack(gather_small(packed, z_count))
    owners = jnp.stack(
        [
            lax.rem(zi - j + z_count, z_count) * 2 + jnp.bitwise_xor(xi, dx)
            for dx in range(2)
            for j in range(z_count)
        ]
    )
    hit = owners[None, :] == jnp.arange(shard_count, dtype=jnp.int32)[:, None]
    vector_table = jnp.sum(jnp.where(hit[:, :, None], vector_stack[None], 0.0), axis=1)

    def vector_part(slot):
        return vector_table[:, slot * piece_d : (slot + 1) * piece_d].reshape(-1)

    gain_one, shift_one, gain_two, shift_two, bias_down = [vector_part(slot) for slot in range(5)]
    bias_up = lax.dynamic_index_in_dim(
        vector_table[:, 5 * piece_d :].reshape(shard_count, 4, ff_part), si, 1, keepdims=False
    ).reshape(1, ff_here)

    line = Line()
    flag = item_lengths[0, 0] > 0
    where = jnp.stack([yi, ci]).astype(jnp.int32)
    qkv_slice = slice_qkv(w_qkv, where, 3 * heads * HD)
    slices = slice_weights(w_out, w_up, w_down, after(where, qkv_slice), shard_count)
    half = model // 2
    qkv_width = 3 * heads * HD
    qkv_parts = gather_weight(qkv_slice)
    down_pair = jnp.stack([slices[4], lax.ppermute(slices[4], "x", SWAP)])
    inputs = after(block_input, down_pair).reshape(tok_count, model).astype(wide)
    normed_one = layer_norm(inputs, gain_one, shift_one).astype(low)
    out_parts = gather_weight(after(slices[0], normed_one), qkv_parts[1])
    out_parts = out_parts + [lax.ppermute(piece, "y", SWAP) for piece in out_parts]

    near_blocks = [2 * z + xi for z in range(z_count)]
    far_blocks = [2 * z + 1 - xi for z in range(z_count)]
    split = near_blocks + far_blocks
    paired = [b for pair in zip(near_blocks, far_blocks) for b in pair]
    zero = jnp.zeros_like(xi)

    def table(*rows):
        return jnp.stack([jnp.stack(row) for row in rows]).astype(jnp.int32)

    qkv_offsets = table(split, [zero] * shard_count)
    up_offsets = table(split + split, [zero] * shard_count + [zero + 1] * shard_count)
    down_offsets = table(split + paired, [zero] * shard_count + [zero + 1] * shard_count)
    out_offsets = table(split + split, [yi] * shard_count + [1 - yi] * shard_count)

    def blocks_at(blocks, n):
        return table(blocks + [zero + n])[0]

    def sum_small(terms, *others):
        def term(j):
            return lax.dynamic_index_in_dim(
                terms, lax.rem(zi - j + z_count, z_count), 0, keepdims=False
            )

        total = term(0).astype(wide)
        for j in range(1, z_count):
            theirs = lax.ppermute(
                term(j), "z", [(i, (i - j) % z_count) for i in range(z_count)]
            )
            total = total + after(theirs, *others).astype(wide)
        return total

    def plain_matmul(left, pieces, offsets, shape, back, body, extras, outs):
        return weight_matmul(left, pieces, offsets, shape, back, body, extras, outs, 512)

    def row_groups(left, pieces, offsets, shape_, back):
        groups = jnp.stack([1 - ci, 3 - ci, ci, 2 + ci]).astype(jnp.int32)
        outs = (shape(2 * tok_count, shape_[0] if back else shape_[1]),) * 2
        return weight_matmul(left, pieces, offsets, shape_, back, None, (), outs, 512, groups)

    def matmul(left, *others):
        return line.leave(*plain_matmul(line.enter(left), *others))

    def grad_chunk(left, right, blocks, n, block, width):
        return line.leave(
            *weight_grad(line.enter(left), right, blocks_at(blocks, n), len(blocks), block, width)
        )[0]

    def far_terms(left, right, block):
        terms = grad_chunk(left, right, far_blocks, 0, block, right.shape[1])
        return lax.ppermute(terms, "x", SWAP)

    def near_terms(left, right, block, addend, parts=1):
        return weight_grad(
            left, right, blocks_at(near_blocks, 0), z_count, block, addend.shape[2], addend, parts
        )

    def sum_over_z(total):
        return lax.psum_scatter(total, "z", scatter_dimension=0, tiled=False)

    def shape(rows, cols, kind=low):
        return jax.ShapeDtypeStruct((rows, cols), kind)

    normed_one = gather_tokens(normed_one, yi, ci, qkv_parts[0])
    cot_flat = after(cotangent.reshape(tok_count, model), normed_one)
    cot_wide = cot_flat.astype(wide)
    cot_all = gather_tokens(cot_flat, yi, ci)
    (projected,) = matmul(
        after(normed_one, cot_all),
        qkv_parts,
        qkv_offsets,
        (model, qkv_width),
        False,
        store_low,
        (),
        (shape(length, qkv_width),),
    )
    up_parts = gather_weight(slices[1], projected)
    up_high = lax.all_gather(slices[2], "z", axis=0, tiled=False)
    down_parts = gather_weight(slices[3], projected)
    down_parts.append(lax.all_gather(down_pair, "z", axis=0, tiled=True))
    positions = jnp.arange(length, dtype=jnp.int32)
    item_label = item_numbers(item_starts[0], item_lengths[0], positions)
    query_item = item_label[:, None]
    key_item = jnp.where((item_label >= 0) & (pad_mask[0] == 1), item_label, -2)[None, :]
    mixed_heads, log_total = line.leave(
        *attention(line.enter(projected), query_item, key_item, heads, 256)
    )

    def attend_out(mixed_heads):
        halves = mixed_heads.reshape(2, 2 * tok_count, heads * HD)
        away = lax.dynamic_index_in_dim(halves, 1 - yi, 0, keepdims=False)
        mine = lax.dynamic_index_in_dim(halves, yi, 0, keepdims=False)
        other = lax.ppermute(away, "y", SWAP)
        mixed = jnp.concatenate(by_bit(yi, mine, other), axis=1)
        (out_partial,) = plain_matmul(
            mixed,
            out_parts,
            out_offsets,
            (half, model),
            False,
            store_low,
            (),
            (shape(2 * tok_count, model),),
        )
        halves = out_partial.reshape(2, tok_count, model)
        away = lax.dynamic_index_in_dim(halves, 1 - ci, 0, keepdims=False)
        home = lax.dynamic_index_in_dim(halves, ci, 0, keepdims=False)
        residual_one = (
            inputs + home.astype(wide) + lax.ppermute(away, "c", SWAP).astype(wide)
        )
        normed_two = layer_norm(residual_one, gain_two, shift_two).astype(low)
        return normed_two, residual_one, mine, other

    up_parts += [up_high, lax.ppermute(after(up_high, mixed_heads), "x", SWAP)]
    normed_two, residual_one, mixed_home, mixed_other = line.leave(
        *stage(flag, attend_out, after(line.enter(mixed_heads), up_parts[0], up_high))
    )
    normed_two = gather_tokens(normed_two, yi, ci, up_parts[1], up_parts[3])
    activated, slope = matmul(
        normed_two,
        up_parts,
        up_offsets,
        (model, ff_here),
        False,
        store_gelu,
        (bias_up,),
        (shape(length, ff_here), shape(length, ff_here, wide)),
    )

    mixed_last = lax.ppermute(after(mixed_home, activated), "y", SWAP)
    others_heads = jnp.concatenate(by_bit(yi, mixed_other, mixed_last), axis=0)
    mixed = jnp.concatenate(by_bit(yi, mixed_heads, others_heads), axis=1)

    down_bias_part = jnp.sum(cot_wide, axis=0)
    down_sum = grad_chunk(
        after(activated, down_parts[1], mixed), cot_all, paired, 0, ff_part, model
    )
    down_pair = lax.psum_scatter(
        down_sum.reshape(z_count, 2, ff_part, model), "z", scatter_dimension=0, tiled=False
    )
    hidden_grad, up_bias_part = matmul(
        cot_all,
        down_parts,
        down_offsets,
        (ff_here, model),
        True,
        store_hidden_grad,
        (slope,),
        (shape(length, ff_here), shape(1, ff_here, wide)),
    )
    up_far = far_terms(normed_two, hidden_grad, piece_d)
    norm_two_parts = line.leave(
        *row_groups(line.enter(hidden_grad), up_parts, up_offsets, (model, ff_here), True)
    )

    def norm_two_back(*norm_two_parts):
        home, away = core_sum(norm_two_parts, yi)
        other = lax.ppermute(away, "y", SWAP)
        feed_parts = row_groups(
            after(activated, away), down_parts, down_offsets, (ff_here, model), False
        )
        norm_two_grad = home_sum(home, after(other, *feed_parts))
        resid_part, gain_two_grad, shift_two_grad = norm_back(
            residual_one, gain_two, norm_two_grad
        )
        residual_grad = cot_wide + resid_part
        branch_grad = residual_grad.astype(low)
        branch_pair = jnp.concatenate(
            by_bit(ci, branch_grad, lax.ppermute(branch_grad, "c", SWAP)), axis=0
        )
        return branch_pair, residual_grad, gain_two_grad, shift_two_grad, feed_parts

    branch_pair, residual_grad, gain_two_grad, shift_two_grad, feed_parts = line.leave(
        *stage(flag, norm_two_back, line.enter(norm_two_parts[0]), norm_two_parts[1])
    )

    out_blocks = far_blocks + near_blocks

    def out_back(branch_pair):
        (mixed_grad_pair,) = plain_matmul(
            branch_pair,
            out_parts,
            out_offsets,
            (half, model),
            True,
            store_low,
            (),
            (shape(2 * tok_count, half),),
        )
        part = heads * HD
        away = lax.dynamic_slice_in_dim(mixed_grad_pair, (1 - yi) * part, part, 1)
        home = lax.dynamic_slice_in_dim(mixed_grad_pair, yi * part, part, 1)
        theirs = lax.ppermute(away, "y", SWAP)
        feed_home, feed_away = core_sum([after(feed_parts[0], away), feed_parts[1]], yi)
        pair = after(branch_pair, away)
        branch_away = lax.dynamic_slice_in_dim(pair, (1 - yi) * half, half, 1)
        branch_home = lax.dynamic_slice_in_dim(pair, yi * half, half, 1)
        theirs = after(theirs, feed_away, branch_away, branch_home)
        mixed_grad = jnp.concatenate(by_bit(yi, home, theirs), axis=0)
        return mixed_grad, feed_home, feed_away, branch_away, branch_home

    mixed_grad, feed_home, feed_away, branch_away, branch_home = line.leave(
        *stage(flag, out_back, line.enter(branch_pair))
    )
    branch_other = lax.ppermute(after(branch_away, mixed_grad), "y", SWAP)
    branch_all = jnp.concatenate(by_bit(yi, branch_home, branch_other), axis=0)
    (proj_grad,) = line.leave(
        attention_back(
            projected,
            line.enter(mixed_grad),
            log_total,
            query_item,
            key_item,
            heads,
            256,
        )
    )
    qkv_far = far_terms(normed_one, proj_grad, piece_d)
    (up_sum,) = line.leave(
        near_terms(
            line.enter(after(normed_two, branch_other)), hidden_grad, piece_d, up_far
        )[0]
    )
    up_shard = sum_over_z(after(up_sum, down_pair))
    norm_one_parts = line.leave(
        *row_groups(line.enter(proj_grad), qkv_parts, qkv_offsets, (model, qkv_width), True)
    )
    out_sum = line.leave(
        *weight_grad(
            line.enter(mixed),
            branch_all,
            blocks_at(out_blocks, 0),
            shard_count,
            piece_d // 2,
            half,
        )
    )[0]
    feed_other = lax.ppermute(after(feed_away, up_sum), "y", SWAP)

    def norm_one_back(*norm_one_parts):
        home, away = core_sum(norm_one_parts, yi)
        away = lax.ppermute(away, "y", SWAP)
        norm_one_grad = home_sum(home, away)
        input_part, gain_one_grad, shift_one_grad = norm_back(inputs, gain_one, norm_one_grad)
        input_grad = (residual_grad + input_part).reshape(1, tok_count, model)
        return input_grad, gain_one_grad, shift_one_grad

    input_grad, gain_one_grad, shift_one_grad = line.leave(
        *stage(flag, norm_one_back, after(line.enter(norm_one_parts[0]), feed_other), norm_one_parts[1])
    )
    (qkv_sum,) = line.leave(
        *near_terms(line.enter(after(normed_one, up_shard)), proj_grad, piece_d, qkv_far)
    )
    qkv_shard = sum_over_z(qkv_sum)

    def ends(up_shard):
        up_other = lax.ppermute(up_shard, "y", SWAP)
        down_far = lax.ppermute(down_pair[1], "x", SWAP)
        output_shard = (residual_one + home_sum(feed_home, feed_other) + bias_down).astype(low)
        output_shard = output_shard.reshape(1, tok_count, model)
        down_shard = (down_pair[0].astype(wide) + down_far.astype(wide)).astype(low)
        return output_shard, down_shard, up_other

    output_shard, down_shard, up_other = line.leave(
        *stage(flag, ends, line.enter(up_shard))
    )

    def more_ends(down_shard):
        up_bias_grad = jnp.where(
            (jnp.arange(4, dtype=jnp.int32) == si)[None, :, None],
            up_bias_part.reshape(shard_count, 1, ff_part),
            0.0,
        ).reshape(shard_count, ff_piece)
        vector_grad = jnp.concatenate(
            [
                part.reshape(shard_count, -1)
                for part in (
                    gain_one_grad,
                    shift_one_grad,
                    gain_two_grad,
                    shift_two_grad,
                    down_bias_part,
                    up_bias_grad,
                )
            ],
            axis=1,
        )
        vector_grad = vector_grad + lax.ppermute(vector_grad, "c", SWAP)
        vector_other = lax.ppermute(vector_grad, "y", SWAP)
        down_other = lax.ppermute(down_shard, "y", SWAP)
        out_away = lax.ppermute(out_sum[:z_count], "x", SWAP)
        up_total = widen_columns(core_pieces(up_shard, up_other), places, shard_count)
        out_both = (out_sum[z_count:].astype(wide) + out_away.astype(wide)).astype(low)
        vector_grad = vector_grad + after(vector_other, up_total)
        return out_both, up_total, after(down_other, up_total), vector_grad

    out_both, up_total, down_other, vector_grad = stage(
        flag, more_ends, after(line.enter(down_shard), down_shard)
    )
    out_shard = sum_over_z(after(out_both, qkv_sum))

    def last(qkv_shard):
        other = lax.ppermute(qkv_shard, "y", SWAP)
        vector_pair = vector_grad.reshape(z_count, 2, -1)
        away = lax.dynamic_index_in_dim(vector_pair, 1 - xi, 1, keepdims=False)
        home = lax.dynamic_index_in_dim(vector_pair, xi, 1, keepdims=False)
        vector_other = lax.ppermute(away, "x", SWAP)
        down_total = widen_rows(core_pieces(down_shard, down_other), places)
        vector_sum = home + after(vector_other, down_total)
        qkv_pieces = core_pieces(qkv_shard, after(other, vector_sum))
        return widen_heads(qkv_pieces, places), down_total, vector_sum

    qkv_total, down_total, vector_sum = stage(flag, last, after(qkv_shard, up_total))
    out_total = widen_quarters(seq_pieces(after(out_shard, qkv_total)), places)
    vector_total = sum_small(after(vector_sum, qkv_total))
    vectors = [vector_total[slot * piece_d : (slot + 1) * piece_d] for slot in range(5)]
    return (
        output_shard,
        input_grad,
        vectors[0],
        vectors[1],
        qkv_total,
        out_total,
        vectors[2],
        vectors[3],
        up_total,
        vector_total[5 * piece_d :],
        down_total,
        vectors[4],
    )


def solution(mesh):
    shard_count, seq_count = mesh.shape["fsdp"], mesh.shape["seq"]

    def step(*args):
        model, hidden = args[0].shape[2], args[12].shape[0]
        rows_each = args[0].shape[0] // shard_count
        if (
            rows_each == 1
            and seq_count == 4
            and model // shard_count == 2 * HD
            and hidden // (4 * shard_count) % 256 == 0
        ):
            fsdp, seq = ("z", "x"), ("y", "c")
            devices = mesh.devices.reshape(shard_count // 2, 2, 2, 2)
            inner, body = Mesh(devices, fsdp + seq), split_shards
        else:
            fsdp, seq = "fsdp", "seq"
            inner, body = mesh, plain_shards
        rows, tokens = P(fsdp, None), P(fsdp, seq, None)
        vector = P(fsdp)
        placed = (tokens, tokens, rows, rows, rows, vector, vector, rows, rows)
        placed += (vector, vector, rows, vector, rows, vector)
        given = (tokens, tokens, vector, vector, rows, rows, vector, vector)
        given += (rows, vector, rows, vector)
        return jax.shard_map(
            body, mesh=inner, in_specs=placed, out_specs=given, check_vma=False
        )(*args)

    return step
```
